32 devices in a mesh: trc: 4 (over z), lat: 4 (over x, core), lon: 2 (over y).
Axes of the slice: x: 2, y: 2, z: 4, core: 2. Of those that a mesh axis runs over, the one named last changes fastest.
Arguments:
- species_concentrations: float32 [32, 8, 128, 256], P('trc', None, 'lat', 'lon'), may hold values from 0.2 to 4
- zonal_velocity_array: float32 [8, 128, 256], P('trc', 'lat', 'lon'), may hold values from -2.5 to 2.5
- meridional_velocity_array: float32 [8, 128, 256], P('trc', 'lat', 'lon'), may hold values from -2.5 to 2.5
- thermal_anomaly: float32 [8, 128, 256], P('trc', 'lat', 'lon'), may hold values from -6 to 6
- ocean_top_height_grid: float32 [128, 256], P('lat', 'lon'), may hold values from -6 to 6
- water_layer_tally: int32 [128, 256], P('lat', 'lon'), may hold values from 0 to 8
- species_interaction_table: float32 [32, 32], replicated, may hold values from -1 to 1
- species_production_pace: float32 [32], replicated, may hold values from 0.2 to 2
- photon_uptake: float32 [32], replicated, may hold values from 0.01 to 0.1
Outputs:
- updated_tracers: float32 [32, 8, 128, 256], P('trc', None, 'lat', 'lon')
- east_out: float32 [8, 128, 256], P('trc', 'lat', 'lon')
- north_out: float32 [8, 128, 256], P('trc', 'lat', 'lon')
- temperature_out: float32 [8, 128, 256], P('trc', 'lat', 'lon')
- height_out: float32 [128, 256], P('lat', 'lon')
The draws below stay inside these ranges and needn't reach their ends.
Inputs may be any that keep to these rules, and one draw needn't show every extreme that they name: `water_layer_tally`: the number of wet levels of a column, counted from the surface; cells below it, and whole columns with 0, are land.
All inputs are finite; a program needn't handle non-finite values.
Results may differ from the reference program's by a relative error of at most 0.0003.
Values sent between devices are 32-bit elements; how exact they have to be, the bound alone decides.
No kernel may reach another device: no remote copies, remote signals or barrier semaphores. Data moves between devices by JAX's collectives and lax.ppermute only.
A program may use at most 64 MiB of HBM per device.

```python
import math
import jax
import jax.numpy as jnp
from jax import lax

TRACERS = 32
VERTICAL_LAYERS = 8
MERIDIAN_STRIPS = 128
ZONAL_STRIPS = 256


def set_ends(array, key, smallest, largest):
    extent = array.shape
    place = [jax.random.randint(jax.random.fold_in(key, axis), (), 0, extent[axis]) for axis in range(len(extent))]
    array = array.at[tuple(place)].set(smallest)
    longest = extent.index(max(extent))
    place[longest] = (place[longest] + 1) % extent[longest]
    return array.at[tuple(place)].set(largest)


def shard_levels(rng, extent, pieces, smallest, top_value):
    level, own = 1.0, jax.random.fold_in(rng, 6)
    for position, parts in pieces:
        draws = jnp.exp(jax.random.uniform(jax.random.fold_in(own, position), (parts,), jnp.float32, smallest / len(pieces), top_value / len(pieces)))
        level = level * jnp.repeat(draws, extent[position] // parts).reshape([-1 if axis == position else 1 for axis in range(len(extent))])
    return level


def bell_draw(rng, dims, scale, limit, shards=(), kind=jnp.bfloat16):
    result = scale * jax.random.normal(rng, dims, jnp.float32)
    if shards:
        result = result * shard_levels(rng, dims, shards, -0.22, 0.18)
    return jnp.clip(result, -limit, limit).astype(kind)


def setup_inputs(seed: int = 0) -> dict:
    splits = jax.random.split(jax.random.key(seed), 10)
    return {
        "species_concentrations": jnp.clip(jnp.exp(math.log(4.0) - 2.9957323 * jax.random.uniform(splits[0], (TRACERS, VERTICAL_LAYERS, MERIDIAN_STRIPS, ZONAL_STRIPS), jnp.float32) ** shard_levels(splits[0], (TRACERS, VERTICAL_LAYERS, MERIDIAN_STRIPS, ZONAL_STRIPS), ((0, 4), (2, 4), (3, 2)), -0.2, 0.2)), 0.2, 4.0),
        "zonal_velocity_array": bell_draw(splits[1], (VERTICAL_LAYERS, MERIDIAN_STRIPS, ZONAL_STRIPS), 0.16, 2.5, ((0, 4), (1, 4), (2, 2)), jnp.float32),
        "meridional_velocity_array": bell_draw(splits[2], (VERTICAL_LAYERS, MERIDIAN_STRIPS, ZONAL_STRIPS), 0.16, 2.5, ((0, 4), (1, 4), (2, 2)), jnp.float32),
        "thermal_anomaly": bell_draw(splits[3], (VERTICAL_LAYERS, MERIDIAN_STRIPS, ZONAL_STRIPS), 1.0, 6.0, ((0, 4), (1, 4), (2, 2)), jnp.float32),
        "ocean_top_height_grid": bell_draw(splits[4], (MERIDIAN_STRIPS, ZONAL_STRIPS), 0.5, 6.0, ((0, 4), (1, 2)), jnp.float32),
        "water_layer_tally": set_ends(jax.random.randint(splits[5], (MERIDIAN_STRIPS, ZONAL_STRIPS), 0, VERTICAL_LAYERS + 1), jax.random.fold_in(splits[5], 1), 0, VERTICAL_LAYERS).astype(jnp.int32),
        "species_interaction_table": bell_draw(splits[6], (TRACERS, TRACERS), TRACERS ** -0.5, 1.0, (), jnp.float32),
        "species_production_pace": jnp.clip(jnp.exp(jax.random.uniform(splits[7], (TRACERS,), jnp.float32, math.log(0.2), math.log(2.0))), 0.2, 2.0),
        "photon_uptake": jnp.clip(jnp.exp(jax.random.uniform(splits[8], (TRACERS,), jnp.float32, math.log(0.01), math.log(0.1))), 0.01, 0.1),
    }


HIGHEST = lax.Precision.HIGHEST
TIME_STEP = 0.1
GRAVITY = 1.0
VISCOSITY = 0.2
BOTTOM_DRAG = 0.05
DEPTH_SCALE = 0.5
CORIOLIS_SCALE = 0.5
COLUMN_DEPTH = 2.0
WATER_ABSORB = 0.2
HALF_LIGHT = 0.5
REACT_STEP = 0.1
WARMING_WEIGHT = 1.0


def limited_slope(ahead, behind):
    smaller = jnp.minimum(jnp.abs(ahead), jnp.abs(behind))
    return jnp.where(ahead * behind > 0, jnp.where(ahead > 0, smaller, -smaller), jnp.zeros_like(smaller))


def face_flux(before, center, after, beyond, vel_here, vel_next, wet_here, wet_next):
    courant = 0.5 * (vel_here + vel_next) * wet_here * wet_next
    upwind_pos = center + 0.5 * (1.0 - courant) * limited_slope(after - center, center - before)
    upwind_neg = after - 0.5 * (1.0 + courant) * limited_slope(beyond - after, after - center)
    return courant * jnp.where(courant >= 0, upwind_pos, upwind_neg)


def transport(field, flow_east, flow_north, wet):
    free_top_height, width = field.shape[-2], field.shape[-1]
    rows = slice(2, free_top_height - 2)
    cols = slice(2, width - 2)
    flux_x = face_flux(field[..., rows, 0:width - 3], field[..., rows, 1:width - 2], field[..., rows, 2:width - 1], field[..., rows, 3:width],
                       flow_east[..., rows, 1:width - 2], flow_east[..., rows, 2:width - 1], wet[..., rows, 1:width - 2], wet[..., rows, 2:width - 1])
    flux_y = face_flux(field[..., 0:free_top_height - 3, cols], field[..., 1:free_top_height - 2, cols], field[..., 2:free_top_height - 1, cols], field[..., 3:free_top_height, cols],
                       flow_north[..., 1:free_top_height - 2, cols], flow_north[..., 2:free_top_height - 1, cols], wet[..., 1:free_top_height - 2, cols], wet[..., 2:free_top_height - 1, cols])
    return field[..., rows, cols] - (flux_x[..., 1:] - flux_x[..., :-1]) - (flux_y[..., 1:, :] - flux_y[..., :-1, :])


def periodic_pad(field, width):
    field = jnp.concatenate([field[..., -width:], field, field[..., :width]], -1)
    pads = [(0, 0)] * (field.ndim - 2) + [(width, width), (0, 0)]
    return jnp.pad(field, pads)


def lat_next(field):
    return jnp.concatenate([field[..., 1:, :], jnp.zeros_like(field[..., :1, :])], -2)


def lat_prev(field):
    return jnp.concatenate([jnp.zeros_like(field[..., :1, :]), field[..., :-1, :]], -2)


def ocean_core(stacked, north, south, east, west, wet, coriolis):
    count = (stacked.shape[0] - 1) // 2
    zonal_flow_value = stacked[:count]
    meridional_flow_value = stacked[count:2 * count]
    free_top_height = stacked[2 * count]
    lap_east = north[:count] + south[:count] + east[:count] + west[:count] - 4.0 * zonal_flow_value
    lap_north = north[count:2 * count] + south[count:2 * count] + east[count:2 * count] + west[count:2 * count] - 4.0 * meridional_flow_value
    grad_x = 0.5 * (east[2 * count] - west[2 * count])
    grad_y = 0.5 * (north[2 * count] - south[2 * count])
    div_levels = 0.5 * (east[:count] - west[:count]) + 0.5 * (north[count:2 * count] - south[count:2 * count])
    new_east = wet * (zonal_flow_value + TIME_STEP * (coriolis * meridional_flow_value - GRAVITY * grad_x + VISCOSITY * lap_east - BOTTOM_DRAG * zonal_flow_value))
    new_north = wet * (meridional_flow_value + TIME_STEP * (-coriolis * zonal_flow_value - GRAVITY * grad_y + VISCOSITY * lap_north - BOTTOM_DRAG * meridional_flow_value))
    return new_east, new_north, free_top_height, jnp.sum(div_levels, 0)


def light_profile(absorbed, wet, surface):
    levels = absorbed.shape[0]
    layer = (COLUMN_DEPTH / levels) * (WATER_ABSORB + absorbed) * wet
    above = jnp.cumsum(layer, 0) - layer
    top_light = surface[None, :, None] * jnp.exp(-above)
    return top_light * (1.0 - jnp.exp(-layer)), top_light / (top_light + HALF_LIGHT)


def reference(species_concentrations, zonal_velocity_array, meridional_velocity_array, thermal_anomaly, ocean_top_height_grid, water_layer_tally, species_interaction_table, species_production_pace, photon_uptake):
    depth_index = jnp.arange(VERTICAL_LAYERS).astype(jnp.int32)
    wet = (depth_index[:, None, None] < water_layer_tally[None]).astype(jnp.float32)
    lat_index = jnp.arange(MERIDIAN_STRIPS).astype(jnp.float32)
    angle = math.pi * ((lat_index + 0.5) / MERIDIAN_STRIPS - 0.5)
    coriolis = CORIOLIS_SCALE * jnp.sin(angle)[:, None]
    surface = 1.0 + jnp.cos(angle)
    east_start = wet * zonal_velocity_array
    north_start = wet * meridional_velocity_array
    zonal_flow_value, meridional_flow_value, free_top_height = east_start, north_start, ocean_top_height_grid
    for substep in range(2):
        stacked = jnp.concatenate([zonal_flow_value, meridional_flow_value, free_top_height[None]], 0)
        zonal_flow_value, meridional_flow_value, free_top_height, divergence = ocean_core(stacked, lat_next(stacked), lat_prev(stacked),
                                                             jnp.roll(stacked, -1, -1), jnp.roll(stacked, 1, -1), wet, coriolis)
        free_top_height = free_top_height - TIME_STEP * DEPTH_SCALE * divergence
    flow_east = periodic_pad(east_start, 2)
    flow_north = periodic_pad(north_start, 2)
    wet_pad = periodic_pad(wet, 2)

    def move_one(field):
        for substep in range(2):
            field = transport(periodic_pad(field, 2), flow_east, flow_north, wet_pad)
        return field

    moved = lax.map(move_one, species_concentrations)
    absorbed = jnp.einsum("n,nkyx->kyx", photon_uptake, jnp.abs(moved), precision=HIGHEST)
    solar_warming, light_factor = light_profile(absorbed, wet, surface)
    mixed = jnp.einsum("mn,nkyx->mkyx", species_interaction_table, moved, precision=HIGHEST)
    species_postchemistry = moved + wet * REACT_STEP * (mixed + species_production_pace[:, None, None, None] * light_factor * moved)
    return species_postchemistry, zonal_flow_value, meridional_flow_value, thermal_anomaly + WARMING_WEIGHT * solar_warming, free_top_height
```

```python
import functools
import math

import jax
import jax.numpy as jnp
from jax import lax
from jax.experimental import pallas as pl
from jax.experimental.pallas import tpu as pltpu
from jax.sharding import PartitionSpec as P

TIME_STEP = 0.1
GRAVITY = 1.0
VISCOSITY = 0.2
BOTTOM_DRAG = 0.05
DEPTH_SCALE = 0.5
CORIOLIS_SCALE = 0.5
COLUMN_DEPTH = 2.0
WATER_ABSORB = 0.2
HALF_LIGHT = 0.5
REACT_STEP = 0.1
WARMING_WEIGHT = 1.0

SUB = 8
LANES = 128
HALO = 4
GROUP = 16
F32 = jnp.float32


def lane_ids():
    return lax.broadcasted_iota(jnp.int32, (SUB, LANES), 1)


def level_ids():
    return lax.broadcasted_iota(jnp.int32, (SUB, LANES), 0)


def roll(x, shift):
    shift = shift % LANES
    return x if shift == 0 else pltpu.roll(x, shift, 1)


def strip_of(rows):
    lane = lane_ids()
    out = None
    for t, value in enumerate(rows):
        rolled = roll(value, GROUP * t + GROUP // 2)
        if out is None:
            out = rolled
        else:
            out = jnp.where(lane // GROUP == t, rolled, out)
    return out


def middle_mask():
    lane = lane_ids() % GROUP
    return (lane >= 4) & (lane < 12)


def pair_up(first, second):
    return jnp.where(middle_mask(), first, roll(second, 8))


def quad_up(a, b, c, d):
    return jnp.where(lane_ids() < 64, pair_up(a, b), roll(pair_up(c, d), 64))


def merge_left(own, got):
    lane = lane_ids() % GROUP
    return jnp.where((lane >= 4) & (lane < 8), got, own)


def merge_right(own, got):
    lane = lane_ids() % GROUP
    return jnp.where((lane >= 8) & (lane < 12), got, own)


def replicate(strip, group):
    out = jnp.where(lane_ids() // GROUP == group, strip, 0.0)
    for shift in (16, 32, 64):
        out = out + roll(out, shift)
    return out


def over_levels(row):
    return jnp.broadcast_to(row[0:1, :], (SUB, LANES))


def pack_tracers_kernel(x_ref, strip_ref, up_ref, down_ref, cols_ref, cup_ref, cdown_ref):
    count, rows = x_ref.shape[0], x_ref.shape[1] // SUB
    half = rows // 2

    def row_strip(r):
        return strip_of([x_ref[t, pl.ds(r, SUB, stride=rows), :] for t in range(count)])

    for r in range(half):
        low, high = row_strip(r), row_strip(r + half)
        strip_ref[r] = low
        strip_ref[r + half] = high
        cols_ref[r] = pair_up(low, high)
    for j in range(2):
        cdown_ref[j] = pair_up(strip_ref[j], strip_ref[j + 2])
        cup_ref[j] = pair_up(strip_ref[rows - HALO + j], strip_ref[rows - HALO + j + 2])
    for t in range(count):
        for j in range(HALO):
            down_ref[t * HALO + j] = x_ref[t, pl.ds(j, SUB, stride=rows), :]
            up_ref[t * HALO + j] = x_ref[t, pl.ds(rows - HALO + j, SUB, stride=rows), :]


def pack_tracers(x):
    count, rows = x.shape[0], x.shape[1] // SUB
    tile = lambda n: jax.ShapeDtypeStruct((n, SUB, LANES), F32)
    return pl.pallas_call(
        pack_tracers_kernel,
        out_shape=(
            tile(rows),
            tile(count * HALO),
            tile(count * HALO),
            tile(rows // 2),
            tile(2),
            tile(2),
        ),
        name="pack_tracers",
    )(x)


def pack_flow_kernel(
    place_ref, own_ref, *refs
):
    (peers, (tally_ref, height_ref, cup_ref, cdown_ref), (flow_ref, strip_ref, cols_ref, up_ref, down_ref, dup_ref, ddown_ref, all_ref)) = (
        refs[:-12],
        refs[-12:-8],
        refs[-8:],
    )
    rows = tally_ref.shape[0]
    span = own_ref.shape[1]
    place = place_ref[0]
    for k, ref in enumerate((own_ref,) + tuple(peers)):
        base = pl.multiple_of((place ^ k) * span, SUB)
        for f in range(2):
            all_ref[f, pl.ds(base, span), :] = ref[f]
    level = level_ids()
    for r in range(rows):
        tally = jnp.broadcast_to(tally_ref[r : r + 1, :], (SUB, LANES))
        height = jnp.broadcast_to(height_ref[r : r + 1, :], (SUB, LANES))
        wet = level < tally
        east = jnp.where(wet, all_ref[0, pl.ds(r, SUB, stride=rows), :], 0.0)
        north = jnp.where(wet, all_ref[1, pl.ds(r, SUB, stride=rows), :], 0.0)
        aux = jnp.where(level == 0, tally.astype(F32), height)
        for f, value in enumerate((east, north, aux)):
            flow_ref[f * rows + r] = value
            if r < HALO:
                down_ref[f * HALO + r] = value
            if r >= rows - HALO:
                up_ref[f * HALO + r - (rows - HALO)] = value
        strip_ref[r] = strip_of([east, north, aux])
    quarter = rows // 4
    for r in range(quarter):
        cols_ref[r] = quad_up(*[strip_ref[r + quarter * q] for q in range(4)])
    for j in range(2):
        dup_ref[j] = cup_ref[j]
        ddown_ref[j] = cdown_ref[j]
    dup_ref[2] = quad_up(*[strip_ref[rows - HALO + j] for j in range(HALO)])
    ddown_ref[2] = quad_up(*[strip_ref[j] for j in range(HALO)])


def pack_flow(place, own, peers, tally, height, cup, cdown):
    rows = tally.shape[0]
    tile = lambda n: jax.ShapeDtypeStruct((n, SUB, LANES), F32)
    vmem = pl.BlockSpec(memory_space=pltpu.VMEM)
    return pl.pallas_call(
        pack_flow_kernel,
        in_specs=[pl.BlockSpec(memory_space=pltpu.SMEM)] + [vmem] * (5 + len(peers)),
        out_shape=(
            tile(3 * rows),
            tile(rows),
            tile(rows // 4),
            tile(3 * HALO),
            tile(3 * HALO),
            tile(3),
            tile(3),
        ),
        scratch_shapes=[pltpu.VMEM((2, SUB * rows, LANES), F32)],
        name="pack_flow",
    )(place, own, *peers, tally, height, cup, cdown)


def flow_row(flow_ref, up_ref, down_ref, f, r, rows):
    if r < 0:
        return up_ref[f * HALO + HALO + r]
    if r >= rows:
        return down_ref[f * HALO + r - rows]
    return flow_ref[f * rows + r]


def quad_row(ref, j, quarter):
    q, r = divmod(j, quarter)
    return roll(ref[r], -(8 * (q % 2) + 64 * (q // 2)))


def flow_strips(flow_ref, strip_ref, up_ref, down_ref, colsl_ref, colsr_ref, corners, r, rows):
    (ul_ref, ur_ref, dl_ref, dr_ref) = corners
    if r < 0:
        own = strip_of([flow_row(flow_ref, up_ref, down_ref, f, r, rows) for f in range(3)])
        left = quad_row(ul_ref.at[pl.ds(2, 1)], r + HALO, 1)
        right = quad_row(ur_ref.at[pl.ds(2, 1)], r + HALO, 1)
    elif r >= rows:
        own = strip_of([flow_row(flow_ref, up_ref, down_ref, f, r, rows) for f in range(3)])
        left = quad_row(dl_ref.at[pl.ds(2, 1)], r - rows, 1)
        right = quad_row(dr_ref.at[pl.ds(2, 1)], r - rows, 1)
    else:
        own = strip_ref[r]
        left = quad_row(colsl_ref, r, rows // 4)
        right = quad_row(colsr_ref, r, rows // 4)
    return merge_left(own, left), merge_right(own, right)


def limited(ahead, behind):
    return jnp.maximum(
        jnp.minimum(ahead, jnp.maximum(behind, 0.0)), jnp.minimum(behind, 0.0)
    )


def face_pair(vel, vel_next, wet, wet_next):
    a = jnp.where(wet & wet_next, 0.5 * (vel + vel_next), 0.0)
    size = jnp.abs(a)
    return a, 0.5 * size * (1.0 - size)


def transport_rows(load, store, ax_ref, bx_ref, ay_ref, by_ref, kind, first, last, xo, yo):
    before, here, after = load(first - 2), load(first - 1), load(first)
    slope_y = limited(after - here, here - before)
    diff = after - here
    flux_below = None
    row, nxt = here, after
    for i in range(first - 1, last):
        far = load(i + 2)
        diff_next = far - nxt
        slope_next = limited(diff_next, diff)
        ay, by = ay_ref[kind, yo + i], by_ref[kind, yo + i]
        positive = ay >= 0.0
        flux = ay * jnp.where(positive, row, nxt) + by * jnp.where(positive, slope_y, slope_next)
        if flux_below is not None:
            ax, bx = ax_ref[kind, xo + i], bx_ref[kind, xo + i]
            east = roll(row, -1)
            dx = east - row
            sx = limited(dx, roll(dx, 1))
            sx_east = roll(sx, -1)
            pos = ax >= 0.0
            fx = ax * jnp.where(pos, row, east) + bx * jnp.where(pos, sx, sx_east)
            store(i, row - (fx - roll(fx, 1)) - (flux - flux_below))
        flux_below = flux
        row, nxt, slope_y, diff = nxt, far, slope_next, diff_next


def transport_kernel(
    place_ref,
    x_ref,
    strip_ref,
    up_ref,
    down_ref,
    colsl_ref,
    colsr_ref,
    flow_ref,
    fstrip_ref,
    fup_ref,
    fdown_ref,
    fcolsl_ref,
    fcolsr_ref,
    ul_ref,
    ur_ref,
    dl_ref,
    dr_ref,
    *refs,
):
    *outs, ext_ref, ax_ref, bx_ref, ay_ref, by_ref, first_ref, moved_ref = refs
    count, rows = x_ref.shape[0], x_ref.shape[1] // SUB
    half = rows // 2
    place = place_ref[0]
    level = level_ids()
    corners = (ul_ref, ur_ref, dl_ref, dr_ref)

    for t in range(count):
        for j in range(HALO):
            ext_ref[t, j] = up_ref[t * HALO + j]
            ext_ref[t, HALO + rows + j] = down_ref[t * HALO + j]
        for r in range(rows):
            ext_ref[t, HALO + r] = x_ref[t, pl.ds(r, SUB, stride=rows), :]
    for r in range(-HALO, rows + HALO):
        if r < 0 or r >= rows:
            src = up_ref if r < 0 else down_ref
            j = r + HALO if r < 0 else r - rows
            lref, rref = (ul_ref, ur_ref) if r < 0 else (dl_ref, dr_ref)
            own = strip_of([src[t * HALO + j] for t in range(count)])
            left, right = lref[j % 2], rref[j % 2]
            if j >= 2:
                left, right = roll(left, -8), roll(right, -8)
        else:
            own = strip_ref[r]
            left, right = colsl_ref[r % half], colsr_ref[r % half]
            if r >= half:
                left, right = roll(left, -8), roll(right, -8)
        ext_ref[count, HALO + r] = merge_left(own, left)
        ext_ref[count + 1, HALO + r] = merge_right(own, right)

    previous = None
    for r in range(-HALO, rows + HALO):
        aux = flow_row(flow_ref, fup_ref, fdown_ref, 2, r, rows)
        main = (
            flow_row(flow_ref, fup_ref, fdown_ref, 0, r, rows),
            flow_row(flow_ref, fup_ref, fdown_ref, 1, r, rows),
            level.astype(F32) < over_levels(aux),
        )
        strips = flow_strips(
            flow_ref, fstrip_ref, fup_ref, fdown_ref, fcolsl_ref, fcolsr_ref, corners, r, rows
        )
        kinds = [main]
        for s in strips:
            kinds.append(
                (
                    replicate(s, 0),
                    replicate(s, 1),
                    level.astype(F32) < over_levels(replicate(s, 2)),
                )
            )
        for kind, (east, north, wet) in enumerate(kinds):
            if -2 <= r < rows + 2:
                wetf = jnp.where(wet, 1.0, 0.0)
                a, b = face_pair(east, roll(east, -1), wet, roll(wetf, -1) > 0.5)
                ax_ref[kind, r + 2] = a
                bx_ref[kind, r + 2] = b
            if previous is not None and -3 <= r - 1 < rows + 2:
                _, vbelow, wbelow = previous[kind]
                a, b = face_pair(vbelow, north, wbelow, wet)
                ay_ref[kind, r - 1 + 3] = a
                by_ref[kind, r - 1 + 3] = b
        previous = kinds

    def one(p, carry):
        kind = jnp.maximum(p - (count - 1), 0)
        transport_rows(
            lambda i: ext_ref[p, HALO + i],
            lambda i, value: first_ref.__setitem__(i + 2, value),
            ax_ref, bx_ref, ay_ref, by_ref, kind, -2, rows + 2, 2, 3,
        )
        transport_rows(
            lambda i: first_ref[2 + i],
            lambda i, value: moved_ref.__setitem__((p, i), value),
            ax_ref, bx_ref, ay_ref, by_ref, kind, 0, rows, 2, 3,
        )
        return carry

    lax.fori_loop(0, count + 2, one, 0)

    lane = lane_ids()
    edge = (lane < 4) | (lane >= LANES - 4)
    from_right = (lane % GROUP >= 4) & (lane % GROUP < 8)
    share = rows // len(outs)
    for k, out_ref in enumerate(outs):
        base = (place ^ k) * share
        for r in range(share):
            joined = jnp.where(from_right, moved_ref[count + 1, base + r], moved_ref[count, base + r])
            for t in range(count):
                out_ref[t * share + r] = jnp.where(
                    edge, roll(joined, -(GROUP * t + 8)), moved_ref[t, base + r]
                )


def transport(place, shards, x, tracer_parts, flow_parts):
    count, rows = x.shape[0], x.shape[1] // SUB
    vmem = pl.BlockSpec(memory_space=pltpu.VMEM)
    tile = lambda *n: pltpu.VMEM(n + (SUB, LANES), F32)
    args = (x,) + tracer_parts + flow_parts
    return pl.pallas_call(
        transport_kernel,
        in_specs=[pl.BlockSpec(memory_space=pltpu.SMEM)] + [vmem] * len(args),
        out_shape=tuple(
            jax.ShapeDtypeStruct((count * rows // shards, SUB, LANES), F32) for _ in range(shards)
        ),
        scratch_shapes=[
            tile(count + 2, rows + 2 * HALO),
            tile(3, rows + 4),
            tile(3, rows + 4),
            tile(3, rows + 5),
            tile(3, rows + 5),
            tile(rows + 4),
            tile(count + 2, rows),
        ],
        name="transport",
    )(place, *args)


def react_kernel(place_ref, table_ref, pace_ref, uptake_ref, surface_ref, tally_ref, *refs):
    shards = (len(refs) - 3) // 2
    ins, outs = refs[:shards], refs[shards : 2 * shards]
    light_ref, wet_ref, heat_ref = refs[2 * shards :]
    total = pace_ref.shape[0]
    count = total // shards
    share = ins[0].shape[0] // count
    place = place_ref[0]
    level = level_ids()

    for r in range(share):
        row = place * share + r
        tally = jnp.broadcast_to(tally_ref[pl.ds(row, 1), :], (SUB, LANES))
        surface = jnp.broadcast_to(surface_ref[pl.ds(row, 1), :], (SUB, LANES))
        wet = jnp.where(level < tally, 1.0, 0.0)
        absorbed = jnp.zeros((SUB, LANES), F32)
        for k, ref in enumerate(ins):
            for t in range(count):
                absorbed = absorbed + uptake_ref[(place ^ k) * count + t] * jnp.abs(ref[t * share + r])
        layer = (COLUMN_DEPTH / SUB) * (WATER_ABSORB + absorbed) * wet
        total_depth = jnp.where(level >= 1, pltpu.roll(layer, 1, 0), 0.0)
        for shift in (1, 2, 4):
            total_depth = total_depth + jnp.where(
                level >= shift, pltpu.roll(total_depth, shift, 0), 0.0
            )
        top = surface * jnp.exp(-total_depth)
        heat_ref[pl.ds(r * SUB, SUB), :] = top * (1.0 - jnp.exp(-layer))
        light_ref[r] = REACT_STEP * wet * (top / (top + HALF_LIGHT))
        wet_ref[r] = REACT_STEP * wet

    block = 4
    for k, out_ref in enumerate(outs):
        for m0 in range(0, count, block):
            dest = [(place ^ k) * count + m0 + j for j in range(block)]
            acc = [[None] * share for _ in range(block)]
            for kk, ref in enumerate(ins):
                for t in range(count):
                    n = (place ^ kk) * count + t
                    values = [ref[t * share + r] for r in range(share)]
                    for j in range(block):
                        c = table_ref[dest[j], n]
                        for r in range(share):
                            term = c * values[r]
                            acc[j][r] = term if acc[j][r] is None else acc[j][r] + term
            for j in range(block):
                pace = pace_ref[dest[j]]
                for r in range(share):
                    own = ins[k][(m0 + j) * share + r]
                    out_ref[(m0 + j) * share + r] = (
                        own + wet_ref[r] * acc[j][r] + pace * (light_ref[r] * own)
                    )
        own_levels = SUB // shards
        for q in range(own_levels):
            start = (place ^ k) * own_levels + q
            out_ref[count * share + q] = heat_ref[pl.ds(start, share, stride=SUB), :]


def react(place, table, pace, uptake, surface, tally, blocks):
    shards = len(blocks)
    share = blocks[0].shape[0] // (pace.shape[0] // shards)
    smem = pl.BlockSpec(memory_space=pltpu.SMEM)
    vmem = pl.BlockSpec(memory_space=pltpu.VMEM)
    return pl.pallas_call(
        react_kernel,
        in_specs=[smem] * 4 + [vmem] * (2 + shards),
        out_shape=tuple(
            jax.ShapeDtypeStruct((b.shape[0] + SUB // shards, SUB, LANES), F32) for b in blocks
        ),
        scratch_shapes=[
            pltpu.VMEM((share, SUB, LANES), F32),
            pltpu.VMEM((share, SUB, LANES), F32),
            pltpu.VMEM((share * SUB, LANES), F32),
        ],
        name="react",
    )(place, table, pace, uptake, surface, tally, *blocks)


def finish_kernel(place_ref, thermal_ref, *refs):
    *ins, out_ref, temp_ref = refs
    shards = len(ins)
    count = out_ref.shape[0]
    rows = out_ref.shape[1] // SUB
    share = rows // shards
    place = place_ref[0]
    own_levels = SUB // shards
    for k, ref in enumerate(ins):
        base = (place ^ k) * share
        for m in range(count):
            for lev in range(SUB):
                dst = pl.multiple_of(lev * rows + base, SUB)
                out_ref[m, pl.ds(dst, share), :] = ref[pl.ds(m * share * SUB + lev, share, stride=SUB), :]
        for q in range(own_levels):
            dst = pl.multiple_of(q * rows + base, SUB)
            heat = ref[pl.ds((count * share + q) * SUB, share), :]
            temp_ref[pl.ds(dst, share), :] = thermal_ref[pl.ds(dst, share), :] + WARMING_WEIGHT * heat


def finish(place, thermal, blocks, count, rows):
    vmem = pl.BlockSpec(memory_space=pltpu.VMEM)
    flat = [b.reshape(-1, LANES) for b in blocks]
    return pl.pallas_call(
        finish_kernel,
        in_specs=[pl.BlockSpec(memory_space=pltpu.SMEM)] + [vmem] * (1 + len(flat)),
        out_shape=(
            jax.ShapeDtypeStruct((count, SUB * rows, LANES), F32),
            jax.ShapeDtypeStruct(thermal.shape, F32),
        ),
        name="finish",
    )(place, thermal, *flat)


def level_sum(x):
    for shift in (4, 2, 1):
        x = x + pltpu.roll(x, shift, 0)
    return x


def momentum_kernel(
    place_ref,
    coriolis_ref,
    inside_ref,
    flow_ref,
    strip_ref,
    fup_ref,
    fdown_ref,
    colsl_ref,
    colsr_ref,
    ul_ref,
    ur_ref,
    dl_ref,
    dr_ref,
    east_ref,
    north_ref,
    height_ref,
    a_ref,
    b_ref,
    c_ref,
):
    rows = height_ref.shape[0]
    own_levels = east_ref.shape[0] // rows
    place = place_ref[0]
    lane = lane_ids()
    level = level_ids().astype(F32)
    corners = (ul_ref, ur_ref, dl_ref, dr_ref)
    for r in range(-2, rows + 2):
        east, north, aux = (flow_row(flow_ref, fup_ref, fdown_ref, f, r, rows) for f in range(3))
        left, right = flow_strips(
            flow_ref, strip_ref, fup_ref, fdown_ref, colsl_ref, colsr_ref, corners, r, rows
        )
        both = [
            jnp.where(lane < GROUP, roll(left, -GROUP * f), roll(right, GROUP - GROUP * f))
            for f in range(3)
        ]
        for p, (u, v, w) in enumerate(((east, north, aux), both)):
            wet = jnp.where(level < over_levels(w), 1.0, 0.0)
            h = jnp.broadcast_to(w[1:2, :], (SUB, LANES))
            for f, value in enumerate((u, v, h, wet)):
                a_ref[p, f, r + 2] = value

    def substep(src, offset, put, first, last):
        for p in range(2):
            for i in range(first, last):
                g = lambda f, d: src[p, f, i + offset + d]
                u, v, h = g(0, 0), g(1, 0), g(2, 0)
                un, us, vn, vs, hn, hs = g(0, 1), g(0, -1), g(1, 1), g(1, -1), g(2, 1), g(2, -1)
                wet = a_ref[p, 3, i + 2]
                cor = jnp.broadcast_to(coriolis_ref[i + 2 : i + 3, :], (SUB, LANES))
                ue, uw, ve, vw, he, hw = (
                    roll(u, -1), roll(u, 1), roll(v, -1), roll(v, 1), roll(h, -1), roll(h, 1),
                )
                div = level_sum(0.5 * (ue - uw) + 0.5 * (vn - vs))
                nu = wet * (
                    u
                    + TIME_STEP
                    * (
                        cor * v
                        - GRAVITY * (0.5 * (he - hw))
                        + VISCOSITY * (un + us + ue + uw - 4.0 * u)
                        - BOTTOM_DRAG * u
                    )
                )
                nv = wet * (
                    v
                    + TIME_STEP
                    * (
                        -cor * u
                        - GRAVITY * (0.5 * (hn - hs))
                        + VISCOSITY * (vn + vs + ve + vw - 4.0 * v)
                        - BOTTOM_DRAG * v
                    )
                )
                nh = h - TIME_STEP * DEPTH_SCALE * div
                put(p, i, nu, nv, nh)

    def put_first(p, i, nu, nv, nh):
        inside = jnp.broadcast_to(inside_ref[i + 2 : i + 3, :], (SUB, LANES))
        for f, value in enumerate((nu, nv, nh * inside)):
            b_ref[p, f, i + 1] = value

    def put_second(p, i, nu, nv, nh):
        for f, value in enumerate((nu, nv, nh)):
            c_ref[p, f, pl.ds(i * SUB, SUB), :] = value

    substep(a_ref, 2, put_first, -1, rows + 1)
    substep(b_ref, 1, put_second, 0, rows)

    def joined(f, start):
        lane8 = lax.broadcasted_iota(jnp.int32, (SUB, LANES), 1)
        main = c_ref[0, f, pl.ds(start, SUB, stride=SUB), :]
        edge = c_ref[1, f, pl.ds(start, SUB, stride=SUB), :]
        out = jnp.where(lane8 < 2, roll(edge, -8), main)
        return jnp.where(lane8 >= LANES - 2, roll(edge, LANES - 2 - (GROUP + 6)), out)

    for j in range(rows // SUB):
        for q in range(own_levels):
            lev = place * own_levels + q
            dst = q * rows + j * SUB
            east_ref[dst : dst + SUB, :] = joined(0, j * SUB * SUB + lev)
            north_ref[dst : dst + SUB, :] = joined(1, j * SUB * SUB + lev)
        height_ref[j * SUB : (j + 1) * SUB, :] = joined(2, j * SUB * SUB)


def momentum(place, coriolis, inside, flow_parts, rows, own_levels):
    vmem = pl.BlockSpec(memory_space=pltpu.VMEM)
    args = (coriolis, inside) + flow_parts
    return pl.pallas_call(
        momentum_kernel,
        in_specs=[pl.BlockSpec(memory_space=pltpu.SMEM)] + [vmem] * len(args),
        out_shape=(
            jax.ShapeDtypeStruct((own_levels * rows, LANES), F32),
            jax.ShapeDtypeStruct((own_levels * rows, LANES), F32),
            jax.ShapeDtypeStruct((rows, LANES), F32),
        ),
        scratch_shapes=[
            pltpu.VMEM((2, 4, rows + 4, SUB, LANES), F32),
            pltpu.VMEM((2, 3, rows + 2, SUB, LANES), F32),
            pltpu.VMEM((2, 3, rows * SUB, LANES), F32),
        ],
        name="momentum",
    )(place, *args)


def to_peer(block, k):
    count = lax.axis_size("trc")
    return lax.ppermute(block, "trc", [(i, i ^ k) for i in range(count)])


def shifted(block, dlat, dlon):
    nlat, nlon = lax.axis_size("lat"), lax.axis_size("lon")
    pairs = [
        (i * nlon + j, (i + dlat) * nlon + (j + dlon) % nlon)
        for i in range(nlat)
        for j in range(nlon)
        if 0 <= i + dlat < nlat
    ]
    return lax.ppermute(block, ("lat", "lon"), pairs)


def both_sides(block, dlat):
    left = shifted(block, dlat, 1)
    if lax.axis_size("lon") == 2:
        return left, left
    return left, shifted(block, dlat, -1)


def body(
    species_concentrations,
    zonal_velocity_array,
    meridional_velocity_array,
    thermal_anomaly,
    ocean_top_height_grid,
    water_layer_tally,
    species_interaction_table,
    species_production_pace,
    photon_uptake,
):
    count, levels, rows, cols = species_concentrations.shape
    own_levels = zonal_velocity_array.shape[0]
    shards = lax.axis_size("trc")
    assert levels == SUB and cols == LANES and count * GROUP == LANES and shards & (shards - 1) == 0
    trc_place = lax.axis_index("trc")
    place = trc_place.astype(jnp.int32).reshape(1)
    lat_total = rows * lax.axis_size("lat")
    lat_first = lax.axis_index("lat") * rows
    lat_global = (lat_first + jnp.arange(-2, rows + 2)).astype(F32)
    angle = math.pi * ((lat_global + 0.5) / lat_total - 0.5)
    spread = lambda v: jnp.broadcast_to(v[:, None], (v.shape[0], LANES))
    coriolis = spread(CORIOLIS_SCALE * jnp.sin(angle))
    surface = spread(1.0 + jnp.cos(angle[2:-2]))
    inside = spread(((lat_global >= 0) & (lat_global < lat_total)).astype(F32))

    x = species_concentrations.reshape(count, levels * rows, cols)
    own = jnp.stack([zonal_velocity_array, meridional_velocity_array]).reshape(
        2, own_levels * rows, cols
    )
    peers = [to_peer(own, k) for k in range(1, shards)]
    strip, up, down, cols_msg, cup, cdown = pack_tracers(x)
    up_in, down_in = shifted(up, 1, 0), shifted(down, -1, 0)
    left_in, right_in = both_sides(cols_msg, 0)
    flow, fstrip, fcols, fup, fdown, dup, ddown = pack_flow(
        place, own, peers, water_layer_tally, ocean_top_height_grid, cup, cdown
    )
    fup_in, fdown_in = shifted(fup, 1, 0), shifted(fdown, -1, 0)
    fleft_in, fright_in = both_sides(fcols, 0)
    ul, ur = both_sides(dup, 1)
    dl, dr = both_sides(ddown, -1)
    flow_parts = (flow, fstrip, fup_in, fdown_in, fleft_in, fright_in, ul, ur, dl, dr)
    moved = transport(
        place, shards, x, (strip, up_in, down_in, left_in, right_in), flow_parts
    )
    blocks = [moved[0]] + [to_peer(moved[k], k) for k in range(1, shards)]
    east_out, north_out, height_out = momentum(
        place, coriolis, inside, flow_parts, rows, own_levels
    )
    reacted = react(
        place,
        species_interaction_table,
        species_production_pace,
        photon_uptake,
        surface,
        water_layer_tally,
        blocks,
    )
    back = [reacted[0]] + [to_peer(reacted[k], k) for k in range(1, shards)]
    updated, temperature = finish(
        place, thermal_anomaly.reshape(own_levels * rows, cols), back, count, rows
    )
    vel = (own_levels, rows, cols)
    return (
        updated.reshape(count, levels, rows, cols),
        east_out.reshape(vel),
        north_out.reshape(vel),
        temperature.reshape(vel),
        height_out,
    )


def solution(mesh):
    return jax.shard_map(
        body,
        mesh=mesh,
        in_specs=(
            P("trc", None, "lat", "lon"),
            P("trc", "lat", "lon"),
            P("trc", "lat", "lon"),
            P("trc", "lat", "lon"),
            P("lat", "lon"),
            P("lat", "lon"),
            P(),
            P(),
            P(),
        ),
        out_specs=(
            P("trc", None, "lat", "lon"),
            P("trc", "lat", "lon"),
            P("trc", "lat", "lon"),
            P("trc", "lat", "lon"),
            P("lat", "lon"),
        ),
        check_vma=False,
    )
```

```python
import functools
import math

import jax
import jax.numpy as jnp
from jax import lax
from jax.experimental import pallas as pl
from jax.experimental.pallas import tpu as pltpu
from jax.sharding import PartitionSpec as P

TIME_STEP = 0.1
GRAVITY = 1.0
VISCOSITY = 0.2
BOTTOM_DRAG = 0.05
DEPTH_SCALE = 0.5
CORIOLIS_SCALE = 0.5
COLUMN_DEPTH = 2.0
WATER_ABSORB = 0.2
HALF_LIGHT = 0.5
REACT_STEP = 0.1
WARMING_WEIGHT = 1.0

SUB = 8
LANES = 128
HALO = 4
GROUP = 16
F32 = jnp.float32


def lane_ids():
    return lax.broadcasted_iota(jnp.int32, (SUB, LANES), 1)


def level_ids():
    return lax.broadcasted_iota(jnp.int32, (SUB, LANES), 0)


def roll(x, shift):
    shift = shift % LANES
    return x if shift == 0 else pltpu.roll(x, shift, 1)


def strip_of(rows):
    lane = lane_ids()
    out = None
    for t, value in enumerate(rows):
        rolled = roll(value, GROUP * t + GROUP // 2)
        if out is None:
            out = rolled
        else:
            out = jnp.where(lane // GROUP == t, rolled, out)
    return out


def middle_mask():
    lane = lane_ids() % GROUP
    return (lane >= 4) & (lane < 12)


def pair_up(first, second):
    return jnp.where(middle_mask(), first, roll(second, 8))


def quad_up(a, b, c, d):
    return jnp.where(lane_ids() < 64, pair_up(a, b), roll(pair_up(c, d), 64))


def merge_left(own, got):
    lane = lane_ids() % GROUP
    return jnp.where((lane >= 4) & (lane < 8), got, own)


def merge_right(own, got):
    lane = lane_ids() % GROUP
    return jnp.where((lane >= 8) & (lane < 12), got, own)


def replicate(strip, group):
    out = jnp.where(lane_ids() // GROUP == group, strip, 0.0)
    for shift in (16, 32, 64):
        out = out + roll(out, shift)
    return out


def over_levels(row):
    return jnp.broadcast_to(row[0:1, :], (SUB, LANES))


def pack_tracers_kernel(x_ref, strip_ref, up_ref, down_ref, cols_ref, cup_ref, cdown_ref):
    count, rows = x_ref.shape[0], x_ref.shape[1] // SUB
    half = rows // 2

    def row_strip(r):
        return strip_of([x_ref[t, pl.ds(r, SUB, stride=rows), :] for t in range(count)])

    for r in range(half):
        low, high = row_strip(r), row_strip(r + half)
        strip_ref[r] = low
        strip_ref[r + half] = high
        cols_ref[r] = pair_up(low, high)
    for j in range(2):
        cdown_ref[j] = pair_up(strip_ref[j], strip_ref[j + 2])
        cup_ref[j] = pair_up(strip_ref[rows - HALO + j], strip_ref[rows - HALO + j + 2])
    for t in range(count):
        for j in range(HALO):
            down_ref[t * HALO + j] = x_ref[t, pl.ds(j, SUB, stride=rows), :]
            up_ref[t * HALO + j] = x_ref[t, pl.ds(rows - HALO + j, SUB, stride=rows), :]


def pack_tracers(x):
    count, rows = x.shape[0], x.shape[1] // SUB
    tile = lambda n: jax.ShapeDtypeStruct((n, SUB, LANES), F32)
    return pl.pallas_call(
        pack_tracers_kernel,
        out_shape=(
            tile(rows),
            tile(count * HALO),
            tile(count * HALO),
            tile(rows // 2),
            tile(2),
            tile(2),
        ),
        name="pack_tracers",
    )(x)


def pack_flow_kernel(place_ref, own_ref, *refs):
    peers, rest = refs[:-15], refs[-15:]
    tally_ref, height_ref, tup_ref, tdown_ref, tcols_ref, cup_ref, cdown_ref = rest[:7]
    flow_ref, strip_ref, cols_ref, up_ref, down_ref, dup_ref, ddown_ref, all_ref = rest[7:]
    rows = tally_ref.shape[0]
    span = own_ref.shape[1]
    place = place_ref[0]
    for k, ref in enumerate((own_ref,) + tuple(peers)):
        base = pl.multiple_of((place ^ k) * span, SUB)
        for f in range(2):
            all_ref[f, pl.ds(base, span), :] = ref[f]
    for src, dst in ((tup_ref, up_ref), (tdown_ref, down_ref), (tcols_ref, cols_ref), (cup_ref, dup_ref), (cdown_ref, ddown_ref)):
        dst[0 : src.shape[0]] = src[...]
    nrow, ncol, ncorner = tup_ref.shape[0], tcols_ref.shape[0], cup_ref.shape[0]
    level = level_ids()
    tally_all = tally_ref[...].astype(F32)
    pair_all = jnp.minimum(tally_all, pltpu.roll(tally_all, LANES - 1, 1))
    wide = lambda v, r: jnp.broadcast_to(v[r : r + 1, :], (SUB, LANES))
    for r in range(rows):
        tally, height, pair = wide(tally_all, r), wide(height_ref, r), wide(pair_all, r)
        wet = level.astype(F32) < tally
        east = jnp.where(wet, all_ref[0, pl.ds(r, SUB, stride=rows), :], 0.0)
        north = jnp.where(wet, all_ref[1, pl.ds(r, SUB, stride=rows), :], 0.0)
        aux = jnp.where(level == 0, tally, jnp.where(level == 1, height, pair))
        for f, value in enumerate((east, north, aux)):
            flow_ref[f * rows + r] = value
            if r < HALO:
                down_ref[nrow + f * HALO + r] = value
            if r >= rows - HALO:
                up_ref[nrow + f * HALO + r - (rows - HALO)] = value
        strip_ref[r] = strip_of([east, north, aux])
    quarter = rows // 4
    for r in range(quarter):
        cols_ref[ncol + r] = quad_up(*[strip_ref[r + quarter * q] for q in range(4)])
    dup_ref[ncorner] = quad_up(*[strip_ref[rows - HALO + j] for j in range(HALO)])
    ddown_ref[ncorner] = quad_up(*[strip_ref[j] for j in range(HALO)])


def pack_flow(place, own, peers, tally, height, messages):
    rows = tally.shape[0]
    tile = lambda n: jax.ShapeDtypeStruct((n, SUB, LANES), F32)
    vmem = pl.BlockSpec(memory_space=pltpu.VMEM)
    tup, tdown, tcols, cup, cdown = messages
    return pl.pallas_call(
        pack_flow_kernel,
        in_specs=[pl.BlockSpec(memory_space=pltpu.SMEM)] + [vmem] * (3 + len(peers) + len(messages)),
        out_shape=(
            tile(3 * rows),
            tile(rows),
            tile(tcols.shape[0] + rows // 4),
            tile(tup.shape[0] + 3 * HALO),
            tile(tdown.shape[0] + 3 * HALO),
            tile(cup.shape[0] + 1),
            tile(cdown.shape[0] + 1),
        ),
        scratch_shapes=[pltpu.VMEM((2, SUB * rows, LANES), F32)],
        name="pack_flow",
    )(place, own, *peers, tally, height, *messages)


class Flow:
    def __init__(self, flow_ref, strip_ref, up_ref, down_ref, left_ref, right_ref, corners):
        self.flow, self.strip, self.up, self.down = flow_ref, strip_ref, up_ref, down_ref
        self.left, self.right, self.corners = left_ref, right_ref, corners
        self.rows = strip_ref.shape[0]
        self.row_base = up_ref.shape[0] - 3 * HALO
        self.col_base = left_ref.shape[0] - self.rows // 4
        self.corner_base = corners[0].shape[0] - 1

    def row(self, f, r):
        if r < 0:
            return self.up[self.row_base + f * HALO + HALO + r]
        if r >= self.rows:
            return self.down[self.row_base + f * HALO + r - self.rows]
        return self.flow[f * self.rows + r]

    def strips(self, r):
        if 0 <= r < self.rows:
            quarter = self.rows // 4
            q, j = divmod(r, quarter)
            own = self.strip[r]
            left, right = self.left[self.col_base + j], self.right[self.col_base + j]
        else:
            own = strip_of([self.row(f, r) for f in range(3)])
            q = r + HALO if r < 0 else r - self.rows
            lref, rref = self.corners[:2] if r < 0 else self.corners[2:]
            left, right = lref[self.corner_base], rref[self.corner_base]
        shift = -(8 * (q % 2) + 64 * (q // 2))
        return merge_left(own, roll(left, shift)), merge_right(own, roll(right, shift))


def limited(ahead, behind):
    return jnp.maximum(
        jnp.minimum(ahead, jnp.maximum(behind, 0.0)), jnp.minimum(behind, 0.0)
    )


def face_pair(vel, vel_next, wet):
    a = jnp.where(wet, 0.5 * (vel + vel_next), 0.0)
    size = jnp.abs(a)
    return a, 0.5 * size * (1.0 - size)


def transport_rows(load, store, ax_ref, bx_ref, ay_ref, by_ref, kind, first, last, xo, yo):
    before, here, after = load(first - 2), load(first - 1), load(first)
    slope_y = limited(after - here, here - before)
    diff = after - here
    flux_below = None
    row, nxt = here, after
    for i in range(first - 1, last):
        far = load(i + 2)
        diff_next = far - nxt
        slope_next = limited(diff_next, diff)
        ay, by = ay_ref[kind, yo + i], by_ref[kind, yo + i]
        positive = ay >= 0.0
        flux = ay * jnp.where(positive, row, nxt) + by * jnp.where(positive, slope_y, slope_next)
        if flux_below is not None:
            ax, bx = ax_ref[kind, xo + i], bx_ref[kind, xo + i]
            east = roll(row, -1)
            dx = east - row
            sx = limited(dx, roll(dx, 1))
            sx_east = roll(sx, -1)
            pos = ax >= 0.0
            fx = ax * jnp.where(pos, row, east) + bx * jnp.where(pos, sx, sx_east)
            store(i, row - (fx - roll(fx, 1)) - (flux - flux_below))
        flux_below = flux
        row, nxt, slope_y, diff = nxt, far, slope_next, diff_next


def select_lanes(moves):
    parts = []
    source = lax.broadcasted_iota(jnp.int32, (LANES, LANES), 0)
    target = lax.broadcasted_iota(jnp.int32, (LANES, LANES), 1)
    for f, d in moves:
        parts.append(jnp.where(source == GROUP * f + target % GROUP + d, 1.0, 0.0))
    return jnp.concatenate(parts, axis=1)


def exact_dot(a, b):
    return jnp.dot(a, b, precision=lax.Precision.HIGHEST, preferred_element_type=F32)


def transport_kernel(
    place_ref,
    x_ref,
    strip_ref,
    flow_ref,
    fstrip_ref,
    up_ref,
    down_ref,
    left_ref,
    right_ref,
    ul_ref,
    ur_ref,
    dl_ref,
    dr_ref,
    *refs,
):
    *outs, ext_ref, ax_ref, bx_ref, ay_ref, by_ref, first_ref, moved_ref, edge_ref, spread_ref, main_ref, shift_ref = refs
    count, rows = x_ref.shape[0], x_ref.shape[1] // SUB
    half = rows // 2
    place = place_ref[0]
    level = level_ids().astype(F32)
    flow = Flow(
        flow_ref, fstrip_ref, up_ref, down_ref, left_ref, right_ref, (ul_ref, ur_ref, dl_ref, dr_ref)
    )

    for r in range(-HALO, rows + HALO):
        at = pl.ds((r + HALO) * SUB, SUB)
        main_ref[at, :] = flow.row(0, r)
        left, right = flow.strips(r)
        edge_ref[0, at, :] = left
        edge_ref[1, at, :] = right
    shift_east = jnp.where(
        lax.broadcasted_iota(jnp.int32, (LANES, LANES), 0)
        == lax.broadcasted_iota(jnp.int32, (LANES, LANES), 1) + 1,
        1.0,
        0.0,
    )
    shift_ref[...] = exact_dot(main_ref[...], shift_east)
    moves = select_lanes(((0, 0), (0, 1), (1, 0), (2, 0), (2, 1)))
    for side in range(2):
        spread_ref[side] = exact_dot(edge_ref[side], moves)

    previous = None
    for r in range(-HALO, rows + HALO):
        at = pl.ds((r + HALO) * SUB, SUB)
        aux = flow.row(2, r)
        wide = lambda v, i: jnp.broadcast_to(v[i : i + 1, :], (SUB, LANES))
        kinds = [(main_ref[at, :], shift_ref[at, :], flow.row(1, r), wide(aux, 0), wide(aux, 2))]
        for side in range(2):
            east, east_next, north, tally, tally_next = (
                spread_ref[side, at, LANES * q : LANES * (q + 1)] for q in range(5)
            )
            tally, tally_next = wide(tally, 0), wide(tally_next, 0)
            kinds.append((east, east_next, north, tally, jnp.minimum(tally, tally_next)))
        for kind, (east, east_next, north, tally, pair) in enumerate(kinds):
            if -2 <= r < rows + 2:
                ax_ref[kind, r + 2], bx_ref[kind, r + 2] = face_pair(east, east_next, level < pair)
            if previous is not None and -3 <= r - 1 < rows + 2:
                below, depth = previous[kind]
                ay_ref[kind, r + 2], by_ref[kind, r + 2] = face_pair(
                    below, north, level < jnp.minimum(depth, tally)
                )
        previous = [(k[2], k[3]) for k in kinds]

    for t in range(count):
        for j in range(HALO):
            ext_ref[t, j] = up_ref[t * HALO + j]
            ext_ref[t, HALO + rows + j] = down_ref[t * HALO + j]
        for r in range(rows):
            ext_ref[t, HALO + r] = x_ref[t, pl.ds(r, SUB, stride=rows), :]
    for r in range(-HALO, rows + HALO):
        if r < 0 or r >= rows:
            src = up_ref if r < 0 else down_ref
            j = r + HALO if r < 0 else r - rows
            lref, rref = (ul_ref, ur_ref) if r < 0 else (dl_ref, dr_ref)
            own = strip_of([src[t * HALO + j] for t in range(count)])
            left, right = lref[j % 2], rref[j % 2]
            if j >= 2:
                left, right = roll(left, -8), roll(right, -8)
        else:
            own = strip_ref[r]
            left, right = left_ref[r % half], right_ref[r % half]
            if r >= half:
                left, right = roll(left, -8), roll(right, -8)
        ext_ref[count, HALO + r] = merge_left(own, left)
        ext_ref[count + 1, HALO + r] = merge_right(own, right)

    def one(p, carry):
        kind = jnp.maximum(p - (count - 1), 0)
        transport_rows(
            lambda i: ext_ref[p, HALO + i],
            lambda i, value: first_ref.__setitem__(i + 2, value),
            ax_ref, bx_ref, ay_ref, by_ref, kind, -2, rows + 2, 2, 3,
        )
        transport_rows(
            lambda i: first_ref[2 + i],
            lambda i, value: moved_ref.__setitem__((p, i), value),
            ax_ref, bx_ref, ay_ref, by_ref, kind, 0, rows, 2, 3,
        )
        return carry

    lax.fori_loop(0, count + 2, one, 0)

    lane = lane_ids()
    edge = (lane < 4) | (lane >= LANES - 4)
    from_right = (lane % GROUP >= 4) & (lane % GROUP < 8)
    share = rows // len(outs)
    for k, out_ref in enumerate(outs):
        base = (place ^ k) * share
        for r in range(share):
            joined = jnp.where(from_right, moved_ref[count + 1, base + r], moved_ref[count, base + r])
            for t in range(count):
                out_ref[t * share + r] = jnp.where(
                    edge, roll(joined, -(GROUP * t + 8)), moved_ref[t, base + r]
                )


def transport(place, shards, x, strip, flow_parts):
    count, rows = x.shape[0], x.shape[1] // SUB
    vmem = pl.BlockSpec(memory_space=pltpu.VMEM)
    tile = lambda *n: pltpu.VMEM(n + (SUB, LANES), F32)
    args = (x, strip) + flow_parts
    return pl.pallas_call(
        transport_kernel,
        in_specs=[pl.BlockSpec(memory_space=pltpu.SMEM)] + [vmem] * len(args),
        out_shape=tuple(
            jax.ShapeDtypeStruct((count * rows // shards, SUB, LANES), F32) for _ in range(shards)
        ),
        scratch_shapes=[
            tile(count + 2, rows + 2 * HALO),
            tile(3, rows + 4),
            tile(3, rows + 4),
            tile(3, rows + 5),
            tile(3, rows + 5),
            tile(rows + 4),
            tile(count + 2, rows),
            pltpu.VMEM((2, (rows + 2 * HALO) * SUB, LANES), F32),
            pltpu.VMEM((2, (rows + 2 * HALO) * SUB, 5 * LANES), F32),
            pltpu.VMEM(((rows + 2 * HALO) * SUB, LANES), F32),
            pltpu.VMEM(((rows + 2 * HALO) * SUB, LANES), F32),
        ],
        name="transport",
    )(place, *args)


def react_kernel(place_ref, table_ref, pace_ref, uptake_ref, surface_ref, tally_ref, *refs):
    shards = (len(refs) - 3) // 2
    ins, outs = refs[:shards], refs[shards : 2 * shards]
    light_ref, wet_ref, heat_ref = refs[2 * shards :]
    total = pace_ref.shape[0]
    count = total // shards
    share = ins[0].shape[0] // count
    place = place_ref[0]
    level = level_ids()

    for r in range(share):
        row = place * share + r
        tally = jnp.broadcast_to(tally_ref[pl.ds(row, 1), :], (SUB, LANES))
        surface = jnp.broadcast_to(surface_ref[pl.ds(row, 1), :], (SUB, LANES))
        wet = jnp.where(level < tally, 1.0, 0.0)
        absorbed = jnp.zeros((SUB, LANES), F32)
        for k, ref in enumerate(ins):
            for t in range(count):
                absorbed = absorbed + uptake_ref[(place ^ k) * count + t] * jnp.abs(ref[t * share + r])
        layer = (COLUMN_DEPTH / SUB) * (WATER_ABSORB + absorbed) * wet
        total_depth = jnp.where(level >= 1, pltpu.roll(layer, 1, 0), 0.0)
        for shift in (1, 2, 4):
            total_depth = total_depth + jnp.where(
                level >= shift, pltpu.roll(total_depth, shift, 0), 0.0
            )
        top = surface * jnp.exp(-total_depth)
        heat_ref[pl.ds(r * SUB, SUB), :] = top * (1.0 - jnp.exp(-layer))
        light_ref[r] = REACT_STEP * wet * (top / (top + HALF_LIGHT))
        wet_ref[r] = REACT_STEP * wet

    block = 4
    for k, out_ref in enumerate(outs):
        for m0 in range(0, count, block):
            dest = [(place ^ k) * count + m0 + j for j in range(block)]
            acc = [[None] * share for _ in range(block)]
            for kk, ref in enumerate(ins):
                for t in range(count):
                    n = (place ^ kk) * count + t
                    values = [ref[t * share + r] for r in range(share)]
                    for j in range(block):
                        c = table_ref[dest[j], n]
                        for r in range(share):
                            term = c * values[r]
                            acc[j][r] = term if acc[j][r] is None else acc[j][r] + term
            for j in range(block):
                pace = pace_ref[dest[j]]
                for r in range(share):
                    own = ins[k][(m0 + j) * share + r]
                    out_ref[(m0 + j) * share + r] = (
                        own + wet_ref[r] * acc[j][r] + pace * (light_ref[r] * own)
                    )
        own_levels = SUB // shards
        for q in range(own_levels):
            start = (place ^ k) * own_levels + q
            out_ref[count * share + q] = heat_ref[pl.ds(start, share, stride=SUB), :]


def react(place, table, pace, uptake, surface, tally, blocks):
    shards = len(blocks)
    share = blocks[0].shape[0] // (pace.shape[0] // shards)
    smem = pl.BlockSpec(memory_space=pltpu.SMEM)
    vmem = pl.BlockSpec(memory_space=pltpu.VMEM)
    return pl.pallas_call(
        react_kernel,
        in_specs=[smem] * 4 + [vmem] * (2 + shards),
        out_shape=tuple(
            jax.ShapeDtypeStruct((b.shape[0] + SUB // shards, SUB, LANES), F32) for b in blocks
        ),
        scratch_shapes=[
            pltpu.VMEM((share, SUB, LANES), F32),
            pltpu.VMEM((share, SUB, LANES), F32),
            pltpu.VMEM((share * SUB, LANES), F32),
        ],
        name="react",
    )(place, table, pace, uptake, surface, tally, *blocks)


def finish_kernel(place_ref, thermal_ref, *refs):
    *ins, out_ref, temp_ref = refs
    shards = len(ins)
    count = out_ref.shape[0]
    rows = out_ref.shape[1] // SUB
    share = rows // shards
    place = place_ref[0]
    own_levels = SUB // shards
    for k, ref in enumerate(ins):
        base = (place ^ k) * share
        for m in range(count):
            for lev in range(SUB):
                dst = pl.multiple_of(lev * rows + base, SUB)
                out_ref[m, pl.ds(dst, share), :] = ref[pl.ds(m * share * SUB + lev, share, stride=SUB), :]
        for q in range(own_levels):
            dst = pl.multiple_of(q * rows + base, SUB)
            heat = ref[pl.ds((count * share + q) * SUB, share), :]
            temp_ref[pl.ds(dst, share), :] = thermal_ref[pl.ds(dst, share), :] + WARMING_WEIGHT * heat


def finish(place, thermal, blocks, count, rows):
    vmem = pl.BlockSpec(memory_space=pltpu.VMEM)
    flat = [b.reshape(-1, LANES) for b in blocks]
    return pl.pallas_call(
        finish_kernel,
        in_specs=[pl.BlockSpec(memory_space=pltpu.SMEM)] + [vmem] * (1 + len(flat)),
        out_shape=(
            jax.ShapeDtypeStruct((count, SUB * rows, LANES), F32),
            jax.ShapeDtypeStruct(thermal.shape, F32),
        ),
        name="finish",
    )(place, thermal, *flat)


def level_sum(x):
    for shift in (4, 2, 1):
        x = x + pltpu.roll(x, shift, 0)
    return x


def momentum_kernel(
    place_ref,
    coriolis_ref,
    inside_ref,
    flow_ref,
    strip_ref,
    fup_ref,
    fdown_ref,
    colsl_ref,
    colsr_ref,
    ul_ref,
    ur_ref,
    dl_ref,
    dr_ref,
    east_ref,
    north_ref,
    height_ref,
    a_ref,
    b_ref,
    c_ref,
):
    rows = height_ref.shape[0]
    own_levels = east_ref.shape[0] // rows
    place = place_ref[0]
    lane = lane_ids()
    level = level_ids().astype(F32)
    flow = Flow(
        flow_ref, strip_ref, fup_ref, fdown_ref, colsl_ref, colsr_ref, (ul_ref, ur_ref, dl_ref, dr_ref)
    )
    for r in range(-2, rows + 2):
        east, north, aux = (flow.row(f, r) for f in range(3))
        left, right = flow.strips(r)
        both = [
            jnp.where(lane < GROUP, roll(left, -GROUP * f), roll(right, GROUP - GROUP * f))
            for f in range(3)
        ]
        for p, (u, v, w) in enumerate(((east, north, aux), both)):
            wet = jnp.where(level < over_levels(w), 1.0, 0.0)
            h = jnp.broadcast_to(w[1:2, :], (SUB, LANES))
            for f, value in enumerate((u, v, h, wet)):
                a_ref[p, f, r + 2] = value

    def substep(src, offset, put, first, last):
        for p in range(2):
            for i in range(first, last):
                g = lambda f, d: src[p, f, i + offset + d]
                u, v, h = g(0, 0), g(1, 0), g(2, 0)
                un, us, vn, vs, hn, hs = g(0, 1), g(0, -1), g(1, 1), g(1, -1), g(2, 1), g(2, -1)
                wet = a_ref[p, 3, i + 2]
                cor = jnp.broadcast_to(coriolis_ref[i + 2 : i + 3, :], (SUB, LANES))
                ue, uw, ve, vw, he, hw = (
                    roll(u, -1), roll(u, 1), roll(v, -1), roll(v, 1), roll(h, -1), roll(h, 1),
                )
                div = level_sum(0.5 * (ue - uw) + 0.5 * (vn - vs))
                nu = wet * (
                    u
                    + TIME_STEP
                    * (
                        cor * v
                        - GRAVITY * (0.5 * (he - hw))
                        + VISCOSITY * (un + us + ue + uw - 4.0 * u)
                        - BOTTOM_DRAG * u
                    )
                )
                nv = wet * (
                    v
                    + TIME_STEP
                    * (
                        -cor * u
                        - GRAVITY * (0.5 * (hn - hs))
                        + VISCOSITY * (vn + vs + ve + vw - 4.0 * v)
                        - BOTTOM_DRAG * v
                    )
                )
                nh = h - TIME_STEP * DEPTH_SCALE * div
                put(p, i, nu, nv, nh)

    def put_first(p, i, nu, nv, nh):
        inside = jnp.broadcast_to(inside_ref[i + 2 : i + 3, :], (SUB, LANES))
        for f, value in enumerate((nu, nv, nh * inside)):
            b_ref[p, f, i + 1] = value

    def put_second(p, i, nu, nv, nh):
        for f, value in enumerate((nu, nv, nh)):
            c_ref[p, f, pl.ds(i * SUB, SUB), :] = value

    substep(a_ref, 2, put_first, -1, rows + 1)
    substep(b_ref, 1, put_second, 0, rows)

    def joined(f, start):
        lane8 = lax.broadcasted_iota(jnp.int32, (SUB, LANES), 1)
        main = c_ref[0, f, pl.ds(start, SUB, stride=SUB), :]
        edge = c_ref[1, f, pl.ds(start, SUB, stride=SUB), :]
        out = jnp.where(lane8 < 2, roll(edge, -8), main)
        return jnp.where(lane8 >= LANES - 2, roll(edge, LANES - 2 - (GROUP + 6)), out)

    for j in range(rows // SUB):
        for q in range(own_levels):
            lev = place * own_levels + q
            dst = q * rows + j * SUB
            east_ref[dst : dst + SUB, :] = joined(0, j * SUB * SUB + lev)
            north_ref[dst : dst + SUB, :] = joined(1, j * SUB * SUB + lev)
        height_ref[j * SUB : (j + 1) * SUB, :] = joined(2, j * SUB * SUB)


def momentum(place, coriolis, inside, flow_parts, rows, own_levels):
    vmem = pl.BlockSpec(memory_space=pltpu.VMEM)
    args = (coriolis, inside) + flow_parts
    return pl.pallas_call(
        momentum_kernel,
        in_specs=[pl.BlockSpec(memory_space=pltpu.SMEM)] + [vmem] * len(args),
        out_shape=(
            jax.ShapeDtypeStruct((own_levels * rows, LANES), F32),
            jax.ShapeDtypeStruct((own_levels * rows, LANES), F32),
            jax.ShapeDtypeStruct((rows, LANES), F32),
        ),
        scratch_shapes=[
            pltpu.VMEM((2, 4, rows + 4, SUB, LANES), F32),
            pltpu.VMEM((2, 3, rows + 2, SUB, LANES), F32),
            pltpu.VMEM((2, 3, rows * SUB, LANES), F32),
        ],
        name="momentum",
    )(place, *args)


def to_peer(block, k):
    count = lax.axis_size("trc")
    return lax.ppermute(block, "trc", [(i, i ^ k) for i in range(count)])


def shifted(block, dlat, dlon):
    nlat, nlon = lax.axis_size("lat"), lax.axis_size("lon")
    pairs = [
        (i * nlon + j, (i + dlat) * nlon + (j + dlon) % nlon)
        for i in range(nlat)
        for j in range(nlon)
        if 0 <= i + dlat < nlat
    ]
    return lax.ppermute(block, ("lat", "lon"), pairs)


def both_sides(block, dlat):
    left = shifted(block, dlat, 1)
    if lax.axis_size("lon") == 2:
        return left, left
    return left, shifted(block, dlat, -1)


def body(
    species_concentrations,
    zonal_velocity_array,
    meridional_velocity_array,
    thermal_anomaly,
    ocean_top_height_grid,
    water_layer_tally,
    species_interaction_table,
    species_production_pace,
    photon_uptake,
):
    count, levels, rows, cols = species_concentrations.shape
    own_levels = zonal_velocity_array.shape[0]
    shards = lax.axis_size("trc")
    assert levels == SUB and cols == LANES and count * GROUP == LANES and shards & (shards - 1) == 0
    trc_place = lax.axis_index("trc")
    place = trc_place.astype(jnp.int32).reshape(1)
    lat_total = rows * lax.axis_size("lat")
    lat_first = lax.axis_index("lat") * rows
    lat_global = (lat_first + jnp.arange(-2, rows + 2)).astype(F32)
    angle = math.pi * ((lat_global + 0.5) / lat_total - 0.5)
    spread = lambda v: jnp.broadcast_to(v[:, None], (v.shape[0], LANES))
    coriolis = spread(CORIOLIS_SCALE * jnp.sin(angle))
    surface = spread(1.0 + jnp.cos(angle[2:-2]))
    inside = spread(((lat_global >= 0) & (lat_global < lat_total)).astype(F32))

    x = species_concentrations.reshape(count, levels * rows, cols)
    own = jnp.stack([zonal_velocity_array, meridional_velocity_array]).reshape(
        2, own_levels * rows, cols
    )
    peers = [to_peer(own, k) for k in range(1, shards)]
    strip, *messages = pack_tracers(x)
    flow, fstrip, fcols, fup, fdown, dup, ddown = pack_flow(
        place, own, peers, water_layer_tally, ocean_top_height_grid, messages
    )
    up_in, down_in = shifted(fup, 1, 0), shifted(fdown, -1, 0)
    left_in, right_in = both_sides(fcols, 0)
    ul, ur = both_sides(dup, 1)
    dl, dr = both_sides(ddown, -1)
    flow_parts = (flow, fstrip, up_in, down_in, left_in, right_in, ul, ur, dl, dr)
    moved = transport(place, shards, x, strip, flow_parts)
    blocks = [moved[0]] + [to_peer(moved[k], k) for k in range(1, shards)]
    east_out, north_out, height_out = momentum(
        place, coriolis, inside, flow_parts, rows, own_levels
    )
    reacted = react(
        place,
        species_interaction_table,
        species_production_pace,
        photon_uptake,
        surface,
        water_layer_tally,
        blocks,
    )
    back = [reacted[0]] + [to_peer(reacted[k], k) for k in range(1, shards)]
    updated, temperature = finish(
        place, thermal_anomaly.reshape(own_levels * rows, cols), back, count, rows
    )
    vel = (own_levels, rows, cols)
    return (
        updated.reshape(count, levels, rows, cols),
        east_out.reshape(vel),
        north_out.reshape(vel),
        temperature.reshape(vel),
        height_out,
    )


def solution(mesh):
    return jax.shard_map(
        body,
        mesh=mesh,
        in_specs=(
            P("trc", None, "lat", "lon"),
            P("trc", "lat", "lon"),
            P("trc", "lat", "lon"),
            P("trc", "lat", "lon"),
            P("lat", "lon"),
            P("lat", "lon"),
            P(),
            P(),
            P(),
        ),
        out_specs=(
            P("trc", None, "lat", "lon"),
            P("trc", "lat", "lon"),
            P("trc", "lat", "lon"),
            P("trc", "lat", "lon"),
            P("lat", "lon"),
        ),
        check_vma=False,
    )
```

```python
import functools
import math

import jax
import jax.numpy as jnp
from jax import lax
from jax.experimental import pallas as pl
from jax.experimental.pallas import tpu as pltpu
from jax.sharding import PartitionSpec as P

TIME_STEP = 0.1
GRAVITY = 1.0
VISCOSITY = 0.2
BOTTOM_DRAG = 0.05
DEPTH_SCALE = 0.5
CORIOLIS_SCALE = 0.5
COLUMN_DEPTH = 2.0
WATER_ABSORB = 0.2
HALF_LIGHT = 0.5
REACT_STEP = 0.1
WARMING_WEIGHT = 1.0

SUB = 8
LANES = 128
HALO = 4
GROUP = 16
F32 = jnp.float32
PARTS = 2


def lane_ids():
    return lax.broadcasted_iota(jnp.int32, (SUB, LANES), 1)


def level_ids():
    return lax.broadcasted_iota(jnp.int32, (SUB, LANES), 0)


def roll(x, shift):
    shift = shift % LANES
    return x if shift == 0 else pltpu.roll(x, shift, 1)


def strip_of(rows):
    lane = lane_ids()
    out = None
    for t, value in enumerate(rows):
        rolled = roll(value, GROUP * t + GROUP // 2)
        if out is None:
            out = rolled
        else:
            out = jnp.where(lane // GROUP == t, rolled, out)
    return out


def middle_mask():
    lane = lane_ids() % GROUP
    return (lane >= 4) & (lane < 12)


def pair_up(first, second):
    return jnp.where(middle_mask(), first, roll(second, 8))


def quad_up(a, b, c, d):
    return jnp.where(lane_ids() < 64, pair_up(a, b), roll(pair_up(c, d), 64))


def merge_left(own, got):
    lane = lane_ids() % GROUP
    return jnp.where((lane >= 4) & (lane < 8), got, own)


def merge_right(own, got):
    lane = lane_ids() % GROUP
    return jnp.where((lane >= 8) & (lane < 12), got, own)


def replicate(strip, group):
    out = jnp.where(lane_ids() // GROUP == group, strip, 0.0)
    for shift in (16, 32, 64):
        out = out + roll(out, shift)
    return out


def over_levels(row):
    return jnp.broadcast_to(row[0:1, :], (SUB, LANES))


def pack_tracers_kernel(x_ref, strip_ref, up_ref, down_ref, cols_ref, cup_ref, cdown_ref):
    count, rows = x_ref.shape[0], x_ref.shape[1] // SUB
    half = rows // 2

    def row_strip(r):
        return strip_of([x_ref[t, pl.ds(r, SUB, stride=rows), :] for t in range(count)])

    for r in range(half):
        low, high = row_strip(r), row_strip(r + half)
        strip_ref[r] = low
        strip_ref[r + half] = high
        cols_ref[r] = pair_up(low, high)
    for j in range(2):
        cdown_ref[j] = pair_up(strip_ref[j], strip_ref[j + 2])
        cup_ref[j] = pair_up(strip_ref[rows - HALO + j], strip_ref[rows - HALO + j + 2])
    for t in range(count):
        for j in range(HALO):
            down_ref[t * HALO + j] = x_ref[t, pl.ds(j, SUB, stride=rows), :]
            up_ref[t * HALO + j] = x_ref[t, pl.ds(rows - HALO + j, SUB, stride=rows), :]


def pack_tracers(x):
    count, rows = x.shape[0], x.shape[1] // SUB
    tile = lambda n: jax.ShapeDtypeStruct((n, SUB, LANES), F32)
    return pl.pallas_call(
        pack_tracers_kernel,
        out_shape=(
            tile(rows),
            tile(count * HALO),
            tile(count * HALO),
            tile(rows // 2),
            tile(2),
            tile(2),
        ),
        name="pack_tracers",
    )(x)


def pack_flow_kernel(place_ref, own_ref, *refs):
    peers, rest = refs[:-15], refs[-15:]
    tally_ref, height_ref, tup_ref, tdown_ref, tcols_ref, cup_ref, cdown_ref = rest[:7]
    flow_ref, strip_ref, cols_ref, up_ref, down_ref, dup_ref, ddown_ref, all_ref = rest[7:]
    rows = tally_ref.shape[0]
    span = own_ref.shape[1]
    place = place_ref[0]
    for k, ref in enumerate((own_ref,) + tuple(peers)):
        base = pl.multiple_of((place ^ k) * span, SUB)
        for f in range(2):
            all_ref[f, pl.ds(base, span), :] = ref[f]
    for src, dst in ((tup_ref, up_ref), (tdown_ref, down_ref), (tcols_ref, cols_ref), (cup_ref, dup_ref), (cdown_ref, ddown_ref)):
        dst[0 : src.shape[0]] = src[...]
    nrow, ncol, ncorner = tup_ref.shape[0], tcols_ref.shape[0], cup_ref.shape[0]
    level = level_ids()
    tally_all = tally_ref[...].astype(F32)
    pair_all = jnp.minimum(tally_all, pltpu.roll(tally_all, LANES - 1, 1))
    wide = lambda v, r: jnp.broadcast_to(v[r : r + 1, :], (SUB, LANES))
    for r in range(rows):
        tally, height, pair = wide(tally_all, r), wide(height_ref, r), wide(pair_all, r)
        wet = level.astype(F32) < tally
        east = jnp.where(wet, all_ref[0, pl.ds(r, SUB, stride=rows), :], 0.0)
        north = jnp.where(wet, all_ref[1, pl.ds(r, SUB, stride=rows), :], 0.0)
        aux = jnp.where(level == 0, tally, jnp.where(level == 1, height, pair))
        for f, value in enumerate((east, north, aux)):
            flow_ref[f * rows + r] = value
            if r < HALO:
                down_ref[nrow + f * HALO + r] = value
            if r >= rows - HALO:
                up_ref[nrow + f * HALO + r - (rows - HALO)] = value
        strip_ref[r] = strip_of([east, north, aux])
    quarter = rows // 4
    for r in range(quarter):
        cols_ref[ncol + r] = quad_up(*[strip_ref[r + quarter * q] for q in range(4)])
    dup_ref[ncorner] = quad_up(*[strip_ref[rows - HALO + j] for j in range(HALO)])
    ddown_ref[ncorner] = quad_up(*[strip_ref[j] for j in range(HALO)])


def pack_flow(place, own, peers, tally, height, messages):
    rows = tally.shape[0]
    tile = lambda n: jax.ShapeDtypeStruct((n, SUB, LANES), F32)
    vmem = pl.BlockSpec(memory_space=pltpu.VMEM)
    tup, tdown, tcols, cup, cdown = messages
    return pl.pallas_call(
        pack_flow_kernel,
        in_specs=[pl.BlockSpec(memory_space=pltpu.SMEM)] + [vmem] * (3 + len(peers) + len(messages)),
        out_shape=(
            tile(3 * rows),
            tile(rows),
            tile(tcols.shape[0] + rows // 4),
            tile(tup.shape[0] + 3 * HALO),
            tile(tdown.shape[0] + 3 * HALO),
            tile(cup.shape[0] + 1),
            tile(cdown.shape[0] + 1),
        ),
        scratch_shapes=[pltpu.VMEM((2, SUB * rows, LANES), F32)],
        name="pack_flow",
    )(place, own, *peers, tally, height, *messages)


class Flow:
    def __init__(self, flow_ref, strip_ref, up_ref, down_ref, left_ref, right_ref, corners):
        self.flow, self.strip, self.up, self.down = flow_ref, strip_ref, up_ref, down_ref
        self.left, self.right, self.corners = left_ref, right_ref, corners
        self.rows = strip_ref.shape[0]
        self.row_base = up_ref.shape[0] - 3 * HALO
        self.col_base = left_ref.shape[0] - self.rows // 4
        self.corner_base = corners[0].shape[0] - 1

    def row(self, f, r):
        if r < 0:
            return self.up[self.row_base + f * HALO + HALO + r]
        if r >= self.rows:
            return self.down[self.row_base + f * HALO + r - self.rows]
        return self.flow[f * self.rows + r]

    def strips(self, r):
        if 0 <= r < self.rows:
            quarter = self.rows // 4
            q, j = divmod(r, quarter)
            own = self.strip[r]
            left, right = self.left[self.col_base + j], self.right[self.col_base + j]
        else:
            own = strip_of([self.row(f, r) for f in range(3)])
            q = r + HALO if r < 0 else r - self.rows
            lref, rref = self.corners[:2] if r < 0 else self.corners[2:]
            left, right = lref[self.corner_base], rref[self.corner_base]
        shift = -(8 * (q % 2) + 64 * (q // 2))
        return merge_left(own, roll(left, shift)), merge_right(own, roll(right, shift))


def limited(ahead, behind):
    return jnp.maximum(
        jnp.minimum(ahead, jnp.maximum(behind, 0.0)), jnp.minimum(behind, 0.0)
    )


def face_pair(vel, vel_next, wet):
    a = jnp.where(wet, 0.5 * (vel + vel_next), 0.0)
    size = jnp.abs(a)
    return a, 0.5 * size * (1.0 - size)


def transport_rows(load, store, ax_ref, bx_ref, ay_ref, by_ref, kind, first, last, xo, yo):
    before, here, after = load(first - 2), load(first - 1), load(first)
    slope_y = limited(after - here, here - before)
    diff = after - here
    flux_below = None
    row, nxt = here, after
    for i in range(first - 1, last):
        far = load(i + 2)
        diff_next = far - nxt
        slope_next = limited(diff_next, diff)
        ay, by = ay_ref[kind, yo + i], by_ref[kind, yo + i]
        positive = ay >= 0.0
        flux = ay * jnp.where(positive, row, nxt) + by * jnp.where(positive, slope_y, slope_next)
        if flux_below is not None:
            ax, bx = ax_ref[kind, xo + i], bx_ref[kind, xo + i]
            east = roll(row, -1)
            dx = east - row
            sx = limited(dx, roll(dx, 1))
            sx_east = roll(sx, -1)
            pos = ax >= 0.0
            fx = ax * jnp.where(pos, row, east) + bx * jnp.where(pos, sx, sx_east)
            store(i, row - (fx - roll(fx, 1)) - (flux - flux_below))
        flux_below = flux
        row, nxt, slope_y, diff = nxt, far, slope_next, diff_next


def select_lanes(moves):
    parts = []
    source = lax.broadcasted_iota(jnp.int32, (LANES, LANES), 0)
    target = lax.broadcasted_iota(jnp.int32, (LANES, LANES), 1)
    for f, d in moves:
        parts.append(jnp.where(source == GROUP * f + target % GROUP + d, 1.0, 0.0))
    return jnp.concatenate(parts, axis=1)


def exact_dot(a, b):
    return jnp.dot(a, b, precision=lax.Precision.HIGHEST, preferred_element_type=F32)


def transport_kernel(
    place_ref,
    x_ref,
    strip_ref,
    flow_ref,
    fstrip_ref,
    up_ref,
    down_ref,
    left_ref,
    right_ref,
    ul_ref,
    ur_ref,
    dl_ref,
    dr_ref,
    *refs,
    first_row,
):
    *outs, ext_ref, ax_ref, bx_ref, ay_ref, by_ref, first_ref, moved_ref, edge_ref, spread_ref, main_ref, shift_ref = refs
    count, rows = x_ref.shape[0], x_ref.shape[1] // SUB
    half = rows // 2
    span = moved_ref.shape[1]
    place = place_ref[0]
    level = level_ids().astype(F32)
    flow = Flow(
        flow_ref, fstrip_ref, up_ref, down_ref, left_ref, right_ref, (ul_ref, ur_ref, dl_ref, dr_ref)
    )

    for q in range(-HALO, span + HALO):
        at = pl.ds((q + HALO) * SUB, SUB)
        main_ref[at, :] = flow.row(0, first_row + q)
        left, right = flow.strips(first_row + q)
        edge_ref[0, at, :] = left
        edge_ref[1, at, :] = right
    shift_east = jnp.where(
        lax.broadcasted_iota(jnp.int32, (LANES, LANES), 0)
        == lax.broadcasted_iota(jnp.int32, (LANES, LANES), 1) + 1,
        1.0,
        0.0,
    )
    shift_ref[...] = exact_dot(main_ref[...], shift_east)
    moves = select_lanes(((0, 0), (0, 1), (1, 0), (2, 0), (2, 1)))
    for side in range(2):
        spread_ref[side] = exact_dot(edge_ref[side], moves)

    previous = None
    for q in range(-HALO, span + HALO):
        at = pl.ds((q + HALO) * SUB, SUB)
        aux = flow.row(2, first_row + q)
        wide = lambda v, i: jnp.broadcast_to(v[i : i + 1, :], (SUB, LANES))
        kinds = [(main_ref[at, :], shift_ref[at, :], flow.row(1, first_row + q), wide(aux, 0), wide(aux, 2))]
        for side in range(2):
            east, east_next, north, tally, tally_next = (
                spread_ref[side, at, LANES * n : LANES * (n + 1)] for n in range(5)
            )
            tally, tally_next = wide(tally, 0), wide(tally_next, 0)
            kinds.append((east, east_next, north, tally, jnp.minimum(tally, tally_next)))
        for kind, (east, east_next, north, tally, pair) in enumerate(kinds):
            if -2 <= q < span + 2:
                ax_ref[kind, q + 2], bx_ref[kind, q + 2] = face_pair(east, east_next, level < pair)
            if previous is not None and -3 <= q - 1 < span + 2:
                below, depth = previous[kind]
                ay_ref[kind, q + 2], by_ref[kind, q + 2] = face_pair(
                    below, north, level < jnp.minimum(depth, tally)
                )
        previous = [(k[2], k[3]) for k in kinds]

    for q in range(-HALO, span + HALO):
        r = first_row + q
        if r < 0 or r >= rows:
            src = up_ref if r < 0 else down_ref
            j = r + HALO if r < 0 else r - rows
            fields = [src[t * HALO + j] for t in range(count)]
            lref, rref = (ul_ref, ur_ref) if r < 0 else (dl_ref, dr_ref)
            own = strip_of(fields)
            left, right = lref[j % 2], rref[j % 2]
            swap = j >= 2
        else:
            fields = [x_ref[t, pl.ds(r, SUB, stride=rows), :] for t in range(count)]
            own = strip_ref[r]
            left, right = left_ref[r % half], right_ref[r % half]
            swap = r >= half
        if swap:
            left, right = roll(left, -8), roll(right, -8)
        fields += [merge_left(own, left), merge_right(own, right)]
        for t, value in enumerate(fields):
            ext_ref[t, HALO + q] = value

    def one(p, carry):
        kind = jnp.maximum(p - (count - 1), 0)
        transport_rows(
            lambda i: ext_ref[p, HALO + i],
            lambda i, value: first_ref.__setitem__(i + 2, value),
            ax_ref, bx_ref, ay_ref, by_ref, kind, -2, span + 2, 2, 3,
        )
        transport_rows(
            lambda i: first_ref[2 + i],
            lambda i, value: moved_ref.__setitem__((p, i), value),
            ax_ref, bx_ref, ay_ref, by_ref, kind, 0, span, 2, 3,
        )
        return carry

    lax.fori_loop(0, count + 2, one, 0)

    lane = lane_ids()
    edge = (lane < 4) | (lane >= LANES - 4)
    from_right = (lane % GROUP >= 4) & (lane % GROUP < 8)
    share = span // len(outs)
    for k, out_ref in enumerate(outs):
        base = (place ^ k) * share
        for r in range(share):
            joined = jnp.where(from_right, moved_ref[count + 1, base + r], moved_ref[count, base + r])
            for t in range(count):
                out_ref[t * share + r] = jnp.where(
                    edge, roll(joined, -(GROUP * t + 8)), moved_ref[t, base + r]
                )


def transport(place, shards, x, strip, flow_parts, first_row, span):
    count = x.shape[0]
    vmem = pl.BlockSpec(memory_space=pltpu.VMEM)
    tile = lambda *n: pltpu.VMEM(n + (SUB, LANES), F32)
    flat = lambda *n: pltpu.VMEM(n, F32)
    args = (x, strip) + flow_parts
    wide = (span + 2 * HALO) * SUB
    return pl.pallas_call(
        functools.partial(transport_kernel, first_row=first_row),
        in_specs=[pl.BlockSpec(memory_space=pltpu.SMEM)] + [vmem] * len(args),
        out_shape=tuple(
            jax.ShapeDtypeStruct((count * span // shards, SUB, LANES), F32) for _ in range(shards)
        ),
        scratch_shapes=[
            tile(count + 2, span + 2 * HALO),
            tile(3, span + 4),
            tile(3, span + 4),
            tile(3, span + 5),
            tile(3, span + 5),
            tile(span + 4),
            tile(count + 2, span),
            flat(2, wide, LANES),
            flat(2, wide, 5 * LANES),
            flat(wide, LANES),
            flat(wide, LANES),
        ],
        name="transport",
    )(place, *args)


def react_kernel(place_ref, table_ref, pace_ref, uptake_ref, surface_ref, tally_ref, *refs, first_row):
    shards = (len(refs) - 3) // 2
    ins, outs = refs[:shards], refs[shards : 2 * shards]
    light_ref, wet_ref, heat_ref = refs[2 * shards :]
    total = pace_ref.shape[0]
    count = total // shards
    share = ins[0].shape[0] // count
    place = place_ref[0]
    level = level_ids()

    for r in range(share):
        row = first_row + place * share + r
        tally = jnp.broadcast_to(tally_ref[pl.ds(row, 1), :], (SUB, LANES))
        surface = jnp.broadcast_to(surface_ref[pl.ds(row, 1), :], (SUB, LANES))
        wet = jnp.where(level < tally, 1.0, 0.0)
        absorbed = jnp.zeros((SUB, LANES), F32)
        for k, ref in enumerate(ins):
            for t in range(count):
                absorbed = absorbed + uptake_ref[(place ^ k) * count + t] * jnp.abs(ref[t * share + r])
        layer = (COLUMN_DEPTH / SUB) * (WATER_ABSORB + absorbed) * wet
        total_depth = jnp.where(level >= 1, pltpu.roll(layer, 1, 0), 0.0)
        for shift in (1, 2, 4):
            total_depth = total_depth + jnp.where(
                level >= shift, pltpu.roll(total_depth, shift, 0), 0.0
            )
        top = surface * jnp.exp(-total_depth)
        heat_ref[pl.ds(r * SUB, SUB), :] = top * (1.0 - jnp.exp(-layer))
        light_ref[r] = REACT_STEP * wet * (top / (top + HALF_LIGHT))
        wet_ref[r] = REACT_STEP * wet

    block = 4
    for k, out_ref in enumerate(outs):
        for m0 in range(0, count, block):
            dest = [(place ^ k) * count + m0 + j for j in range(block)]
            acc = [[None] * share for _ in range(block)]
            for kk, ref in enumerate(ins):
                for t in range(count):
                    n = (place ^ kk) * count + t
                    values = [ref[t * share + r] for r in range(share)]
                    for j in range(block):
                        c = table_ref[dest[j], n]
                        for r in range(share):
                            term = c * values[r]
                            acc[j][r] = term if acc[j][r] is None else acc[j][r] + term
            for j in range(block):
                pace = pace_ref[dest[j]]
                for r in range(share):
                    own = ins[k][(m0 + j) * share + r]
                    out_ref[(m0 + j) * share + r] = (
                        own + wet_ref[r] * acc[j][r] + pace * (light_ref[r] * own)
                    )
        own_levels = SUB // shards
        out_ref[count * share] = jnp.concatenate(
            [
                heat_ref[pl.ds((place ^ k) * own_levels + q, share, stride=SUB), :]
                for q in range(own_levels)
            ],
            axis=0,
        )


def react(place, table, pace, uptake, surface, tally, blocks, first_row):
    shards = len(blocks)
    share = blocks[0].shape[0] // (pace.shape[0] // shards)
    smem = pl.BlockSpec(memory_space=pltpu.SMEM)
    vmem = pl.BlockSpec(memory_space=pltpu.VMEM)
    assert share * (SUB // shards) == SUB
    return pl.pallas_call(
        functools.partial(react_kernel, first_row=first_row),
        in_specs=[smem] * 4 + [vmem] * (2 + shards),
        out_shape=tuple(
            jax.ShapeDtypeStruct((b.shape[0] + 1, SUB, LANES), F32) for b in blocks
        ),
        scratch_shapes=[
            pltpu.VMEM((share, SUB, LANES), F32),
            pltpu.VMEM((share, SUB, LANES), F32),
            pltpu.VMEM((share * SUB, LANES), F32),
        ],
        name="react",
    )(place, table, pace, uptake, surface, tally, *blocks)


def finish_kernel(place_ref, thermal_ref, *refs, shards):
    ins, (out_ref, temp_ref, cells_ref, heat_ref) = refs[:shards], refs[-4:]
    count, _, span, _ = out_ref.shape
    share = span // shards
    place = place_ref[0]
    own_levels = SUB // shards
    level = level_ids()
    for k, ref in enumerate(ins):
        base = (place ^ k) * share
        for m in range(count):
            for r in range(share):
                at = pl.multiple_of((m * span + base + r) * SUB, SUB)
                cells_ref[pl.ds(at, SUB), :] = ref[m * share + r]
        heat = ref[count * share]
        for q in range(own_levels):
            heat_ref[q, place ^ k] = heat if q == 0 else pltpu.roll(heat, SUB - q * share, 0)
    per_tile = SUB // share
    for b in range(span // SUB):
        for m in range(count):
            for lev in range(SUB):
                start = (m * span + b * SUB) * SUB + lev
                out_ref[m, lev, b * SUB : (b + 1) * SUB, :] = cells_ref[pl.ds(start, SUB, stride=SUB), :]
        for q in range(own_levels):
            heat = heat_ref[q, b * per_tile]
            for n in range(1, per_tile):
                part = pltpu.roll(heat_ref[q, b * per_tile + n], n * share, 0)
                heat = jnp.where(level // share == n, part, heat)
            at = slice(b * SUB, (b + 1) * SUB)
            temp_ref[q, at, :] = thermal_ref[q, at, :] + WARMING_WEIGHT * heat


def finish(place, thermal, blocks, shape, part, parts, before):
    shards = len(blocks)
    count, levels, rows, cols = shape
    own_levels = thermal.shape[0]
    span = rows // parts
    vmem = pl.BlockSpec(memory_space=pltpu.VMEM)
    hold = pl.BlockSpec(memory_space=pl.ANY)
    of_part = lambda *lead: pl.BlockSpec(
        lead + (span, cols), lambda i: (0,) * len(lead) + (part, 0)
    )
    return pl.pallas_call(
        functools.partial(finish_kernel, shards=shards),
        grid=(1,),
        in_specs=[pl.BlockSpec(memory_space=pltpu.SMEM), of_part(own_levels)]
        + [vmem] * shards
        + [hold] * len(before),
        out_specs=(of_part(count, levels), of_part(own_levels)),
        out_shape=(jax.ShapeDtypeStruct(shape, F32), jax.ShapeDtypeStruct(thermal.shape, F32)),
        input_output_aliases={2 + shards + i: i for i in range(len(before))},
        scratch_shapes=[
            pltpu.VMEM((count * span * SUB, LANES), F32),
            pltpu.VMEM((own_levels, shards, SUB, LANES), F32),
        ],
        name="finish",
    )(place, thermal, *blocks, *before)


def level_sum(x):
    for shift in (4, 2, 1):
        x = x + pltpu.roll(x, shift, 0)
    return x


def momentum_kernel(
    place_ref,
    coriolis_ref,
    inside_ref,
    flow_ref,
    strip_ref,
    fup_ref,
    fdown_ref,
    colsl_ref,
    colsr_ref,
    ul_ref,
    ur_ref,
    dl_ref,
    dr_ref,
    east_ref,
    north_ref,
    height_ref,
    a_ref,
    b_ref,
    c_ref,
):
    rows = height_ref.shape[0]
    own_levels = east_ref.shape[0] // rows
    place = place_ref[0]
    lane = lane_ids()
    level = level_ids().astype(F32)
    flow = Flow(
        flow_ref, strip_ref, fup_ref, fdown_ref, colsl_ref, colsr_ref, (ul_ref, ur_ref, dl_ref, dr_ref)
    )
    for r in range(-2, rows + 2):
        east, north, aux = (flow.row(f, r) for f in range(3))
        left, right = flow.strips(r)
        both = [
            jnp.where(lane < GROUP, roll(left, -GROUP * f), roll(right, GROUP - GROUP * f))
            for f in range(3)
        ]
        for p, (u, v, w) in enumerate(((east, north, aux), both)):
            wet = jnp.where(level < over_levels(w), 1.0, 0.0)
            h = jnp.broadcast_to(w[1:2, :], (SUB, LANES))
            for f, value in enumerate((u, v, h, wet)):
                a_ref[p, f, r + 2] = value

    def substep(src, offset, put, first, last):
        for p in range(2):
            for i in range(first, last):
                g = lambda f, d: src[p, f, i + offset + d]
                u, v, h = g(0, 0), g(1, 0), g(2, 0)
                un, us, vn, vs, hn, hs = g(0, 1), g(0, -1), g(1, 1), g(1, -1), g(2, 1), g(2, -1)
                wet = a_ref[p, 3, i + 2]
                cor = jnp.broadcast_to(coriolis_ref[i + 2 : i + 3, :], (SUB, LANES))
                ue, uw, ve, vw, he, hw = (
                    roll(u, -1), roll(u, 1), roll(v, -1), roll(v, 1), roll(h, -1), roll(h, 1),
                )
                div = level_sum(0.5 * (ue - uw) + 0.5 * (vn - vs))
                nu = wet * (
                    u
                    + TIME_STEP
                    * (
                        cor * v
                        - GRAVITY * (0.5 * (he - hw))
                        + VISCOSITY * (un + us + ue + uw - 4.0 * u)
                        - BOTTOM_DRAG * u
                    )
                )
                nv = wet * (
                    v
                    + TIME_STEP
                    * (
                        -cor * u
                        - GRAVITY * (0.5 * (hn - hs))
                        + VISCOSITY * (vn + vs + ve + vw - 4.0 * v)
                        - BOTTOM_DRAG * v
                    )
                )
                nh = h - TIME_STEP * DEPTH_SCALE * div
                put(p, i, nu, nv, nh)

    def put_first(p, i, nu, nv, nh):
        inside = jnp.broadcast_to(inside_ref[i + 2 : i + 3, :], (SUB, LANES))
        for f, value in enumerate((nu, nv, nh * inside)):
            b_ref[p, f, i + 1] = value

    def put_second(p, i, nu, nv, nh):
        for f, value in enumerate((nu, nv, nh)):
            c_ref[p, f, pl.ds(i * SUB, SUB), :] = value

    substep(a_ref, 2, put_first, -1, rows + 1)
    substep(b_ref, 1, put_second, 0, rows)

    def joined(f, start):
        lane8 = lax.broadcasted_iota(jnp.int32, (SUB, LANES), 1)
        main = c_ref[0, f, pl.ds(start, SUB, stride=SUB), :]
        edge = c_ref[1, f, pl.ds(start, SUB, stride=SUB), :]
        out = jnp.where(lane8 < 2, roll(edge, -8), main)
        return jnp.where(lane8 >= LANES - 2, roll(edge, LANES - 2 - (GROUP + 6)), out)

    for j in range(rows // SUB):
        for q in range(own_levels):
            lev = place * own_levels + q
            dst = q * rows + j * SUB
            east_ref[dst : dst + SUB, :] = joined(0, j * SUB * SUB + lev)
            north_ref[dst : dst + SUB, :] = joined(1, j * SUB * SUB + lev)
        height_ref[j * SUB : (j + 1) * SUB, :] = joined(2, j * SUB * SUB)


def momentum(place, coriolis, inside, flow_parts, rows, own_levels):
    vmem = pl.BlockSpec(memory_space=pltpu.VMEM)
    args = (coriolis, inside) + flow_parts
    return pl.pallas_call(
        momentum_kernel,
        in_specs=[pl.BlockSpec(memory_space=pltpu.SMEM)] + [vmem] * len(args),
        out_shape=(
            jax.ShapeDtypeStruct((own_levels * rows, LANES), F32),
            jax.ShapeDtypeStruct((own_levels * rows, LANES), F32),
            jax.ShapeDtypeStruct((rows, LANES), F32),
        ),
        scratch_shapes=[
            pltpu.VMEM((2, 4, rows + 4, SUB, LANES), F32),
            pltpu.VMEM((2, 3, rows + 2, SUB, LANES), F32),
            pltpu.VMEM((2, 3, rows * SUB, LANES), F32),
        ],
        name="momentum",
    )(place, *args)


def to_peer(block, k):
    count = lax.axis_size("trc")
    return lax.ppermute(block, "trc", [(i, i ^ k) for i in range(count)])


def shifted(block, dlat, dlon):
    nlat, nlon = lax.axis_size("lat"), lax.axis_size("lon")
    pairs = [
        (i * nlon + j, (i + dlat) * nlon + (j + dlon) % nlon)
        for i in range(nlat)
        for j in range(nlon)
        if 0 <= i + dlat < nlat
    ]
    return lax.ppermute(block, ("lat", "lon"), pairs)


def both_sides(block, dlat):
    left = shifted(block, dlat, 1)
    if lax.axis_size("lon") == 2:
        return left, left
    return left, shifted(block, dlat, -1)


def body(
    species_concentrations,
    zonal_velocity_array,
    meridional_velocity_array,
    thermal_anomaly,
    ocean_top_height_grid,
    water_layer_tally,
    species_interaction_table,
    species_production_pace,
    photon_uptake,
):
    count, levels, rows, cols = species_concentrations.shape
    own_levels = zonal_velocity_array.shape[0]
    shards = lax.axis_size("trc")
    assert levels == SUB and cols == LANES and count * GROUP == LANES and shards & (shards - 1) == 0
    trc_place = lax.axis_index("trc")
    place = trc_place.astype(jnp.int32).reshape(1)
    lat_total = rows * lax.axis_size("lat")
    lat_first = lax.axis_index("lat") * rows
    lat_global = (lat_first + jnp.arange(-2, rows + 2)).astype(F32)
    angle = math.pi * ((lat_global + 0.5) / lat_total - 0.5)
    spread = lambda v: jnp.broadcast_to(v[:, None], (v.shape[0], LANES))
    coriolis = spread(CORIOLIS_SCALE * jnp.sin(angle))
    surface = spread(1.0 + jnp.cos(angle[2:-2]))
    inside = spread(((lat_global >= 0) & (lat_global < lat_total)).astype(F32))

    x = species_concentrations.reshape(count, levels * rows, cols)
    own = jnp.stack([zonal_velocity_array, meridional_velocity_array]).reshape(
        2, own_levels * rows, cols
    )
    peers = [to_peer(own, k) for k in range(1, shards)]
    strip, *messages = pack_tracers(x)
    flow, fstrip, fcols, fup, fdown, dup, ddown = pack_flow(
        place, own, peers, water_layer_tally, ocean_top_height_grid, messages
    )
    up_in, down_in = shifted(fup, 1, 0), shifted(fdown, -1, 0)
    left_in, right_in = both_sides(fcols, 0)
    ul, ur = both_sides(dup, 1)
    dl, dr = both_sides(ddown, -1)
    flow_parts = (flow, fstrip, up_in, down_in, left_in, right_in, ul, ur, dl, dr)
    span = rows // PARTS
    blocks = []
    for part in range(PARTS):
        moved = transport(place, shards, x, strip, flow_parts, part * span, span)
        blocks.append([moved[0]] + [to_peer(moved[k], k) for k in range(1, shards)])
    back = []
    for part in range(PARTS):
        reacted = react(
            place,
            species_interaction_table,
            species_production_pace,
            photon_uptake,
            surface,
            water_layer_tally,
            blocks[part],
            part * span,
        )
        back.append([reacted[0]] + [to_peer(reacted[k], k) for k in range(1, shards)])
    late, back[-1][0] = lax.optimization_barrier((place, back[-1][0]))
    east_out, north_out, height_out = momentum(late, coriolis, inside, flow_parts, rows, own_levels)
    done = ()
    for part in range(PARTS):
        done = finish(
            place, thermal_anomaly, back[part], species_concentrations.shape, part, PARTS, done
        )
    updated, temperature = done
    vel = (own_levels, rows, cols)
    return (
        updated,
        east_out.reshape(vel),
        north_out.reshape(vel),
        temperature,
        height_out,
    )


def solution(mesh):
    return jax.shard_map(
        body,
        mesh=mesh,
        in_specs=(
            P("trc", None, "lat", "lon"),
            P("trc", "lat", "lon"),
            P("trc", "lat", "lon"),
            P("trc", "lat", "lon"),
            P("lat", "lon"),
            P("lat", "lon"),
            P(),
            P(),
            P(),
        ),
        out_specs=(
            P("trc", None, "lat", "lon"),
            P("trc", "lat", "lon"),
            P("trc", "lat", "lon"),
            P("trc", "lat", "lon"),
            P("lat", "lon"),
        ),
        check_vma=False,
    )
```

```python
import functools
import math

import jax
import jax.numpy as jnp
from jax import lax
from jax.experimental import pallas as pl
from jax.experimental.pallas import tpu as pltpu
from jax.sharding import PartitionSpec as P

TIME_STEP = 0.1
GRAVITY = 1.0
VISCOSITY = 0.2
BOTTOM_DRAG = 0.05
DEPTH_SCALE = 0.5
CORIOLIS_SCALE = 0.5
COLUMN_DEPTH = 2.0
WATER_ABSORB = 0.2
HALF_LIGHT = 0.5
REACT_STEP = 0.1
WARMING_WEIGHT = 1.0

SUB = 8
LANES = 128
HALO = 4
CORNER = 3
GROUP = 16
F32 = jnp.float32
TOGETHER = 2
PARTS = 2


def lane_ids():
    return lax.broadcasted_iota(jnp.int32, (SUB, LANES), 1)


def level_ids():
    return lax.broadcasted_iota(jnp.int32, (SUB, LANES), 0)


def roll(x, shift):
    shift = shift % LANES
    return x if shift == 0 else pltpu.roll(x, shift, 1)


def strip_of(rows):
    lane = lane_ids()
    out = None
    for t, value in enumerate(rows):
        rolled = roll(value, GROUP * t + GROUP // 2)
        if out is None:
            out = rolled
        else:
            out = jnp.where(lane // GROUP == t, rolled, out)
    return out


def middle_mask():
    lane = lane_ids() % GROUP
    return (lane >= 4) & (lane < 12)


def pair_up(first, second):
    return jnp.where(middle_mask(), first, roll(second, 8))


def quad_up(a, b, c, d):
    return jnp.where(lane_ids() < 64, pair_up(a, b), roll(pair_up(c, d), 64))


def merge_left(own, got):
    lane = lane_ids() % GROUP
    return jnp.where((lane >= 4) & (lane < 8), got, own)


def merge_right(own, got):
    lane = lane_ids() % GROUP
    return jnp.where((lane >= 8) & (lane < 12), got, own)


def replicate(strip, group):
    out = jnp.where(lane_ids() // GROUP == group, strip, 0.0)
    for shift in (16, 32, 64):
        out = out + roll(out, shift)
    return out


def over_levels(row):
    return jnp.broadcast_to(row[0:1, :], (SUB, LANES))


def pack_tracers_kernel(x_ref, strip_ref, up_ref, down_ref, cols_ref):
    count, rows = x_ref.shape[0], x_ref.shape[1] // SUB
    half = rows // 2

    def row_strip(r):
        return strip_of([x_ref[t, pl.ds(r, SUB, stride=rows), :] for t in range(count)])

    for r in range(half):
        low, high = row_strip(r), row_strip(r + half)
        strip_ref[r] = low
        strip_ref[r + half] = high
        cols_ref[r] = pair_up(low, high)
    for t in range(count):
        for j in range(HALO):
            down_ref[t * HALO + j] = x_ref[t, pl.ds(j, SUB, stride=rows), :]
            up_ref[t * HALO + j] = x_ref[t, pl.ds(rows - HALO + j, SUB, stride=rows), :]


def pack_tracers(x):
    count, rows = x.shape[0], x.shape[1] // SUB
    tile = lambda n: jax.ShapeDtypeStruct((n, SUB, LANES), F32)
    return pl.pallas_call(
        pack_tracers_kernel,
        out_shape=(
            tile(rows),
            tile(count * HALO),
            tile(count * HALO),
            tile(rows // 2),
        ),
        name="pack_tracers",
    )(x)


def pack_flow_kernel(place_ref, own_ref, *refs):
    peers, rest = refs[:-11], refs[-11:]
    tally_ref, height_ref, tup_ref, tdown_ref, tcols_ref = rest[:5]
    flow_ref, strip_ref, cols_ref, up_ref, down_ref, all_ref = rest[5:]
    rows = tally_ref.shape[0]
    span = own_ref.shape[1]
    place = place_ref[0]
    for k, ref in enumerate((own_ref,) + tuple(peers)):
        base = pl.multiple_of((place ^ k) * span, SUB)
        for f in range(2):
            all_ref[f, pl.ds(base, span), :] = ref[f]
    for src, dst in ((tup_ref, up_ref), (tdown_ref, down_ref), (tcols_ref, cols_ref)):
        dst[0 : src.shape[0]] = src[...]
    nrow, ncol = tup_ref.shape[0], tcols_ref.shape[0]
    level = level_ids()
    tally_all = tally_ref[...].astype(F32)
    pair_all = jnp.minimum(tally_all, pltpu.roll(tally_all, LANES - 1, 1))
    wide = lambda v, r: jnp.broadcast_to(v[r : r + 1, :], (SUB, LANES))
    for r in range(rows):
        tally, height, pair = wide(tally_all, r), wide(height_ref, r), wide(pair_all, r)
        wet = level.astype(F32) < tally
        east = jnp.where(wet, all_ref[0, pl.ds(r, SUB, stride=rows), :], 0.0)
        north = jnp.where(wet, all_ref[1, pl.ds(r, SUB, stride=rows), :], 0.0)
        aux = jnp.where(level == 0, tally, jnp.where(level == 1, height, pair))
        for f, value in enumerate((east, north, aux)):
            flow_ref[f * rows + r] = value
            if r < HALO:
                down_ref[nrow + f * HALO + r] = value
            if r >= rows - HALO:
                up_ref[nrow + f * HALO + r - (rows - HALO)] = value
        strip_ref[r] = strip_of([east, north, aux])
    quarter = rows // 4
    for r in range(quarter):
        cols_ref[ncol + r] = quad_up(*[strip_ref[r + quarter * q] for q in range(4)])


def pack_flow(place, own, peers, tally, height, messages):
    rows = tally.shape[0]
    tile = lambda n: jax.ShapeDtypeStruct((n, SUB, LANES), F32)
    vmem = pl.BlockSpec(memory_space=pltpu.VMEM)
    tup, tdown, tcols = messages
    return pl.pallas_call(
        pack_flow_kernel,
        in_specs=[pl.BlockSpec(memory_space=pltpu.SMEM)] + [vmem] * (3 + len(peers) + len(messages)),
        out_shape=(
            tile(3 * rows),
            tile(rows),
            tile(tcols.shape[0] + rows // 4),
            tile(tup.shape[0] + 3 * HALO),
            tile(tdown.shape[0] + 3 * HALO),
        ),
        scratch_shapes=[pltpu.VMEM((2, SUB * rows, LANES), F32)],
        name="pack_flow",
    )(place, own, *peers, tally, height, *messages)


def pack_edges_kernel(up_ref, down_ref, cols_ref, out_ref):
    own = cols_ref.shape[0]
    out_ref[0:own] = cols_ref[...]
    count = up_ref.shape[0] // HALO - 3
    for n, ref in enumerate((up_ref, down_ref)):
        row = lambda f, j: ref[f * HALO + j]
        tracers = [strip_of([row(t, j) for t in range(count)]) for j in range(HALO)]
        flows = [strip_of([row(count + f, j) for f in range(3)]) for j in range(HALO)]
        base = own + n * CORNER
        for j in range(2):
            out_ref[base + j] = pair_up(tracers[j], tracers[j + 2])
        out_ref[base + 2] = quad_up(*flows)


def pack_edges(up, down, cols):
    return pl.pallas_call(
        pack_edges_kernel,
        out_shape=jax.ShapeDtypeStruct((cols.shape[0] + 2 * CORNER, SUB, LANES), F32),
        name="pack_edges",
    )(up, down, cols)


class Flow:
    def __init__(self, flow_ref, strip_ref, up_ref, down_ref, left_ref, right_ref):
        self.flow, self.strip, self.up, self.down = flow_ref, strip_ref, up_ref, down_ref
        self.left, self.right = left_ref, right_ref
        self.rows = strip_ref.shape[0]
        self.row_base = up_ref.shape[0] - 3 * HALO
        self.corner_base = left_ref.shape[0] - 2 * CORNER
        self.col_base = self.corner_base - self.rows // 4

    def corner(self, r):
        return self.corner_base if r < 0 else self.corner_base + CORNER

    def row(self, f, r):
        if r < 0:
            return self.up[self.row_base + f * HALO + HALO + r]
        if r >= self.rows:
            return self.down[self.row_base + f * HALO + r - self.rows]
        return self.flow[f * self.rows + r]

    def strips(self, r):
        if 0 <= r < self.rows:
            quarter = self.rows // 4
            q, j = divmod(r, quarter)
            own = self.strip[r]
            left, right = self.left[self.col_base + j], self.right[self.col_base + j]
        else:
            own = strip_of([self.row(f, r) for f in range(3)])
            q = r + HALO if r < 0 else r - self.rows
            at = self.corner(r) + CORNER - 1
            left, right = self.left[at], self.right[at]
        shift = -(8 * (q % 2) + 64 * (q // 2))
        return merge_left(own, roll(left, shift)), merge_right(own, roll(right, shift))


def limited(ahead, behind):
    return jnp.maximum(
        jnp.minimum(ahead, jnp.maximum(behind, 0.0)), jnp.minimum(behind, 0.0)
    )


def face_pair(vel, vel_next, wet):
    a = jnp.where(wet, 0.5 * (vel + vel_next), 0.0)
    size = jnp.abs(a)
    return a, 0.5 * size * (1.0 - size)


def transport_rows(streams, ax_ref, bx_ref, ay_ref, by_ref, first, last):
    states = []
    for load, _, _ in streams:
        before, here, after = load(first - 2), load(first - 1), load(first)
        states.append((here, after, limited(after - here, here - before), after - here, None))
    for i in range(first - 1, last):
        for n, (load, store, kind) in enumerate(streams):
            row, nxt, slope, diff, below = states[n]
            far = load(i + 2)
            diff_next = far - nxt
            slope_next = limited(diff_next, diff)
            ay, by = ay_ref[kind, i + 3], by_ref[kind, i + 3]
            positive = ay >= 0.0
            above = ay * jnp.where(positive, row, nxt) + by * jnp.where(positive, slope, slope_next)
            if below is not None:
                ax, bx = ax_ref[kind, i + 2], bx_ref[kind, i + 2]
                east = roll(row, -1)
                dx = east - row
                sx = limited(dx, roll(dx, 1))
                sx_east = roll(sx, -1)
                pos = ax >= 0.0
                fx = ax * jnp.where(pos, row, east) + bx * jnp.where(pos, sx, sx_east)
                store(i, row - (fx - roll(fx, 1)) - (above - below))
            states[n] = (nxt, far, slope_next, diff_next, above)


def select_lanes(moves):
    parts = []
    source = lax.broadcasted_iota(jnp.int32, (LANES, LANES), 0)
    target = lax.broadcasted_iota(jnp.int32, (LANES, LANES), 1)
    for f, d in moves:
        parts.append(jnp.where(source == GROUP * f + target % GROUP + d, 1.0, 0.0))
    return jnp.concatenate(parts, axis=1)


def exact_dot(a, b):
    return jnp.dot(a, b, precision=lax.Precision.HIGHEST, preferred_element_type=F32)


def transport_kernel(
    place_ref,
    x_ref,
    strip_ref,
    flow_ref,
    fstrip_ref,
    up_ref,
    down_ref,
    left_ref,
    right_ref,
    *refs,
    first_row,
):
    *outs, ext_ref, ax_ref, bx_ref, ay_ref, by_ref, first_ref, moved_ref, edge_ref, spread_ref, main_ref, shift_ref = refs
    count, rows = x_ref.shape[0], x_ref.shape[1] // SUB
    half = rows // 2
    span = moved_ref.shape[1]
    place = place_ref[0]
    level = level_ids().astype(F32)
    flow = Flow(flow_ref, fstrip_ref, up_ref, down_ref, left_ref, right_ref)

    for q in range(-HALO, span + HALO):
        at = pl.ds((q + HALO) * SUB, SUB)
        main_ref[at, :] = flow.row(0, first_row + q)
        left, right = flow.strips(first_row + q)
        edge_ref[0, at, :] = left
        edge_ref[1, at, :] = right
    shift_east = jnp.where(
        lax.broadcasted_iota(jnp.int32, (LANES, LANES), 0)
        == lax.broadcasted_iota(jnp.int32, (LANES, LANES), 1) + 1,
        1.0,
        0.0,
    )
    shift_ref[...] = exact_dot(main_ref[...], shift_east)
    moves = select_lanes(((0, 0), (0, 1), (1, 0), (2, 0), (2, 1)))
    for side in range(2):
        spread_ref[side] = exact_dot(edge_ref[side], moves)

    previous = None
    for q in range(-HALO, span + HALO):
        at = pl.ds((q + HALO) * SUB, SUB)
        aux = flow.row(2, first_row + q)
        wide = lambda v, i: jnp.broadcast_to(v[i : i + 1, :], (SUB, LANES))
        kinds = [(main_ref[at, :], shift_ref[at, :], flow.row(1, first_row + q), wide(aux, 0), wide(aux, 2))]
        for side in range(2):
            east, east_next, north, tally, tally_next = (
                spread_ref[side, at, LANES * n : LANES * (n + 1)] for n in range(5)
            )
            tally, tally_next = wide(tally, 0), wide(tally_next, 0)
            kinds.append((east, east_next, north, tally, jnp.minimum(tally, tally_next)))
        for kind, (east, east_next, north, tally, pair) in enumerate(kinds):
            if -2 <= q < span + 2:
                ax_ref[kind, q + 2], bx_ref[kind, q + 2] = face_pair(east, east_next, level < pair)
            if previous is not None and -3 <= q - 1 < span + 2:
                below, depth = previous[kind]
                ay_ref[kind, q + 2], by_ref[kind, q + 2] = face_pair(
                    below, north, level < jnp.minimum(depth, tally)
                )
        previous = [(k[2], k[3]) for k in kinds]

    for q in range(-HALO, span + HALO):
        r = first_row + q
        if r < 0 or r >= rows:
            src = up_ref if r < 0 else down_ref
            j = r + HALO if r < 0 else r - rows
            fields = [src[t * HALO + j] for t in range(count)]
            own = strip_of(fields)
            left, right = left_ref[flow.corner(r) + j % 2], right_ref[flow.corner(r) + j % 2]
            swap = j >= 2
        else:
            fields = [x_ref[t, pl.ds(r, SUB, stride=rows), :] for t in range(count)]
            own = strip_ref[r]
            left, right = left_ref[r % half], right_ref[r % half]
            swap = r >= half
        if swap:
            left, right = roll(left, -8), roll(right, -8)
        fields += [merge_left(own, left), merge_right(own, right)]
        for t, value in enumerate(fields):
            ext_ref[t, HALO + q] = value

    def some(c, carry):
        places = [c * TOGETHER + n for n in range(TOGETHER)]
        kinds = [jnp.maximum(p - (count - 1), 0) for p in places]
        transport_rows(
            [
                (
                    lambda i, p=p: ext_ref[p, HALO + i],
                    lambda i, value, n=n: first_ref.__setitem__((n, i + 2), value),
                    kinds[n],
                )
                for n, p in enumerate(places)
            ],
            ax_ref, bx_ref, ay_ref, by_ref, -2, span + 2,
        )
        transport_rows(
            [
                (
                    lambda i, n=n: first_ref[n, 2 + i],
                    lambda i, value, p=p: moved_ref.__setitem__((p, i), value),
                    kinds[n],
                )
                for n, p in enumerate(places)
            ],
            ax_ref, bx_ref, ay_ref, by_ref, 0, span,
        )
        return carry

    lax.fori_loop(0, (count + 2) // TOGETHER, some, 0)

    lane = lane_ids()
    edge = (lane < 4) | (lane >= LANES - 4)
    from_right = (lane % GROUP >= 4) & (lane % GROUP < 8)
    share = span // len(outs)
    for k, out_ref in enumerate(outs):
        base = (place ^ k) * share
        for r in range(share):
            joined = jnp.where(from_right, moved_ref[count + 1, base + r], moved_ref[count, base + r])
            for t in range(count):
                out_ref[t * share + r] = jnp.where(
                    edge, roll(joined, -(GROUP * t + 8)), moved_ref[t, base + r]
                )


def transport(place, shards, x, strip, flow_parts, first_row, span):
    count = x.shape[0]
    vmem = pl.BlockSpec(memory_space=pltpu.VMEM)
    tile = lambda *n: pltpu.VMEM(n + (SUB, LANES), F32)
    flat = lambda *n: pltpu.VMEM(n, F32)
    args = (x, strip) + flow_parts
    wide = (span + 2 * HALO) * SUB
    return pl.pallas_call(
        functools.partial(transport_kernel, first_row=first_row),
        in_specs=[pl.BlockSpec(memory_space=pltpu.SMEM)] + [vmem] * len(args),
        out_shape=tuple(
            jax.ShapeDtypeStruct((count * span // shards, SUB, LANES), F32) for _ in range(shards)
        ),
        scratch_shapes=[
            tile(count + 2, span + 2 * HALO),
            tile(3, span + 4),
            tile(3, span + 4),
            tile(3, span + 5),
            tile(3, span + 5),
            tile(TOGETHER, span + 4),
            tile(count + 2, span),
            flat(2, wide, LANES),
            flat(2, wide, 5 * LANES),
            flat(wide, LANES),
            flat(wide, LANES),
        ],
        name="transport",
    )(place, *args)


def react_kernel(place_ref, table_ref, pace_ref, uptake_ref, surface_ref, tally_ref, *refs, first_row):
    shards = (len(refs) - 3) // 2
    ins, outs = refs[:shards], refs[shards : 2 * shards]
    light_ref, wet_ref, heat_ref = refs[2 * shards :]
    total = pace_ref.shape[0]
    count = total // shards
    share = ins[0].shape[0] // count
    place = place_ref[0]
    level = level_ids()

    for r in range(share):
        row = first_row + place * share + r
        tally = jnp.broadcast_to(tally_ref[pl.ds(row, 1), :], (SUB, LANES))
        surface = jnp.broadcast_to(surface_ref[pl.ds(row, 1), :], (SUB, LANES))
        wet = jnp.where(level < tally, 1.0, 0.0)
        absorbed = jnp.zeros((SUB, LANES), F32)
        for k, ref in enumerate(ins):
            for t in range(count):
                absorbed = absorbed + uptake_ref[(place ^ k) * count + t] * jnp.abs(ref[t * share + r])
        layer = (COLUMN_DEPTH / SUB) * (WATER_ABSORB + absorbed) * wet
        total_depth = jnp.where(level >= 1, pltpu.roll(layer, 1, 0), 0.0)
        for shift in (1, 2, 4):
            total_depth = total_depth + jnp.where(
                level >= shift, pltpu.roll(total_depth, shift, 0), 0.0
            )
        top = surface * jnp.exp(-total_depth)
        heat_ref[pl.ds(r * SUB, SUB), :] = top * (1.0 - jnp.exp(-layer))
        light_ref[r] = REACT_STEP * wet * (top / (top + HALF_LIGHT))
        wet_ref[r] = REACT_STEP * wet

    block = 4
    for k, out_ref in enumerate(outs):
        for m0 in range(0, count, block):
            dest = [(place ^ k) * count + m0 + j for j in range(block)]
            acc = [[None] * share for _ in range(block)]
            for kk, ref in enumerate(ins):
                for t in range(count):
                    n = (place ^ kk) * count + t
                    values = [ref[t * share + r] for r in range(share)]
                    for j in range(block):
                        c = table_ref[dest[j], n]
                        for r in range(share):
                            term = c * values[r]
                            acc[j][r] = term if acc[j][r] is None else acc[j][r] + term
            for j in range(block):
                pace = pace_ref[dest[j]]
                for r in range(share):
                    own = ins[k][(m0 + j) * share + r]
                    out_ref[(m0 + j) * share + r] = (
                        own + wet_ref[r] * acc[j][r] + pace * (light_ref[r] * own)
                    )
        own_levels = SUB // shards
        out_ref[count * share] = jnp.concatenate(
            [
                heat_ref[pl.ds((place ^ k) * own_levels + q, share, stride=SUB), :]
                for q in range(own_levels)
            ],
            axis=0,
        )


def react(place, table, pace, uptake, surface, tally, blocks, first_row):
    shards = len(blocks)
    share = blocks[0].shape[0] // (pace.shape[0] // shards)
    smem = pl.BlockSpec(memory_space=pltpu.SMEM)
    vmem = pl.BlockSpec(memory_space=pltpu.VMEM)
    assert share * (SUB // shards) == SUB
    return pl.pallas_call(
        functools.partial(react_kernel, first_row=first_row),
        in_specs=[smem] * 4 + [vmem] * (2 + shards),
        out_shape=tuple(
            jax.ShapeDtypeStruct((b.shape[0] + 1, SUB, LANES), F32) for b in blocks
        ),
        scratch_shapes=[
            pltpu.VMEM((share, SUB, LANES), F32),
            pltpu.VMEM((share, SUB, LANES), F32),
            pltpu.VMEM((share * SUB, LANES), F32),
        ],
        name="react",
    )(place, table, pace, uptake, surface, tally, *blocks)


def finish_kernel(place_ref, thermal_ref, *refs, shards):
    ins, (out_ref, temp_ref, cells_ref, heat_ref) = refs[:shards], refs[-4:]
    count, _, span, _ = out_ref.shape
    share = span // shards
    place = place_ref[0]
    own_levels = SUB // shards
    level = level_ids()
    for k, ref in enumerate(ins):
        base = (place ^ k) * share
        for m in range(count):
            for r in range(share):
                at = pl.multiple_of((m * span + base + r) * SUB, SUB)
                cells_ref[pl.ds(at, SUB), :] = ref[m * share + r]
        heat = ref[count * share]
        for q in range(own_levels):
            heat_ref[q, place ^ k] = heat if q == 0 else pltpu.roll(heat, SUB - q * share, 0)
    per_tile = SUB // share
    for b in range(span // SUB):
        for m in range(count):
            for lev in range(SUB):
                start = (m * span + b * SUB) * SUB + lev
                out_ref[m, lev, b * SUB : (b + 1) * SUB, :] = cells_ref[pl.ds(start, SUB, stride=SUB), :]
        for q in range(own_levels):
            heat = heat_ref[q, b * per_tile]
            for n in range(1, per_tile):
                part = pltpu.roll(heat_ref[q, b * per_tile + n], n * share, 0)
                heat = jnp.where(level // share == n, part, heat)
            at = slice(b * SUB, (b + 1) * SUB)
            temp_ref[q, at, :] = thermal_ref[q, at, :] + WARMING_WEIGHT * heat


def finish(place, thermal, blocks, shape, part, parts, before):
    shards = len(blocks)
    count, levels, rows, cols = shape
    own_levels = thermal.shape[0]
    span = rows // parts
    vmem = pl.BlockSpec(memory_space=pltpu.VMEM)
    hold = pl.BlockSpec(memory_space=pl.ANY)
    of_part = lambda *lead: pl.BlockSpec(
        lead + (span, cols), lambda i: (0,) * len(lead) + (part, 0)
    )
    return pl.pallas_call(
        functools.partial(finish_kernel, shards=shards),
        grid=(1,),
        in_specs=[pl.BlockSpec(memory_space=pltpu.SMEM), of_part(own_levels)]
        + [vmem] * shards
        + [hold] * len(before),
        out_specs=(of_part(count, levels), of_part(own_levels)),
        out_shape=(jax.ShapeDtypeStruct(shape, F32), jax.ShapeDtypeStruct(thermal.shape, F32)),
        input_output_aliases={2 + shards + i: i for i in range(len(before))},
        scratch_shapes=[
            pltpu.VMEM((count * span * SUB, LANES), F32),
            pltpu.VMEM((own_levels, shards, SUB, LANES), F32),
        ],
        name="finish",
    )(place, thermal, *blocks, *before)


def level_sum(x):
    for shift in (4, 2, 1):
        x = x + pltpu.roll(x, shift, 0)
    return x


def momentum_kernel(
    place_ref,
    coriolis_ref,
    inside_ref,
    flow_ref,
    strip_ref,
    fup_ref,
    fdown_ref,
    colsl_ref,
    colsr_ref,
    east_ref,
    north_ref,
    height_ref,
    a_ref,
    b_ref,
    c_ref,
):
    rows = height_ref.shape[0]
    own_levels = east_ref.shape[0] // rows
    place = place_ref[0]
    lane = lane_ids()
    level = level_ids().astype(F32)
    flow = Flow(flow_ref, strip_ref, fup_ref, fdown_ref, colsl_ref, colsr_ref)
    for r in range(-2, rows + 2):
        east, north, aux = (flow.row(f, r) for f in range(3))
        left, right = flow.strips(r)
        both = [
            jnp.where(lane < GROUP, roll(left, -GROUP * f), roll(right, GROUP - GROUP * f))
            for f in range(3)
        ]
        for p, (u, v, w) in enumerate(((east, north, aux), both)):
            wet = jnp.where(level < over_levels(w), 1.0, 0.0)
            h = jnp.broadcast_to(w[1:2, :], (SUB, LANES))
            for f, value in enumerate((u, v, h, wet)):
                a_ref[p, f, r + 2] = value

    def substep(src, offset, put, first, last):
        for p in range(2):
            for i in range(first, last):
                g = lambda f, d: src[p, f, i + offset + d]
                u, v, h = g(0, 0), g(1, 0), g(2, 0)
                un, us, vn, vs, hn, hs = g(0, 1), g(0, -1), g(1, 1), g(1, -1), g(2, 1), g(2, -1)
                wet = a_ref[p, 3, i + 2]
                cor = jnp.broadcast_to(coriolis_ref[i + 2 : i + 3, :], (SUB, LANES))
                ue, uw, ve, vw, he, hw = (
                    roll(u, -1), roll(u, 1), roll(v, -1), roll(v, 1), roll(h, -1), roll(h, 1),
                )
                div = level_sum(0.5 * (ue - uw) + 0.5 * (vn - vs))
                nu = wet * (
                    u
                    + TIME_STEP
                    * (
                        cor * v
                        - GRAVITY * (0.5 * (he - hw))
                        + VISCOSITY * (un + us + ue + uw - 4.0 * u)
                        - BOTTOM_DRAG * u
                    )
                )
                nv = wet * (
                    v
                    + TIME_STEP
                    * (
                        -cor * u
                        - GRAVITY * (0.5 * (hn - hs))
                        + VISCOSITY * (vn + vs + ve + vw - 4.0 * v)
                        - BOTTOM_DRAG * v
                    )
                )
                nh = h - TIME_STEP * DEPTH_SCALE * div
                put(p, i, nu, nv, nh)

    def put_first(p, i, nu, nv, nh):
        inside = jnp.broadcast_to(inside_ref[i + 2 : i + 3, :], (SUB, LANES))
        for f, value in enumerate((nu, nv, nh * inside)):
            b_ref[p, f, i + 1] = value

    def put_second(p, i, nu, nv, nh):
        for f, value in enumerate((nu, nv, nh)):
            c_ref[p, f, pl.ds(i * SUB, SUB), :] = value

    substep(a_ref, 2, put_first, -1, rows + 1)
    substep(b_ref, 1, put_second, 0, rows)

    def joined(f, start):
        lane8 = lax.broadcasted_iota(jnp.int32, (SUB, LANES), 1)
        main = c_ref[0, f, pl.ds(start, SUB, stride=SUB), :]
        edge = c_ref[1, f, pl.ds(start, SUB, stride=SUB), :]
        out = jnp.where(lane8 < 2, roll(edge, -8), main)
        return jnp.where(lane8 >= LANES - 2, roll(edge, LANES - 2 - (GROUP + 6)), out)

    for j in range(rows // SUB):
        for q in range(own_levels):
            lev = place * own_levels + q
            dst = q * rows + j * SUB
            east_ref[dst : dst + SUB, :] = joined(0, j * SUB * SUB + lev)
            north_ref[dst : dst + SUB, :] = joined(1, j * SUB * SUB + lev)
        height_ref[j * SUB : (j + 1) * SUB, :] = joined(2, j * SUB * SUB)


def momentum(place, coriolis, inside, flow_parts, rows, own_levels):
    vmem = pl.BlockSpec(memory_space=pltpu.VMEM)
    args = (coriolis, inside) + flow_parts
    return pl.pallas_call(
        momentum_kernel,
        in_specs=[pl.BlockSpec(memory_space=pltpu.SMEM)] + [vmem] * len(args),
        out_shape=(
            jax.ShapeDtypeStruct((own_levels * rows, LANES), F32),
            jax.ShapeDtypeStruct((own_levels * rows, LANES), F32),
            jax.ShapeDtypeStruct((rows, LANES), F32),
        ),
        scratch_shapes=[
            pltpu.VMEM((2, 4, rows + 4, SUB, LANES), F32),
            pltpu.VMEM((2, 3, rows + 2, SUB, LANES), F32),
            pltpu.VMEM((2, 3, rows * SUB, LANES), F32),
        ],
        name="momentum",
    )(place, *args)


def to_peer(block, k):
    count = lax.axis_size("trc")
    return lax.ppermute(block, "trc", [(i, i ^ k) for i in range(count)])


def from_lat(block, step):
    count = lax.axis_size("lat")
    return lax.ppermute(
        block, "lat", [(i, i + step) for i in range(count) if 0 <= i + step < count]
    )


def both_sides(block):
    count = lax.axis_size("lon")
    left = lax.ppermute(block, "lon", [(i, (i + 1) % count) for i in range(count)])
    if count == 2:
        return left, left
    return left, lax.ppermute(block, "lon", [(i, (i - 1) % count) for i in range(count)])


def body(
    species_concentrations,
    zonal_velocity_array,
    meridional_velocity_array,
    thermal_anomaly,
    ocean_top_height_grid,
    water_layer_tally,
    species_interaction_table,
    species_production_pace,
    photon_uptake,
):
    count, levels, rows, cols = species_concentrations.shape
    own_levels = zonal_velocity_array.shape[0]
    shards = lax.axis_size("trc")
    assert levels == SUB and cols == LANES and count * GROUP == LANES and shards & (shards - 1) == 0
    trc_place = lax.axis_index("trc")
    place = trc_place.astype(jnp.int32).reshape(1)
    lat_total = rows * lax.axis_size("lat")
    lat_first = lax.axis_index("lat") * rows
    lat_global = (lat_first + jnp.arange(-2, rows + 2)).astype(F32)
    angle = math.pi * ((lat_global + 0.5) / lat_total - 0.5)
    spread = lambda v: jnp.broadcast_to(v[:, None], (v.shape[0], LANES))
    coriolis = spread(CORIOLIS_SCALE * jnp.sin(angle))
    surface = spread(1.0 + jnp.cos(angle[2:-2]))
    inside = spread(((lat_global >= 0) & (lat_global < lat_total)).astype(F32))

    x = species_concentrations.reshape(count, levels * rows, cols)
    own = jnp.stack([zonal_velocity_array, meridional_velocity_array]).reshape(
        2, own_levels * rows, cols
    )
    peers = [to_peer(own, k) for k in range(1, shards)]
    strip, *messages = pack_tracers(x)
    flow, fstrip, fcols, fup, fdown = pack_flow(
        place, own, peers, water_layer_tally, ocean_top_height_grid, messages
    )
    up_in, down_in = from_lat(fup, 1), from_lat(fdown, -1)
    left_in, right_in = both_sides(pack_edges(up_in, down_in, fcols))
    flow_parts = (flow, fstrip, up_in, down_in, left_in, right_in)
    span = rows // PARTS
    blocks = []
    for part in range(PARTS):
        moved = transport(place, shards, x, strip, flow_parts, part * span, span)
        blocks.append([moved[0]] + [to_peer(moved[k], k) for k in range(1, shards)])
    back = []
    for part in range(PARTS):
        reacted = react(
            place,
            species_interaction_table,
            species_production_pace,
            photon_uptake,
            surface,
            water_layer_tally,
            blocks[part],
            part * span,
        )
        back.append([reacted[0]] + [to_peer(reacted[k], k) for k in range(1, shards)])
    late, back[-1][0] = lax.optimization_barrier((place, back[-1][0]))
    east_out, north_out, height_out = momentum(late, coriolis, inside, flow_parts, rows, own_levels)
    done = ()
    for part in range(PARTS):
        done = finish(
            place, thermal_anomaly, back[part], species_concentrations.shape, part, PARTS, done
        )
    updated, temperature = done
    vel = (own_levels, rows, cols)
    return (
        updated,
        east_out.reshape(vel),
        north_out.reshape(vel),
        temperature,
        height_out,
    )


def solution(mesh):
    return jax.shard_map(
        body,
        mesh=mesh,
        in_specs=(
            P("trc", None, "lat", "lon"),
            P("trc", "lat", "lon"),
            P("trc", "lat", "lon"),
            P("trc", "lat", "lon"),
            P("lat", "lon"),
            P("lat", "lon"),
            P(),
            P(),
            P(),
        ),
        out_specs=(
            P("trc", None, "lat", "lon"),
            P("trc", "lat", "lon"),
            P("trc", "lat", "lon"),
            P("trc", "lat", "lon"),
            P("lat", "lon"),
        ),
        check_vma=False,
    )
```

```python
import functools
import math

import jax
import jax.numpy as jnp
from jax import lax
from jax.experimental import pallas as pl
from jax.experimental.pallas import tpu as pltpu
from jax.sharding import PartitionSpec as P

TIME_STEP = 0.1
GRAVITY = 1.0
VISCOSITY = 0.2
BOTTOM_DRAG = 0.05
DEPTH_SCALE = 0.5
CORIOLIS_SCALE = 0.5
COLUMN_DEPTH = 2.0
WATER_ABSORB = 0.2
HALF_LIGHT = 0.5
REACT_STEP = 0.1
WARMING_WEIGHT = 1.0

SUB = 8
LANES = 128
HALO = 4
CORNER = 3
GROUP = 16
F32 = jnp.float32
TOGETHER = 2
PARTS = 2


def lane_ids():
    return lax.broadcasted_iota(jnp.int32, (SUB, LANES), 1)


def level_ids():
    return lax.broadcasted_iota(jnp.int32, (SUB, LANES), 0)


def roll(x, shift):
    shift = shift % LANES
    return x if shift == 0 else pltpu.roll(x, shift, 1)


def strip_of(rows):
    lane = lane_ids()
    out = None
    for t, value in enumerate(rows):
        rolled = roll(value, GROUP * t + GROUP // 2)
        if out is None:
            out = rolled
        else:
            out = jnp.where(lane // GROUP == t, rolled, out)
    return out


def middle_mask():
    lane = lane_ids() % GROUP
    return (lane >= 4) & (lane < 12)


def pair_up(first, second):
    return jnp.where(middle_mask(), first, roll(second, 8))


def quad_up(a, b, c, d):
    return jnp.where(lane_ids() < 64, pair_up(a, b), roll(pair_up(c, d), 64))


def merge_left(own, got):
    lane = lane_ids() % GROUP
    return jnp.where((lane >= 4) & (lane < 8), got, own)


def merge_right(own, got):
    lane = lane_ids() % GROUP
    return jnp.where((lane >= 8) & (lane < 12), got, own)


def replicate(strip, group):
    out = jnp.where(lane_ids() // GROUP == group, strip, 0.0)
    for shift in (16, 32, 64):
        out = out + roll(out, shift)
    return out


def over_levels(row):
    return jnp.broadcast_to(row[0:1, :], (SUB, LANES))


def grant(mib):
    return pltpu.CompilerParams(vmem_limit_bytes=mib << 20)


def pack_tracers_kernel(x_ref, strip_ref, up_ref, down_ref, cols_ref):
    count, rows = x_ref.shape[0], x_ref.shape[1] // SUB
    half = rows // 2

    def row_strip(r):
        return strip_of([x_ref[t, pl.ds(r, SUB, stride=rows), :] for t in range(count)])

    for r in range(half):
        low, high = row_strip(r), row_strip(r + half)
        strip_ref[r] = low
        strip_ref[r + half] = high
        cols_ref[r] = pair_up(low, high)
    for t in range(count):
        for j in range(HALO):
            down_ref[t * HALO + j] = x_ref[t, pl.ds(j, SUB, stride=rows), :]
            up_ref[t * HALO + j] = x_ref[t, pl.ds(rows - HALO + j, SUB, stride=rows), :]


def pack_tracers(x):
    count, rows = x.shape[0], x.shape[1] // SUB
    tile = lambda n: jax.ShapeDtypeStruct((n, SUB, LANES), F32)
    return pl.pallas_call(
        pack_tracers_kernel,
        out_shape=(
            tile(rows),
            tile(count * HALO),
            tile(count * HALO),
            tile(rows // 2),
        ),
        compiler_params=grant(8),
        name="pack_tracers",
    )(x)


def pack_flow_kernel(place_ref, own_ref, *refs):
    peers, rest = refs[:-11], refs[-11:]
    tally_ref, height_ref, tup_ref, tdown_ref, tcols_ref = rest[:5]
    flow_ref, strip_ref, cols_ref, up_ref, down_ref, all_ref = rest[5:]
    rows = tally_ref.shape[0]
    span = own_ref.shape[1]
    place = place_ref[0]
    for k, ref in enumerate((own_ref,) + tuple(peers)):
        base = pl.multiple_of((place ^ k) * span, SUB)
        for f in range(2):
            all_ref[f, pl.ds(base, span), :] = ref[f]
    for src, dst in ((tup_ref, up_ref), (tdown_ref, down_ref), (tcols_ref, cols_ref)):
        dst[0 : src.shape[0]] = src[...]
    nrow, ncol = tup_ref.shape[0], tcols_ref.shape[0]
    level = level_ids()
    tally_all = tally_ref[...].astype(F32)
    pair_all = jnp.minimum(tally_all, pltpu.roll(tally_all, LANES - 1, 1))
    wide = lambda v, r: jnp.broadcast_to(v[r : r + 1, :], (SUB, LANES))
    for r in range(rows):
        tally, height, pair = wide(tally_all, r), wide(height_ref, r), wide(pair_all, r)
        wet = level.astype(F32) < tally
        east = jnp.where(wet, all_ref[0, pl.ds(r, SUB, stride=rows), :], 0.0)
        north = jnp.where(wet, all_ref[1, pl.ds(r, SUB, stride=rows), :], 0.0)
        aux = jnp.where(level == 0, tally, jnp.where(level == 1, height, pair))
        for f, value in enumerate((east, north, aux)):
            flow_ref[f * rows + r] = value
            if r < HALO:
                down_ref[nrow + f * HALO + r] = value
            if r >= rows - HALO:
                up_ref[nrow + f * HALO + r - (rows - HALO)] = value
        strip_ref[r] = strip_of([east, north, aux])
    quarter = rows // 4
    for r in range(quarter):
        cols_ref[ncol + r] = quad_up(*[strip_ref[r + quarter * q] for q in range(4)])


def pack_flow(place, own, peers, tally, height, messages):
    rows = tally.shape[0]
    tile = lambda n: jax.ShapeDtypeStruct((n, SUB, LANES), F32)
    vmem = pl.BlockSpec(memory_space=pltpu.VMEM)
    tup, tdown, tcols = messages
    return pl.pallas_call(
        pack_flow_kernel,
        in_specs=[pl.BlockSpec(memory_space=pltpu.SMEM)] + [vmem] * (3 + len(peers) + len(messages)),
        out_shape=(
            tile(3 * rows),
            tile(rows),
            tile(tcols.shape[0] + rows // 4),
            tile(tup.shape[0] + 3 * HALO),
            tile(tdown.shape[0] + 3 * HALO),
        ),
        scratch_shapes=[pltpu.VMEM((2, SUB * rows, LANES), F32)],
        compiler_params=grant(8),
        name="pack_flow",
    )(place, own, *peers, tally, height, *messages)


def pack_edges_kernel(up_ref, down_ref, cols_ref, out_ref):
    own = cols_ref.shape[0]
    out_ref[0:own] = cols_ref[...]
    count = up_ref.shape[0] // HALO - 3
    for n, ref in enumerate((up_ref, down_ref)):
        row = lambda f, j: ref[f * HALO + j]
        tracers = [strip_of([row(t, j) for t in range(count)]) for j in range(HALO)]
        flows = [strip_of([row(count + f, j) for f in range(3)]) for j in range(HALO)]
        base = own + n * CORNER
        for j in range(2):
            out_ref[base + j] = pair_up(tracers[j], tracers[j + 2])
        out_ref[base + 2] = quad_up(*flows)


def pack_edges(up, down, cols):
    return pl.pallas_call(
        pack_edges_kernel,
        out_shape=jax.ShapeDtypeStruct((cols.shape[0] + 2 * CORNER, SUB, LANES), F32),
        compiler_params=grant(8),
        name="pack_edges",
    )(up, down, cols)


class Flow:
    def __init__(self, flow_ref, strip_ref, up_ref, down_ref, left_ref, right_ref):
        self.flow, self.strip, self.up, self.down = flow_ref, strip_ref, up_ref, down_ref
        self.left, self.right = left_ref, right_ref
        self.rows = strip_ref.shape[0]
        self.row_base = up_ref.shape[0] - 3 * HALO
        self.corner_base = left_ref.shape[0] - 2 * CORNER
        self.col_base = self.corner_base - self.rows // 4

    def corner(self, r):
        return self.corner_base if r < 0 else self.corner_base + CORNER

    def row(self, f, r):
        if r < 0:
            return self.up[self.row_base + f * HALO + HALO + r]
        if r >= self.rows:
            return self.down[self.row_base + f * HALO + r - self.rows]
        return self.flow[f * self.rows + r]

    def strips(self, r):
        if 0 <= r < self.rows:
            quarter = self.rows // 4
            q, j = divmod(r, quarter)
            own = self.strip[r]
            left, right = self.left[self.col_base + j], self.right[self.col_base + j]
        else:
            own = strip_of([self.row(f, r) for f in range(3)])
            q = r + HALO if r < 0 else r - self.rows
            at = self.corner(r) + CORNER - 1
            left, right = self.left[at], self.right[at]
        shift = -(8 * (q % 2) + 64 * (q // 2))
        return merge_left(own, roll(left, shift)), merge_right(own, roll(right, shift))


def limited(ahead, behind):
    return jnp.maximum(
        jnp.minimum(ahead, jnp.maximum(behind, 0.0)), jnp.minimum(behind, 0.0)
    )


def face_pair(vel, vel_next, wet):
    a = jnp.where(wet, 0.5 * (vel + vel_next), 0.0)
    size = jnp.abs(a)
    return a, 0.5 * size * (1.0 - size)


def transport_rows(streams, ax_ref, bx_ref, ay_ref, by_ref, first, last):
    states = []
    for load, _, _ in streams:
        before, here, after = load(first - 2), load(first - 1), load(first)
        states.append((here, after, limited(after - here, here - before), after - here, None))
    for i in range(first - 1, last):
        for n, (load, store, kind) in enumerate(streams):
            row, nxt, slope, diff, below = states[n]
            far = load(i + 2)
            diff_next = far - nxt
            slope_next = limited(diff_next, diff)
            ay, by = ay_ref[kind, i + 3], by_ref[kind, i + 3]
            positive = ay >= 0.0
            above = ay * jnp.where(positive, row, nxt) + by * jnp.where(positive, slope, slope_next)
            if below is not None:
                ax, bx = ax_ref[kind, i + 2], bx_ref[kind, i + 2]
                east = roll(row, -1)
                dx = east - row
                sx = limited(dx, roll(dx, 1))
                sx_east = roll(sx, -1)
                pos = ax >= 0.0
                fx = ax * jnp.where(pos, row, east) + bx * jnp.where(pos, sx, sx_east)
                store(i, row - (fx - roll(fx, 1)) - (above - below))
            states[n] = (nxt, far, slope_next, diff_next, above)


def select_lanes(moves):
    parts = []
    source = lax.broadcasted_iota(jnp.int32, (LANES, LANES), 0)
    target = lax.broadcasted_iota(jnp.int32, (LANES, LANES), 1)
    for f, d in moves:
        parts.append(jnp.where(source == GROUP * f + target % GROUP + d, 1.0, 0.0))
    return jnp.concatenate(parts, axis=1)


def exact_dot(a, b):
    return jnp.dot(a, b, precision=lax.Precision.HIGHEST, preferred_element_type=F32)


def transport_kernel(
    place_ref,
    x_ref,
    strip_ref,
    flow_ref,
    fstrip_ref,
    up_ref,
    down_ref,
    left_ref,
    right_ref,
    *refs,
    first_row,
):
    *outs, ext_ref, ax_ref, bx_ref, ay_ref, by_ref, first_ref, moved_ref, edge_ref, spread_ref, main_ref, shift_ref = refs
    count, rows = x_ref.shape[0], x_ref.shape[1] // SUB
    half = rows // 2
    span = moved_ref.shape[1]
    place = place_ref[0]
    level = level_ids().astype(F32)
    flow = Flow(flow_ref, fstrip_ref, up_ref, down_ref, left_ref, right_ref)

    for q in range(-HALO, span + HALO):
        at = pl.ds((q + HALO) * SUB, SUB)
        main_ref[at, :] = flow.row(0, first_row + q)
        left, right = flow.strips(first_row + q)
        edge_ref[0, at, :] = left
        edge_ref[1, at, :] = right
    shift_east = jnp.where(
        lax.broadcasted_iota(jnp.int32, (LANES, LANES), 0)
        == lax.broadcasted_iota(jnp.int32, (LANES, LANES), 1) + 1,
        1.0,
        0.0,
    )
    shift_ref[...] = exact_dot(main_ref[...], shift_east)
    moves = select_lanes(((0, 0), (0, 1), (1, 0), (2, 0), (2, 1)))
    for side in range(2):
        spread_ref[side] = exact_dot(edge_ref[side], moves)

    previous = None
    for q in range(-HALO, span + HALO):
        at = pl.ds((q + HALO) * SUB, SUB)
        aux = flow.row(2, first_row + q)
        wide = lambda v, i: jnp.broadcast_to(v[i : i + 1, :], (SUB, LANES))
        kinds = [(main_ref[at, :], shift_ref[at, :], flow.row(1, first_row + q), wide(aux, 0), wide(aux, 2))]
        for side in range(2):
            east, east_next, north, tally, tally_next = (
                spread_ref[side, at, LANES * n : LANES * (n + 1)] for n in range(5)
            )
            tally, tally_next = wide(tally, 0), wide(tally_next, 0)
            kinds.append((east, east_next, north, tally, jnp.minimum(tally, tally_next)))
        for kind, (east, east_next, north, tally, pair) in enumerate(kinds):
            if -2 <= q < span + 2:
                ax_ref[kind, q + 2], bx_ref[kind, q + 2] = face_pair(east, east_next, level < pair)
            if previous is not None and -3 <= q - 1 < span + 2:
                below, depth = previous[kind]
                ay_ref[kind, q + 2], by_ref[kind, q + 2] = face_pair(
                    below, north, level < jnp.minimum(depth, tally)
                )
        previous = [(k[2], k[3]) for k in kinds]

    for q in range(-HALO, span + HALO):
        r = first_row + q
        if r < 0 or r >= rows:
            src = up_ref if r < 0 else down_ref
            j = r + HALO if r < 0 else r - rows
            fields = [src[t * HALO + j] for t in range(count)]
            own = strip_of(fields)
            left, right = left_ref[flow.corner(r) + j % 2], right_ref[flow.corner(r) + j % 2]
            swap = j >= 2
        else:
            fields = [x_ref[t, pl.ds(r, SUB, stride=rows), :] for t in range(count)]
            own = strip_ref[r]
            left, right = left_ref[r % half], right_ref[r % half]
            swap = r >= half
        if swap:
            left, right = roll(left, -8), roll(right, -8)
        fields += [merge_left(own, left), merge_right(own, right)]
        for t, value in enumerate(fields):
            ext_ref[t, HALO + q] = value

    def some(c, carry):
        places = [c * TOGETHER + n for n in range(TOGETHER)]
        kinds = [jnp.maximum(p - (count - 1), 0) for p in places]
        transport_rows(
            [
                (
                    lambda i, p=p: ext_ref[p, HALO + i],
                    lambda i, value, n=n: first_ref.__setitem__((n, i + 2), value),
                    kinds[n],
                )
                for n, p in enumerate(places)
            ],
            ax_ref, bx_ref, ay_ref, by_ref, -2, span + 2,
        )
        transport_rows(
            [
                (
                    lambda i, n=n: first_ref[n, 2 + i],
                    lambda i, value, p=p: moved_ref.__setitem__((p, i), value),
                    kinds[n],
                )
                for n, p in enumerate(places)
            ],
            ax_ref, bx_ref, ay_ref, by_ref, 0, span,
        )
        return carry

    lax.fori_loop(0, (count + 2) // TOGETHER, some, 0)

    lane = lane_ids()
    edge = (lane < 4) | (lane >= LANES - 4)
    from_right = (lane % GROUP >= 4) & (lane % GROUP < 8)
    share = span // len(outs)
    for k, out_ref in enumerate(outs):
        base = (place ^ k) * share
        for r in range(share):
            joined = jnp.where(from_right, moved_ref[count + 1, base + r], moved_ref[count, base + r])
            for t in range(count):
                out_ref[t * share + r] = jnp.where(
                    edge, roll(joined, -(GROUP * t + 8)), moved_ref[t, base + r]
                )


def transport(place, shards, x, strip, flow_parts, first_row, span):
    count = x.shape[0]
    vmem = pl.BlockSpec(memory_space=pltpu.VMEM)
    tile = lambda *n: pltpu.VMEM(n + (SUB, LANES), F32)
    flat = lambda *n: pltpu.VMEM(n, F32)
    args = (x, strip) + flow_parts
    wide = (span + 2 * HALO) * SUB
    return pl.pallas_call(
        functools.partial(transport_kernel, first_row=first_row),
        in_specs=[pl.BlockSpec(memory_space=pltpu.SMEM)] + [vmem] * len(args),
        out_shape=tuple(
            jax.ShapeDtypeStruct((count * span // shards, SUB, LANES), F32) for _ in range(shards)
        ),
        scratch_shapes=[
            tile(count + 2, span + 2 * HALO),
            tile(3, span + 4),
            tile(3, span + 4),
            tile(3, span + 5),
            tile(3, span + 5),
            tile(TOGETHER, span + 4),
            tile(count + 2, span),
            flat(2, wide, LANES),
            flat(2, wide, 5 * LANES),
            flat(wide, LANES),
            flat(wide, LANES),
        ],
        compiler_params=grant(20),
        name="transport",
    )(place, *args)


def react_kernel(place_ref, table_ref, pace_ref, uptake_ref, surface_ref, tally_ref, *refs, first_row):
    shards = (len(refs) - 3) // 2
    ins, outs = refs[:shards], refs[shards : 2 * shards]
    light_ref, wet_ref, heat_ref = refs[2 * shards :]
    total = pace_ref.shape[0]
    count = total // shards
    share = ins[0].shape[0] // count
    place = place_ref[0]
    level = level_ids()

    for r in range(share):
        row = first_row + place * share + r
        tally = jnp.broadcast_to(tally_ref[pl.ds(row, 1), :], (SUB, LANES))
        surface = surface_ref[row]
        wet = jnp.where(level < tally, 1.0, 0.0)
        absorbed = jnp.zeros((SUB, LANES), F32)
        for k, ref in enumerate(ins):
            for t in range(count):
                absorbed = absorbed + uptake_ref[(place ^ k) * count + t] * jnp.abs(ref[t * share + r])
        layer = (COLUMN_DEPTH / SUB) * (WATER_ABSORB + absorbed) * wet
        total_depth = jnp.where(level >= 1, pltpu.roll(layer, 1, 0), 0.0)
        for shift in (1, 2, 4):
            total_depth = total_depth + jnp.where(
                level >= shift, pltpu.roll(total_depth, shift, 0), 0.0
            )
        top = surface * jnp.exp(-total_depth)
        heat_ref[pl.ds(r * SUB, SUB), :] = top * (1.0 - jnp.exp(-layer))
        light_ref[r] = REACT_STEP * wet * (top / (top + HALF_LIGHT))
        wet_ref[r] = REACT_STEP * wet

    block = 4
    for k, out_ref in enumerate(outs):
        for m0 in range(0, count, block):
            dest = [(place ^ k) * count + m0 + j for j in range(block)]
            acc = [[None] * share for _ in range(block)]
            for kk, ref in enumerate(ins):
                for t in range(count):
                    n = (place ^ kk) * count + t
                    values = [ref[t * share + r] for r in range(share)]
                    for j in range(block):
                        c = table_ref[dest[j], n]
                        for r in range(share):
                            term = c * values[r]
                            acc[j][r] = term if acc[j][r] is None else acc[j][r] + term
            for j in range(block):
                pace = pace_ref[dest[j]]
                for r in range(share):
                    own = ins[k][(m0 + j) * share + r]
                    out_ref[(m0 + j) * share + r] = (
                        own + wet_ref[r] * acc[j][r] + pace * (light_ref[r] * own)
                    )
        own_levels = SUB // shards
        out_ref[count * share] = jnp.concatenate(
            [
                heat_ref[pl.ds((place ^ k) * own_levels + q, share, stride=SUB), :]
                for q in range(own_levels)
            ],
            axis=0,
        )


def react(place, table, pace, uptake, surface, tally, blocks, first_row):
    shards = len(blocks)
    share = blocks[0].shape[0] // (pace.shape[0] // shards)
    smem = pl.BlockSpec(memory_space=pltpu.SMEM)
    vmem = pl.BlockSpec(memory_space=pltpu.VMEM)
    assert share * (SUB // shards) == SUB
    return pl.pallas_call(
        functools.partial(react_kernel, first_row=first_row),
        in_specs=[smem] * 5 + [vmem] * (1 + shards),
        out_shape=tuple(
            jax.ShapeDtypeStruct((b.shape[0] + 1, SUB, LANES), F32) for b in blocks
        ),
        scratch_shapes=[
            pltpu.VMEM((share, SUB, LANES), F32),
            pltpu.VMEM((share, SUB, LANES), F32),
            pltpu.VMEM((share * SUB, LANES), F32),
        ],
        compiler_params=grant(8),
        name="react",
    )(place, table, pace, uptake, surface, tally, *blocks)


def finish_kernel(place_ref, thermal_ref, *refs, shards):
    ins, (out_ref, temp_ref, cells_ref, heat_ref) = refs[:shards], refs[-4:]
    count, _, span, _ = out_ref.shape
    share = span // shards
    place = place_ref[0]
    own_levels = SUB // shards
    level = level_ids()
    for k, ref in enumerate(ins):
        base = (place ^ k) * share
        for m in range(count):
            for r in range(share):
                at = pl.multiple_of((m * span + base + r) * SUB, SUB)
                cells_ref[pl.ds(at, SUB), :] = ref[m * share + r]
        heat = ref[count * share]
        for q in range(own_levels):
            heat_ref[q, place ^ k] = heat if q == 0 else pltpu.roll(heat, SUB - q * share, 0)
    per_tile = SUB // share
    for b in range(span // SUB):
        for m in range(count):
            for lev in range(SUB):
                start = (m * span + b * SUB) * SUB + lev
                out_ref[m, lev, b * SUB : (b + 1) * SUB, :] = cells_ref[pl.ds(start, SUB, stride=SUB), :]
        for q in range(own_levels):
            heat = heat_ref[q, b * per_tile]
            for n in range(1, per_tile):
                part = pltpu.roll(heat_ref[q, b * per_tile + n], n * share, 0)
                heat = jnp.where(level // share == n, part, heat)
            at = slice(b * SUB, (b + 1) * SUB)
            temp_ref[q, at, :] = thermal_ref[q, at, :] + WARMING_WEIGHT * heat


def finish(place, thermal, blocks, shape, part, parts, before):
    shards = len(blocks)
    count, levels, rows, cols = shape
    own_levels = thermal.shape[0]
    span = rows // parts
    vmem = pl.BlockSpec(memory_space=pltpu.VMEM)
    hold = pl.BlockSpec(memory_space=pl.ANY)
    of_part = lambda *lead: pl.BlockSpec(
        lead + (span, cols), lambda i: (0,) * len(lead) + (part, 0)
    )
    return pl.pallas_call(
        functools.partial(finish_kernel, shards=shards),
        grid=(1,),
        in_specs=[pl.BlockSpec(memory_space=pltpu.SMEM), of_part(own_levels)]
        + [vmem] * shards
        + [hold] * len(before),
        out_specs=(of_part(count, levels), of_part(own_levels)),
        out_shape=(jax.ShapeDtypeStruct(shape, F32), jax.ShapeDtypeStruct(thermal.shape, F32)),
        input_output_aliases={2 + shards + i: i for i in range(len(before))},
        scratch_shapes=[
            pltpu.VMEM((count * span * SUB, LANES), F32),
            pltpu.VMEM((own_levels, shards, SUB, LANES), F32),
        ],
        compiler_params=grant(12),
        name="finish",
    )(place, thermal, *blocks, *before)


def level_sum(x):
    for shift in (4, 2, 1):
        x = x + pltpu.roll(x, shift, 0)
    return x


def momentum_kernel(
    place_ref,
    coriolis_ref,
    inside_ref,
    flow_ref,
    strip_ref,
    fup_ref,
    fdown_ref,
    colsl_ref,
    colsr_ref,
    east_ref,
    north_ref,
    height_ref,
    a_ref,
    b_ref,
    c_ref,
):
    rows = height_ref.shape[0]
    own_levels = east_ref.shape[0] // rows
    place = place_ref[0]
    lane = lane_ids()
    level = level_ids().astype(F32)
    flow = Flow(flow_ref, strip_ref, fup_ref, fdown_ref, colsl_ref, colsr_ref)
    for r in range(-2, rows + 2):
        east, north, aux = (flow.row(f, r) for f in range(3))
        left, right = flow.strips(r)
        both = [
            jnp.where(lane < GROUP, roll(left, -GROUP * f), roll(right, GROUP - GROUP * f))
            for f in range(3)
        ]
        for p, (u, v, w) in enumerate(((east, north, aux), both)):
            wet = jnp.where(level < over_levels(w), 1.0, 0.0)
            h = jnp.broadcast_to(w[1:2, :], (SUB, LANES))
            for f, value in enumerate((u, v, h, wet)):
                a_ref[p, f, r + 2] = value

    def substep(src, offset, put, first, last):
        for p in range(2):
            for i in range(first, last):
                g = lambda f, d: src[p, f, i + offset + d]
                u, v, h = g(0, 0), g(1, 0), g(2, 0)
                un, us, vn, vs, hn, hs = g(0, 1), g(0, -1), g(1, 1), g(1, -1), g(2, 1), g(2, -1)
                wet = a_ref[p, 3, i + 2]
                cor = coriolis_ref[i + 2]
                ue, uw, ve, vw, he, hw = (
                    roll(u, -1), roll(u, 1), roll(v, -1), roll(v, 1), roll(h, -1), roll(h, 1),
                )
                div = level_sum(0.5 * (ue - uw) + 0.5 * (vn - vs))
                nu = wet * (
                    u
                    + TIME_STEP
                    * (
                        cor * v
                        - GRAVITY * (0.5 * (he - hw))
                        + VISCOSITY * (un + us + ue + uw - 4.0 * u)
                        - BOTTOM_DRAG * u
                    )
                )
                nv = wet * (
                    v
                    + TIME_STEP
                    * (
                        -cor * u
                        - GRAVITY * (0.5 * (hn - hs))
                        + VISCOSITY * (vn + vs + ve + vw - 4.0 * v)
                        - BOTTOM_DRAG * v
                    )
                )
                nh = h - TIME_STEP * DEPTH_SCALE * div
                put(p, i, nu, nv, nh)

    def put_first(p, i, nu, nv, nh):
        inside = inside_ref[i + 2]
        for f, value in enumerate((nu, nv, nh * inside)):
            b_ref[p, f, i + 1] = value

    def put_second(p, i, nu, nv, nh):
        for f, value in enumerate((nu, nv, nh)):
            c_ref[p, f, pl.ds(i * SUB, SUB), :] = value

    substep(a_ref, 2, put_first, -1, rows + 1)
    substep(b_ref, 1, put_second, 0, rows)

    def joined(f, start):
        lane8 = lax.broadcasted_iota(jnp.int32, (SUB, LANES), 1)
        main = c_ref[0, f, pl.ds(start, SUB, stride=SUB), :]
        edge = c_ref[1, f, pl.ds(start, SUB, stride=SUB), :]
        out = jnp.where(lane8 < 2, roll(edge, -8), main)
        return jnp.where(lane8 >= LANES - 2, roll(edge, LANES - 2 - (GROUP + 6)), out)

    for j in range(rows // SUB):
        for q in range(own_levels):
            lev = place * own_levels + q
            dst = q * rows + j * SUB
            east_ref[dst : dst + SUB, :] = joined(0, j * SUB * SUB + lev)
            north_ref[dst : dst + SUB, :] = joined(1, j * SUB * SUB + lev)
        height_ref[j * SUB : (j + 1) * SUB, :] = joined(2, j * SUB * SUB)


def momentum(place, coriolis, inside, flow_parts, rows, own_levels):
    vmem = pl.BlockSpec(memory_space=pltpu.VMEM)
    args = (coriolis, inside) + flow_parts
    return pl.pallas_call(
        momentum_kernel,
        in_specs=[pl.BlockSpec(memory_space=pltpu.SMEM)] * 3 + [vmem] * len(flow_parts),
        out_shape=(
            jax.ShapeDtypeStruct((own_levels * rows, LANES), F32),
            jax.ShapeDtypeStruct((own_levels * rows, LANES), F32),
            jax.ShapeDtypeStruct((rows, LANES), F32),
        ),
        scratch_shapes=[
            pltpu.VMEM((2, 4, rows + 4, SUB, LANES), F32),
            pltpu.VMEM((2, 3, rows + 2, SUB, LANES), F32),
            pltpu.VMEM((2, 3, rows * SUB, LANES), F32),
        ],
        compiler_params=grant(12),
        name="momentum",
    )(place, *args)


def to_peer(block, k):
    count = lax.axis_size("trc")
    return lax.ppermute(block, "trc", [(i, i ^ k) for i in range(count)])


def from_lat(block, step):
    count = lax.axis_size("lat")
    return lax.ppermute(
        block, "lat", [(i, i + step) for i in range(count) if 0 <= i + step < count]
    )


def both_sides(block):
    count = lax.axis_size("lon")
    left = lax.ppermute(block, "lon", [(i, (i + 1) % count) for i in range(count)])
    if count == 2:
        return left, left
    return left, lax.ppermute(block, "lon", [(i, (i - 1) % count) for i in range(count)])


def body(
    species_concentrations,
    zonal_velocity_array,
    meridional_velocity_array,
    thermal_anomaly,
    ocean_top_height_grid,
    water_layer_tally,
    species_interaction_table,
    species_production_pace,
    photon_uptake,
):
    count, levels, rows, cols = species_concentrations.shape
    own_levels = zonal_velocity_array.shape[0]
    shards = lax.axis_size("trc")
    assert levels == SUB and cols == LANES and count * GROUP == LANES and shards & (shards - 1) == 0
    trc_place = lax.axis_index("trc")
    place = trc_place.astype(jnp.int32).reshape(1)
    lat_total = rows * lax.axis_size("lat")
    lat_first = lax.axis_index("lat") * rows
    lat_global = (lat_first + jnp.arange(-2, rows + 2)).astype(F32)
    angle = math.pi * ((lat_global + 0.5) / lat_total - 0.5)
    coriolis = CORIOLIS_SCALE * jnp.sin(angle)
    surface = 1.0 + jnp.cos(angle[2:-2])
    inside = ((lat_global >= 0) & (lat_global < lat_total)).astype(F32)

    x = species_concentrations.reshape(count, levels * rows, cols)
    own = jnp.stack([zonal_velocity_array, meridional_velocity_array]).reshape(
        2, own_levels * rows, cols
    )
    peers = [to_peer(own, k) for k in range(1, shards)]
    strip, *messages = pack_tracers(x)
    flow, fstrip, fcols, fup, fdown = pack_flow(
        place, own, peers, water_layer_tally, ocean_top_height_grid, messages
    )
    up_in, down_in = from_lat(fup, 1), from_lat(fdown, -1)
    left_in, right_in = both_sides(pack_edges(up_in, down_in, fcols))
    flow_parts = (flow, fstrip, up_in, down_in, left_in, right_in)
    span = rows // PARTS
    blocks = []
    for part in range(PARTS):
        moved = transport(place, shards, x, strip, flow_parts, part * span, span)
        blocks.append([moved[0]] + [to_peer(moved[k], k) for k in range(1, shards)])
    back = []
    for part in range(PARTS):
        reacted = react(
            place,
            species_interaction_table,
            species_production_pace,
            photon_uptake,
            surface,
            water_layer_tally,
            blocks[part],
            part * span,
        )
        back.append([reacted[0]] + [to_peer(reacted[k], k) for k in range(1, shards)])
    late, back[-1][0] = lax.optimization_barrier((place, back[-1][0]))
    east_out, north_out, height_out = momentum(late, coriolis, inside, flow_parts, rows, own_levels)
    done = ()
    for part in range(PARTS):
        done = finish(
            place, thermal_anomaly, back[part], species_concentrations.shape, part, PARTS, done
        )
    updated, temperature = done
    vel = (own_levels, rows, cols)
    return (
        updated,
        east_out.reshape(vel),
        north_out.reshape(vel),
        temperature,
        height_out,
    )


def solution(mesh):
    return jax.shard_map(
        body,
        mesh=mesh,
        in_specs=(
            P("trc", None, "lat", "lon"),
            P("trc", "lat", "lon"),
            P("trc", "lat", "lon"),
            P("trc", "lat", "lon"),
            P("lat", "lon"),
            P("lat", "lon"),
            P(),
            P(),
            P(),
        ),
        out_specs=(
            P("trc", None, "lat", "lon"),
            P("trc", "lat", "lon"),
            P("trc", "lat", "lon"),
            P("trc", "lat", "lon"),
            P("lat", "lon"),
        ),
        check_vma=False,
    )
```

```python
import functools
import math

import jax
import jax.numpy as jnp
from jax import lax
from jax.experimental import pallas as pl
from jax.experimental.pallas import tpu as pltpu
from jax.sharding import PartitionSpec as P

TIME_STEP = 0.1
GRAVITY = 1.0
VISCOSITY = 0.2
BOTTOM_DRAG = 0.05
DEPTH_SCALE = 0.5
CORIOLIS_SCALE = 0.5
COLUMN_DEPTH = 2.0
WATER_ABSORB = 0.2
HALF_LIGHT = 0.5
REACT_STEP = 0.1
WARMING_WEIGHT = 1.0

SUB = 8
LANES = 128
HALO = 4
CORNER = 3
GROUP = 16
F32 = jnp.float32
TOGETHER = 2


def lane_ids():
    return lax.broadcasted_iota(jnp.int32, (SUB, LANES), 1)


def level_ids():
    return lax.broadcasted_iota(jnp.int32, (SUB, LANES), 0)


def roll(x, shift):
    shift = shift % LANES
    return x if shift == 0 else pltpu.roll(x, shift, 1)


def strip_of(rows):
    lane = lane_ids()
    out = None
    for t, value in enumerate(rows):
        rolled = roll(value, GROUP * t + GROUP // 2)
        if out is None:
            out = rolled
        else:
            out = jnp.where(lane // GROUP == t, rolled, out)
    return out


def middle_mask():
    lane = lane_ids() % GROUP
    return (lane >= 4) & (lane < 12)


def pair_up(first, second):
    return jnp.where(middle_mask(), first, roll(second, 8))


def quad_up(a, b, c, d):
    return jnp.where(lane_ids() < 64, pair_up(a, b), roll(pair_up(c, d), 64))


def merge_left(own, got):
    lane = lane_ids() % GROUP
    return jnp.where((lane >= 4) & (lane < 8), got, own)


def merge_right(own, got):
    lane = lane_ids() % GROUP
    return jnp.where((lane >= 8) & (lane < 12), got, own)


def over_levels(row):
    return jnp.broadcast_to(row[0:1, :], (SUB, LANES))


def grant(mib):
    return pltpu.CompilerParams(vmem_limit_bytes=mib << 20)


def pack_tracers_kernel(x_ref, strip_ref, up_ref, down_ref, cols_ref):
    count, rows = x_ref.shape[0], x_ref.shape[1] // SUB
    half = rows // 2

    def row_strip(r):
        return strip_of([x_ref[t, pl.ds(r, SUB, stride=rows), :] for t in range(count)])

    for r in range(half):
        low, high = row_strip(r), row_strip(r + half)
        strip_ref[r] = low
        strip_ref[r + half] = high
        cols_ref[r] = pair_up(low, high)
    for t in range(count):
        for j in range(HALO):
            down_ref[t * HALO + j] = x_ref[t, pl.ds(j, SUB, stride=rows), :]
            up_ref[t * HALO + j] = x_ref[t, pl.ds(rows - HALO + j, SUB, stride=rows), :]


def pack_tracers(x):
    count, rows = x.shape[0], x.shape[1] // SUB
    tile = lambda n: jax.ShapeDtypeStruct((n, SUB, LANES), F32)
    return pl.pallas_call(
        pack_tracers_kernel,
        out_shape=(
            tile(rows),
            tile(count * HALO),
            tile(count * HALO),
            tile(rows // 2),
        ),
        compiler_params=grant(8),
        name="pack_tracers",
    )(x)


def pack_flow_kernel(place_ref, own_ref, *refs):
    peers, rest = refs[:-11], refs[-11:]
    tally_ref, height_ref, tup_ref, tdown_ref, tcols_ref = rest[:5]
    flow_ref, strip_ref, cols_ref, up_ref, down_ref, all_ref = rest[5:]
    rows = tally_ref.shape[0]
    span = own_ref.shape[1]
    place = place_ref[0]
    for k, ref in enumerate((own_ref,) + tuple(peers)):
        base = pl.multiple_of((place ^ k) * span, SUB)
        for f in range(2):
            all_ref[f, pl.ds(base, span), :] = ref[f]
    for src, dst in ((tup_ref, up_ref), (tdown_ref, down_ref), (tcols_ref, cols_ref)):
        dst[0 : src.shape[0]] = src[...]
    nrow, ncol = tup_ref.shape[0], tcols_ref.shape[0]
    level = level_ids()
    tally_all = tally_ref[...].astype(F32)
    pair_all = jnp.minimum(tally_all, pltpu.roll(tally_all, LANES - 1, 1))
    wide = lambda v, r: jnp.broadcast_to(v[r : r + 1, :], (SUB, LANES))
    for r in range(rows):
        tally, height, pair = wide(tally_all, r), wide(height_ref, r), wide(pair_all, r)
        wet = level.astype(F32) < tally
        east = jnp.where(wet, all_ref[0, pl.ds(r, SUB, stride=rows), :], 0.0)
        north = jnp.where(wet, all_ref[1, pl.ds(r, SUB, stride=rows), :], 0.0)
        aux = jnp.where(level == 0, tally, jnp.where(level == 1, height, pair))
        for f, value in enumerate((east, north, aux)):
            flow_ref[f * rows + r] = value
            if r < HALO:
                down_ref[nrow + f * HALO + r] = value
            if r >= rows - HALO:
                up_ref[nrow + f * HALO + r - (rows - HALO)] = value
        strip_ref[r] = strip_of([east, north, aux])
    quarter = rows // 4
    for r in range(quarter):
        cols_ref[ncol + r] = quad_up(*[strip_ref[r + quarter * q] for q in range(4)])


def pack_flow(place, own, peers, tally, height, messages):
    rows = tally.shape[0]
    tile = lambda n: jax.ShapeDtypeStruct((n, SUB, LANES), F32)
    vmem = pl.BlockSpec(memory_space=pltpu.VMEM)
    tup, tdown, tcols = messages
    return pl.pallas_call(
        pack_flow_kernel,
        in_specs=[pl.BlockSpec(memory_space=pltpu.SMEM)] + [vmem] * (3 + len(peers) + len(messages)),
        out_shape=(
            tile(3 * rows),
            tile(rows),
            tile(tcols.shape[0] + rows // 4),
            tile(tup.shape[0] + 3 * HALO),
            tile(tdown.shape[0] + 3 * HALO),
        ),
        scratch_shapes=[pltpu.VMEM((2, SUB * rows, LANES), F32)],
        compiler_params=grant(8),
        name="pack_flow",
    )(place, own, *peers, tally, height, *messages)


def pack_edges_kernel(up_ref, down_ref, out_ref):
    count = up_ref.shape[0] // HALO - 3
    for n, ref in enumerate((up_ref, down_ref)):
        row = lambda f, j: ref[f * HALO + j]
        tracers = [strip_of([row(t, j) for t in range(count)]) for j in range(HALO)]
        flows = [strip_of([row(count + f, j) for f in range(3)]) for j in range(HALO)]
        base = n * CORNER
        for j in range(2):
            out_ref[base + j] = pair_up(tracers[j], tracers[j + 2])
        out_ref[base + 2] = quad_up(*flows)


def pack_edges(up, down):
    return pl.pallas_call(
        pack_edges_kernel,
        out_shape=jax.ShapeDtypeStruct((2 * CORNER, SUB, LANES), F32),
        compiler_params=grant(8),
        name="pack_edges",
    )(up, down)


class Flow:
    def __init__(self, flow_ref, strip_ref, left_ref, right_ref, outer=()):
        self.flow, self.strip = flow_ref, strip_ref
        self.left, self.right = left_ref, right_ref
        self.rows = strip_ref.shape[0]
        self.col_base = left_ref.shape[0] - self.rows // 4
        if outer:
            self.up, self.down, self.corner_left, self.corner_right = outer
            self.row_base = self.up.shape[0] - 3 * HALO

    def corner(self, r):
        return 0 if r < 0 else CORNER

    def row(self, f, r):
        if r < 0:
            return self.up[self.row_base + f * HALO + HALO + r]
        if r >= self.rows:
            return self.down[self.row_base + f * HALO + r - self.rows]
        return self.flow[f * self.rows + r]

    def strips(self, r):
        if 0 <= r < self.rows:
            quarter = self.rows // 4
            q, j = divmod(r, quarter)
            own = self.strip[r]
            left, right = self.left[self.col_base + j], self.right[self.col_base + j]
        else:
            own = strip_of([self.row(f, r) for f in range(3)])
            q = r + HALO if r < 0 else r - self.rows
            at = self.corner(r) + CORNER - 1
            left, right = self.corner_left[at], self.corner_right[at]
        shift = -(8 * (q % 2) + 64 * (q // 2))
        return merge_left(own, roll(left, shift)), merge_right(own, roll(right, shift))


def limited(ahead, behind):
    return jnp.maximum(
        jnp.minimum(ahead, jnp.maximum(behind, 0.0)), jnp.minimum(behind, 0.0)
    )


def face_pair(vel, vel_next, wet):
    a = jnp.where(wet, 0.5 * (vel + vel_next), 0.0)
    size = jnp.abs(a)
    return a, 0.5 * size * (1.0 - size)


def transport_rows(streams, ax_ref, bx_ref, ay_ref, by_ref, first, last):
    states = []
    for load, *_ in streams:
        before, here, after = load(first - 2), load(first - 1), load(first)
        states.append((here, after, limited(after - here, here - before), after - here, None))
    for i in range(first - 1, last):
        for n, (load, store, kind, xo, yo) in enumerate(streams):
            row, nxt, slope, diff, below = states[n]
            far = load(i + 2)
            diff_next = far - nxt
            slope_next = limited(diff_next, diff)
            ay, by = ay_ref[kind, yo + i], by_ref[kind, yo + i]
            positive = ay >= 0.0
            above = ay * jnp.where(positive, row, nxt) + by * jnp.where(positive, slope, slope_next)
            if below is not None:
                ax, bx = ax_ref[kind, xo + i], bx_ref[kind, xo + i]
                east = roll(row, -1)
                dx = east - row
                sx = limited(dx, roll(dx, 1))
                sx_east = roll(sx, -1)
                pos = ax >= 0.0
                fx = ax * jnp.where(pos, row, east) + bx * jnp.where(pos, sx, sx_east)
                store(i, row - (fx - roll(fx, 1)) - (above - below))
            states[n] = (nxt, far, slope_next, diff_next, above)


def select_lanes(moves):
    parts = []
    source = lax.broadcasted_iota(jnp.int32, (LANES, LANES), 0)
    target = lax.broadcasted_iota(jnp.int32, (LANES, LANES), 1)
    for f, d in moves:
        parts.append(jnp.where(source == GROUP * f + target % GROUP + d, 1.0, 0.0))
    return jnp.concatenate(parts, axis=1)


def exact_dot(a, b):
    return jnp.dot(a, b, precision=lax.Precision.HIGHEST, preferred_element_type=F32)


def transport_kernel(
    place_ref, x_ref, strip_ref, flow_ref, fstrip_ref, left_ref, right_ref, *refs, firsts, span, shards
):
    outer, outs, scratch = refs[: -shards - 11], refs[-shards - 11 : -11], refs[-11:]
    ext_ref, ax_ref, bx_ref, ay_ref, by_ref, first_ref, moved_ref, edge_ref, spread_ref, main_ref, shift_ref = scratch
    count, rows = x_ref.shape[0], x_ref.shape[1] // SUB
    half = rows // 2
    place = place_ref[0]
    level = level_ids().astype(F32)
    flow = Flow(flow_ref, fstrip_ref, left_ref, right_ref, outer)
    wide = span + 2 * HALO
    every = [(n, q, first + q) for n, first in enumerate(firsts) for q in range(-HALO, span + HALO)]
    tile_at = lambda n, q: pl.ds((n * wide + q + HALO) * SUB, SUB)

    for n, q, r in every:
        main_ref[tile_at(n, q), :] = flow.row(0, r)
        left, right = flow.strips(r)
        edge_ref[0, tile_at(n, q), :] = left
        edge_ref[1, tile_at(n, q), :] = right
    shift_east = jnp.where(
        lax.broadcasted_iota(jnp.int32, (LANES, LANES), 0)
        == lax.broadcasted_iota(jnp.int32, (LANES, LANES), 1) + 1,
        1.0,
        0.0,
    )
    shift_ref[...] = exact_dot(main_ref[...], shift_east)
    moves = select_lanes(((0, 0), (0, 1), (1, 0), (2, 0), (2, 1)))
    for side in range(2):
        spread_ref[side] = exact_dot(edge_ref[side], moves)

    previous = None
    for n, q, r in every:
        at = tile_at(n, q)
        aux = flow.row(2, r)
        spread = lambda v, i: jnp.broadcast_to(v[i : i + 1, :], (SUB, LANES))
        kinds = [(main_ref[at, :], shift_ref[at, :], flow.row(1, r), spread(aux, 0), spread(aux, 2))]
        for side in range(2):
            east, east_next, north, tally, tally_next = (
                spread_ref[side, at, LANES * j : LANES * (j + 1)] for j in range(5)
            )
            tally, tally_next = spread(tally, 0), spread(tally_next, 0)
            kinds.append((east, east_next, north, tally, jnp.minimum(tally, tally_next)))
        for kind, (east, east_next, north, tally, pair) in enumerate(kinds):
            if -2 <= q < span + 2:
                i = n * (span + 4) + q + 2
                ax_ref[kind, i], bx_ref[kind, i] = face_pair(east, east_next, level < pair)
            if -2 <= q < span + 3:
                i = n * (span + 5) + q + 2
                below, depth = previous[kind]
                ay_ref[kind, i], by_ref[kind, i] = face_pair(
                    below, north, level < jnp.minimum(depth, tally)
                )
        previous = [(k[2], k[3]) for k in kinds]

    for n, q, r in every:
        if r < 0 or r >= rows:
            src = flow.up if r < 0 else flow.down
            j = r + HALO if r < 0 else r - rows
            fields = [src[t * HALO + j] for t in range(count)]
            own = strip_of(fields)
            at = flow.corner(r) + j % 2
            left, right = flow.corner_left[at], flow.corner_right[at]
            swap = j >= 2
        else:
            fields = [x_ref[t, pl.ds(r, SUB, stride=rows), :] for t in range(count)]
            own = strip_ref[r]
            left, right = left_ref[r % half], right_ref[r % half]
            swap = r >= half
        if swap:
            left, right = roll(left, -8), roll(right, -8)
        fields += [merge_left(own, left), merge_right(own, right)]
        for t, value in enumerate(fields):
            ext_ref[t, n * wide + HALO + q] = value

    def some(c, carry):
        before, after = [], []
        for j in range(TOGETHER):
            p = c * TOGETHER + j
            kind = jnp.maximum(p - (count - 1), 0)
            for n in range(len(firsts)):
                xo, yo = n * (span + 4) + 2, n * (span + 5) + 3

                def load_start(i, p=p, n=n):
                    return ext_ref[p, n * wide + HALO + i]

                def store_first(i, value, j=j, xo=xo):
                    first_ref[j, xo + i] = value

                def load_first(i, j=j, xo=xo):
                    return first_ref[j, xo + i]

                def store_moved(i, value, p=p, n=n):
                    moved_ref[p, n * span + i] = value

                before.append((load_start, store_first, kind, xo, yo))
                after.append((load_first, store_moved, kind, xo, yo))
        transport_rows(before, ax_ref, bx_ref, ay_ref, by_ref, -2, span + 2)
        transport_rows(after, ax_ref, bx_ref, ay_ref, by_ref, 0, span)
        return carry

    lax.fori_loop(0, (count + 2) // TOGETHER, some, 0)

    lane = lane_ids()
    edge = (lane < 4) | (lane >= LANES - 4)
    from_right = (lane % GROUP >= 4) & (lane % GROUP < 8)
    share = span * len(firsts) // len(outs)
    for k, out_ref in enumerate(outs):
        base = (place ^ k) * share
        for r in range(share):
            joined = jnp.where(from_right, moved_ref[count + 1, base + r], moved_ref[count, base + r])
            for t in range(count):
                out_ref[t * share + r] = jnp.where(
                    edge, roll(joined, -(GROUP * t + 8)), moved_ref[t, base + r]
                )


def transport(place, shards, x, strip, flow_parts, firsts, span):
    count = x.shape[0]
    vmem = pl.BlockSpec(memory_space=pltpu.VMEM)
    tile = lambda *n: pltpu.VMEM(n + (SUB, LANES), F32)
    flat = lambda *n: pltpu.VMEM(n, F32)
    args = (x, strip) + flow_parts
    pieces = len(firsts)
    wide = (span + 2 * HALO) * pieces
    return pl.pallas_call(
        functools.partial(transport_kernel, firsts=firsts, span=span, shards=shards),
        in_specs=[pl.BlockSpec(memory_space=pltpu.SMEM)] + [vmem] * len(args),
        out_shape=tuple(
            jax.ShapeDtypeStruct((count * span * pieces // shards, SUB, LANES), F32)
            for _ in range(shards)
        ),
        scratch_shapes=[
            tile(count + 2, wide),
            tile(3, (span + 4) * pieces),
            tile(3, (span + 4) * pieces),
            tile(3, (span + 5) * pieces),
            tile(3, (span + 5) * pieces),
            tile(TOGETHER, (span + 4) * pieces),
            tile(count + 2, span * pieces),
            flat(2, wide * SUB, LANES),
            flat(2, wide * SUB, 5 * LANES),
            flat(wide * SUB, LANES),
            flat(wide * SUB, LANES),
        ],
        compiler_params=grant(20),
        name="transport",
    )(place, *args)


def react_kernel(place_ref, table_ref, pace_ref, uptake_ref, surface_ref, tally_ref, *refs, firsts):
    shards = (len(refs) - 3) // 2
    ins, outs = refs[:shards], refs[shards : 2 * shards]
    light_ref, wet_ref, heat_ref = refs[2 * shards :]
    total = pace_ref.shape[0]
    count = total // shards
    share = ins[0].shape[0] // count
    place = place_ref[0]
    level = level_ids()

    for r in range(share):
        at = place * share + r
        span = share * shards // len(firsts)
        row = firsts[0] + at
        for n in range(1, len(firsts)):
            row = jnp.where(at >= n * span, firsts[n] + at - n * span, row)
        tally = jnp.broadcast_to(tally_ref[pl.ds(row, 1), :], (SUB, LANES))
        surface = surface_ref[row]
        wet = jnp.where(level < tally, 1.0, 0.0)
        absorbed = jnp.zeros((SUB, LANES), F32)
        for k, ref in enumerate(ins):
            for t in range(count):
                absorbed = absorbed + uptake_ref[(place ^ k) * count + t] * jnp.abs(ref[t * share + r])
        layer = (COLUMN_DEPTH / SUB) * (WATER_ABSORB + absorbed) * wet
        total_depth = jnp.where(level >= 1, pltpu.roll(layer, 1, 0), 0.0)
        for shift in (1, 2, 4):
            total_depth = total_depth + jnp.where(
                level >= shift, pltpu.roll(total_depth, shift, 0), 0.0
            )
        top = surface * jnp.exp(-total_depth)
        heat_ref[pl.ds(r * SUB, SUB), :] = top * (1.0 - jnp.exp(-layer))
        light_ref[r] = REACT_STEP * wet * (top / (top + HALF_LIGHT))
        wet_ref[r] = REACT_STEP * wet

    block = 4
    for k, out_ref in enumerate(outs):
        for m0 in range(0, count, block):
            dest = [(place ^ k) * count + m0 + j for j in range(block)]
            acc = [[None] * share for _ in range(block)]
            for kk, ref in enumerate(ins):
                for t in range(count):
                    n = (place ^ kk) * count + t
                    values = [ref[t * share + r] for r in range(share)]
                    for j in range(block):
                        c = table_ref[dest[j], n]
                        for r in range(share):
                            term = c * values[r]
                            acc[j][r] = term if acc[j][r] is None else acc[j][r] + term
            for j in range(block):
                pace = pace_ref[dest[j]]
                for r in range(share):
                    own = ins[k][(m0 + j) * share + r]
                    out_ref[(m0 + j) * share + r] = (
                        own + wet_ref[r] * acc[j][r] + pace * (light_ref[r] * own)
                    )
        own_levels = SUB // shards
        out_ref[count * share] = jnp.concatenate(
            [
                heat_ref[pl.ds((place ^ k) * own_levels + q, share, stride=SUB), :]
                for q in range(own_levels)
            ],
            axis=0,
        )


def react(place, table, pace, uptake, surface, tally, blocks, firsts):
    shards = len(blocks)
    share = blocks[0].shape[0] // (pace.shape[0] // shards)
    smem = pl.BlockSpec(memory_space=pltpu.SMEM)
    vmem = pl.BlockSpec(memory_space=pltpu.VMEM)
    assert share * (SUB // shards) == SUB
    return pl.pallas_call(
        functools.partial(react_kernel, firsts=firsts),
        in_specs=[smem] * 5 + [vmem] * (1 + shards),
        out_shape=tuple(
            jax.ShapeDtypeStruct((b.shape[0] + 1, SUB, LANES), F32) for b in blocks
        ),
        scratch_shapes=[
            pltpu.VMEM((share, SUB, LANES), F32),
            pltpu.VMEM((share, SUB, LANES), F32),
            pltpu.VMEM((share * SUB, LANES), F32),
        ],
        compiler_params=grant(8),
        name="react",
    )(place, table, pace, uptake, surface, tally, *blocks)


def finish_kernel(place_ref, thermal_ref, *refs, shards, span):
    ins, (out_ref, temp_ref, cells_ref, heat_ref) = refs[:shards], refs[-4:]
    count = out_ref.shape[0]
    share = span // shards
    own_levels = SUB // shards
    level = level_ids()
    b = pl.program_id(0)

    @pl.when(b == 0)
    def _():
        place = place_ref[0]
        for k, ref in enumerate(ins):
            base = (place ^ k) * share
            for m in range(count):
                for r in range(share):
                    at = pl.multiple_of((m * span + base + r) * SUB, SUB)
                    cells_ref[pl.ds(at, SUB), :] = ref[m * share + r]
            heat = ref[count * share]
            for q in range(own_levels):
                heat_ref[q, place ^ k] = heat if q == 0 else pltpu.roll(heat, SUB - q * share, 0)

    per_tile = SUB // share
    for m in range(count):
        for lev in range(SUB):
            start = b * (SUB * SUB) + (m * span * SUB + lev)
            out_ref[m, lev] = cells_ref[pl.ds(start, SUB, stride=SUB), :]
    for q in range(own_levels):
        heat = heat_ref[q, b * per_tile]
        for n in range(1, per_tile):
            part = pltpu.roll(heat_ref[q, b * per_tile + n], n * share, 0)
            heat = jnp.where(level // share == n, part, heat)
        temp_ref[q] = thermal_ref[q] + WARMING_WEIGHT * heat


def finish(place, thermal, blocks, shape, firsts, span, before):
    shards = len(blocks)
    count, levels, _, cols = shape
    own_levels = thermal.shape[0]
    assert span % SUB == 0 and len(firsts) <= 2 and all(first % SUB == 0 for first in firsts)
    per = span // SUB
    step = per if len(firsts) == 1 else (firsts[1] - firsts[0]) // SUB
    assert len(firsts) == 1 or per == 1
    row_tile = lambda i: firsts[0] // SUB + (i if len(firsts) == 1 else i * step)
    vmem = pl.BlockSpec(memory_space=pltpu.VMEM)
    hold = pl.BlockSpec(memory_space=pl.ANY)
    of_band = lambda *lead: pl.BlockSpec(
        lead + (SUB, cols), lambda i: (0,) * len(lead) + (row_tile(i), 0)
    )
    total = span * len(firsts)
    return pl.pallas_call(
        functools.partial(finish_kernel, shards=shards, span=total),
        grid=(total // SUB,),
        in_specs=[pl.BlockSpec(memory_space=pltpu.SMEM), of_band(own_levels)]
        + [vmem] * shards
        + [hold] * len(before),
        out_specs=(of_band(count, levels), of_band(own_levels)),
        out_shape=(jax.ShapeDtypeStruct(shape, F32), jax.ShapeDtypeStruct(thermal.shape, F32)),
        input_output_aliases={2 + shards + i: i for i in range(len(before))},
        scratch_shapes=[
            pltpu.VMEM((count * total * SUB, LANES), F32),
            pltpu.VMEM((own_levels, shards, SUB, LANES), F32),
        ],
        compiler_params=grant(12),
        name="finish",
    )(place, thermal, *blocks, *before)


def level_sum(x):
    for shift in (4, 2, 1):
        x = x + pltpu.roll(x, shift, 0)
    return x


def momentum_kernel(
    place_ref,
    coriolis_ref,
    inside_ref,
    flow_ref,
    strip_ref,
    left_ref,
    right_ref,
    up_ref,
    down_ref,
    cleft_ref,
    cright_ref,
    east_ref,
    north_ref,
    height_ref,
    a_ref,
    b_ref,
    c_ref,
):
    rows = height_ref.shape[0]
    own_levels = east_ref.shape[0] // rows
    place = place_ref[0]
    lane = lane_ids()
    level = level_ids().astype(F32)
    flow = Flow(flow_ref, strip_ref, left_ref, right_ref, (up_ref, down_ref, cleft_ref, cright_ref))
    for r in range(-2, rows + 2):
        east, north, aux = (flow.row(f, r) for f in range(3))
        left, right = flow.strips(r)
        both = [
            jnp.where(lane < GROUP, roll(left, -GROUP * f), roll(right, GROUP - GROUP * f))
            for f in range(3)
        ]
        for p, (u, v, w) in enumerate(((east, north, aux), both)):
            wet = jnp.where(level < over_levels(w), 1.0, 0.0)
            h = jnp.broadcast_to(w[1:2, :], (SUB, LANES))
            for f, value in enumerate((u, v, h, wet)):
                a_ref[p, f, r + 2] = value

    def substep(src, offset, put, first, last):
        for p in range(2):
            for i in range(first, last):
                g = lambda f, d: src[p, f, i + offset + d]
                u, v, h = g(0, 0), g(1, 0), g(2, 0)
                un, us, vn, vs, hn, hs = g(0, 1), g(0, -1), g(1, 1), g(1, -1), g(2, 1), g(2, -1)
                wet = a_ref[p, 3, i + 2]
                cor = coriolis_ref[i + 2]
                ue, uw, ve, vw, he, hw = (
                    roll(u, -1), roll(u, 1), roll(v, -1), roll(v, 1), roll(h, -1), roll(h, 1),
                )
                div = level_sum(0.5 * (ue - uw) + 0.5 * (vn - vs))
                nu = wet * (
                    u
                    + TIME_STEP
                    * (
                        cor * v
                        - GRAVITY * (0.5 * (he - hw))
                        + VISCOSITY * (un + us + ue + uw - 4.0 * u)
                        - BOTTOM_DRAG * u
                    )
                )
                nv = wet * (
                    v
                    + TIME_STEP
                    * (
                        -cor * u
                        - GRAVITY * (0.5 * (hn - hs))
                        + VISCOSITY * (vn + vs + ve + vw - 4.0 * v)
                        - BOTTOM_DRAG * v
                    )
                )
                nh = h - TIME_STEP * DEPTH_SCALE * div
                put(p, i, nu, nv, nh)

    def put_first(p, i, nu, nv, nh):
        inside = inside_ref[i + 2]
        for f, value in enumerate((nu, nv, nh * inside)):
            b_ref[p, f, i + 1] = value

    def put_second(p, i, nu, nv, nh):
        for f, value in enumerate((nu, nv, nh)):
            c_ref[p, f, pl.ds(i * SUB, SUB), :] = value

    substep(a_ref, 2, put_first, -1, rows + 1)
    substep(b_ref, 1, put_second, 0, rows)

    def joined(f, start):
        lane8 = lax.broadcasted_iota(jnp.int32, (SUB, LANES), 1)
        main = c_ref[0, f, pl.ds(start, SUB, stride=SUB), :]
        edge = c_ref[1, f, pl.ds(start, SUB, stride=SUB), :]
        out = jnp.where(lane8 < 2, roll(edge, -8), main)
        return jnp.where(lane8 >= LANES - 2, roll(edge, LANES - 2 - (GROUP + 6)), out)

    for j in range(rows // SUB):
        for q in range(own_levels):
            lev = place * own_levels + q
            dst = q * rows + j * SUB
            east_ref[dst : dst + SUB, :] = joined(0, j * SUB * SUB + lev)
            north_ref[dst : dst + SUB, :] = joined(1, j * SUB * SUB + lev)
        height_ref[j * SUB : (j + 1) * SUB, :] = joined(2, j * SUB * SUB)


def momentum(place, coriolis, inside, flow_parts, rows, own_levels):
    vmem = pl.BlockSpec(memory_space=pltpu.VMEM)
    args = (coriolis, inside) + flow_parts
    return pl.pallas_call(
        momentum_kernel,
        in_specs=[pl.BlockSpec(memory_space=pltpu.SMEM)] * 3 + [vmem] * len(flow_parts),
        out_shape=(
            jax.ShapeDtypeStruct((own_levels * rows, LANES), F32),
            jax.ShapeDtypeStruct((own_levels * rows, LANES), F32),
            jax.ShapeDtypeStruct((rows, LANES), F32),
        ),
        scratch_shapes=[
            pltpu.VMEM((2, 4, rows + 4, SUB, LANES), F32),
            pltpu.VMEM((2, 3, rows + 2, SUB, LANES), F32),
            pltpu.VMEM((2, 3, rows * SUB, LANES), F32),
        ],
        compiler_params=grant(12),
        name="momentum",
    )(place, *args)


def to_peer(block, k):
    count = lax.axis_size("trc")
    return lax.ppermute(block, "trc", [(i, i ^ k) for i in range(count)])


def exchanged(blocks):
    out = [blocks[0]]
    for k in range(1, len(blocks)):
        out.append(to_peer(blocks[k], k))
    return out


def from_lat(block, step):
    count = lax.axis_size("lat")
    return lax.ppermute(
        block, "lat", [(i, i + step) for i in range(count) if 0 <= i + step < count]
    )


def both_sides(block):
    count = lax.axis_size("lon")
    left = lax.ppermute(block, "lon", [(i, (i + 1) % count) for i in range(count)])
    if count == 2:
        return left, left
    return left, lax.ppermute(block, "lon", [(i, (i - 1) % count) for i in range(count)])


def body(
    species_concentrations,
    zonal_velocity_array,
    meridional_velocity_array,
    thermal_anomaly,
    ocean_top_height_grid,
    water_layer_tally,
    species_interaction_table,
    species_production_pace,
    photon_uptake,
):
    count, levels, rows, cols = species_concentrations.shape
    own_levels = zonal_velocity_array.shape[0]
    shards = lax.axis_size("trc")
    assert levels == SUB and cols == LANES and count * GROUP == LANES and shards & (shards - 1) == 0
    trc_place = lax.axis_index("trc")
    place = trc_place.astype(jnp.int32).reshape(1)
    lat_total = rows * lax.axis_size("lat")
    lat_first = lax.axis_index("lat") * rows
    lat_global = (lat_first + jnp.arange(-2, rows + 2)).astype(F32)
    angle = math.pi * ((lat_global + 0.5) / lat_total - 0.5)
    coriolis = CORIOLIS_SCALE * jnp.sin(angle)
    surface = 1.0 + jnp.cos(angle[2:-2])
    inside = ((lat_global >= 0) & (lat_global < lat_total)).astype(F32)

    x = species_concentrations.reshape(count, levels * rows, cols)
    own = jnp.stack([zonal_velocity_array, meridional_velocity_array]).reshape(
        2, own_levels * rows, cols
    )
    peers = [to_peer(own, k) for k in range(1, shards)]
    strip, *messages = pack_tracers(x)
    flow, fstrip, fcols, fup, fdown = pack_flow(
        place, own, peers, water_layer_tally, ocean_top_height_grid, messages
    )
    left_in, right_in = both_sides(fcols)
    up_in, down_in = from_lat(fup, 1), from_lat(fdown, -1)
    corner = pack_edges(up_in, down_in)
    cleft_in, cright_in = both_sides(corner)
    inner = (flow, fstrip, left_in, right_in)
    outer = (up_in, down_in, cleft_in, cright_in)
    quarter = rows // 4
    bands = (((quarter,), 2 * quarter, inner), ((0, 3 * quarter), quarter, inner + outer))
    blocks = []
    for firsts, span, parts in bands:
        moved = transport(place, shards, x, strip, parts, firsts, span)
        blocks.append(exchanged(moved))
    back = []
    for n, (firsts, span, _) in enumerate(bands):
        reacted = react(
            place,
            species_interaction_table,
            species_production_pace,
            photon_uptake,
            surface,
            water_layer_tally,
            blocks[n],
            firsts,
        )
        back.append(exchanged(reacted))
    late, back[-1][0] = lax.optimization_barrier((place, back[-1][0]))
    east_out, north_out, height_out = momentum(
        late, coriolis, inside, inner + outer, rows, own_levels
    )
    done = ()
    for n, (firsts, span, _) in enumerate(bands):
        done = finish(
            place, thermal_anomaly, back[n], species_concentrations.shape, firsts, span, done
        )
    updated, temperature = done
    vel = (own_levels, rows, cols)
    return (
        updated,
        east_out.reshape(vel),
        north_out.reshape(vel),
        temperature,
        height_out,
    )


def solution(mesh):
    return jax.shard_map(
        body,
        mesh=mesh,
        in_specs=(
            P("trc", None, "lat", "lon"),
            P("trc", "lat", "lon"),
            P("trc", "lat", "lon"),
            P("trc", "lat", "lon"),
            P("lat", "lon"),
            P("lat", "lon"),
            P(),
            P(),
            P(),
        ),
        out_specs=(
            P("trc", None, "lat", "lon"),
            P("trc", "lat", "lon"),
            P("trc", "lat", "lon"),
            P("trc", "lat", "lon"),
            P("lat", "lon"),
        ),
        check_vma=False,
    )
```

```python
import functools
import math

import jax
import jax.numpy as jnp
from jax import lax
from jax.experimental import pallas as pl
from jax.experimental.pallas import tpu as pltpu
from jax.sharding import PartitionSpec as P

TIME_STEP = 0.1
GRAVITY = 1.0
VISCOSITY = 0.2
BOTTOM_DRAG = 0.05
DEPTH_SCALE = 0.5
CORIOLIS_SCALE = 0.5
COLUMN_DEPTH = 2.0
WATER_ABSORB = 0.2
HALF_LIGHT = 0.5
REACT_STEP = 0.1
WARMING_WEIGHT = 1.0

SUB = 8
LANES = 128
HALO = 4
CORNER = 3
GROUP = 16
F32 = jnp.float32


def lane_ids():
    return lax.broadcasted_iota(jnp.int32, (SUB, LANES), 1)


def level_ids():
    return lax.broadcasted_iota(jnp.int32, (SUB, LANES), 0)


def roll(x, shift):
    shift = shift % LANES
    return x if shift == 0 else pltpu.roll(x, shift, 1)


def strip_of(rows):
    lane = lane_ids()
    out = None
    for t, value in enumerate(rows):
        rolled = roll(value, GROUP * t + GROUP // 2)
        if out is None:
            out = rolled
        else:
            out = jnp.where(lane // GROUP == t, rolled, out)
    return out


def middle_mask():
    lane = lane_ids() % GROUP
    return (lane >= 4) & (lane < 12)


def pair_up(first, second):
    return jnp.where(middle_mask(), first, roll(second, 8))


def quad_up(a, b, c, d):
    return jnp.where(lane_ids() < 64, pair_up(a, b), roll(pair_up(c, d), 64))


def merge_left(own, got):
    lane = lane_ids() % GROUP
    return jnp.where((lane >= 4) & (lane < 8), got, own)


def merge_right(own, got):
    lane = lane_ids() % GROUP
    return jnp.where((lane >= 8) & (lane < 12), got, own)


def band_row(firsts, span, at):
    row = firsts[0] + at
    for n in range(1, len(firsts)):
        row = jnp.where(at >= n * span, firsts[n] + at - n * span, row)
    return row


def over_levels(row):
    return jnp.broadcast_to(row[0:1, :], (SUB, LANES))


def grant(mib):
    return pltpu.CompilerParams(vmem_limit_bytes=mib << 20)


def pack_tracers_kernel(x_ref, strip_ref, up_ref, down_ref, cols_ref):
    count, rows = x_ref.shape[0], x_ref.shape[1] // SUB
    half = rows // 2

    def row_strip(r):
        return strip_of([x_ref[t, pl.ds(r, SUB, stride=rows), :] for t in range(count)])

    for r in range(half):
        low, high = row_strip(r), row_strip(r + half)
        strip_ref[r] = low
        strip_ref[r + half] = high
        cols_ref[r] = pair_up(low, high)
    for t in range(count):
        for j in range(HALO):
            down_ref[t * HALO + j] = x_ref[t, pl.ds(j, SUB, stride=rows), :]
            up_ref[t * HALO + j] = x_ref[t, pl.ds(rows - HALO + j, SUB, stride=rows), :]


def pack_tracers(x):
    count, rows = x.shape[0], x.shape[1] // SUB
    tile = lambda n: jax.ShapeDtypeStruct((n, SUB, LANES), F32)
    return pl.pallas_call(
        pack_tracers_kernel,
        out_shape=(
            tile(rows),
            tile(count * HALO),
            tile(count * HALO),
            tile(rows // 2),
        ),
        compiler_params=grant(8),
        name="pack_tracers",
    )(x)


def pack_flow_kernel(place_ref, own_ref, *refs):
    peers, rest = refs[:-11], refs[-11:]
    tally_ref, height_ref, tup_ref, tdown_ref, tcols_ref = rest[:5]
    flow_ref, strip_ref, cols_ref, up_ref, down_ref, all_ref = rest[5:]
    rows = tally_ref.shape[0]
    span = own_ref.shape[1]
    place = place_ref[0]
    for k, ref in enumerate((own_ref,) + tuple(peers)):
        base = pl.multiple_of((place ^ k) * span, SUB)
        for f in range(2):
            all_ref[f, pl.ds(base, span), :] = ref[f]
    for src, dst in ((tup_ref, up_ref), (tdown_ref, down_ref), (tcols_ref, cols_ref)):
        dst[0 : src.shape[0]] = src[...]
    nrow, ncol = tup_ref.shape[0], tcols_ref.shape[0]
    level = level_ids()
    tally_all = tally_ref[...].astype(F32)
    pair_all = jnp.minimum(tally_all, pltpu.roll(tally_all, LANES - 1, 1))
    wide = lambda v, r: jnp.broadcast_to(v[r : r + 1, :], (SUB, LANES))
    for r in range(rows):
        tally, height, pair = wide(tally_all, r), wide(height_ref, r), wide(pair_all, r)
        wet = level.astype(F32) < tally
        east = jnp.where(wet, all_ref[0, pl.ds(r, SUB, stride=rows), :], 0.0)
        north = jnp.where(wet, all_ref[1, pl.ds(r, SUB, stride=rows), :], 0.0)
        aux = jnp.where(level == 0, tally, jnp.where(level == 1, height, pair))
        for f, value in enumerate((east, north, aux)):
            flow_ref[f * rows + r] = value
            if r < HALO:
                down_ref[nrow + f * HALO + r] = value
            if r >= rows - HALO:
                up_ref[nrow + f * HALO + r - (rows - HALO)] = value
        strip_ref[r] = strip_of([east, north, aux])
    quarter = rows // 4
    for r in range(quarter):
        cols_ref[ncol + r] = quad_up(*[strip_ref[r + quarter * q] for q in range(4)])


def pack_flow(place, own, peers, tally, height, messages):
    rows = tally.shape[0]
    tile = lambda n: jax.ShapeDtypeStruct((n, SUB, LANES), F32)
    vmem = pl.BlockSpec(memory_space=pltpu.VMEM)
    tup, tdown, tcols = messages
    return pl.pallas_call(
        pack_flow_kernel,
        in_specs=[pl.BlockSpec(memory_space=pltpu.SMEM)] + [vmem] * (3 + len(peers) + len(messages)),
        out_shape=(
            tile(3 * rows),
            tile(rows),
            tile(tcols.shape[0] + rows // 4),
            tile(tup.shape[0] + 3 * HALO),
            tile(tdown.shape[0] + 3 * HALO),
        ),
        scratch_shapes=[pltpu.VMEM((2, SUB * rows, LANES), F32)],
        compiler_params=grant(8),
        name="pack_flow",
    )(place, own, *peers, tally, height, *messages)


def pack_edges_kernel(up_ref, down_ref, out_ref):
    count = up_ref.shape[0] // HALO - 3
    for n, ref in enumerate((up_ref, down_ref)):
        row = lambda f, j: ref[f * HALO + j]
        tracers = [strip_of([row(t, j) for t in range(count)]) for j in range(HALO)]
        flows = [strip_of([row(count + f, j) for f in range(3)]) for j in range(HALO)]
        base = n * CORNER
        for j in range(2):
            out_ref[base + j] = pair_up(tracers[j], tracers[j + 2])
        out_ref[base + 2] = quad_up(*flows)


def pack_edges(up, down):
    return pl.pallas_call(
        pack_edges_kernel,
        out_shape=jax.ShapeDtypeStruct((2 * CORNER, SUB, LANES), F32),
        compiler_params=grant(8),
        name="pack_edges",
    )(up, down)


class Flow:
    def __init__(self, flow_ref, strip_ref, left_ref, right_ref, outer=()):
        self.flow, self.strip = flow_ref, strip_ref
        self.left, self.right = left_ref, right_ref
        self.rows = strip_ref.shape[0]
        self.col_base = left_ref.shape[0] - self.rows // 4
        if outer:
            self.up, self.down, self.corner_left, self.corner_right = outer
            self.row_base = self.up.shape[0] - 3 * HALO

    def corner(self, r):
        return 0 if r < 0 else CORNER

    def row(self, f, r):
        if r < 0:
            return self.up[self.row_base + f * HALO + HALO + r]
        if r >= self.rows:
            return self.down[self.row_base + f * HALO + r - self.rows]
        return self.flow[f * self.rows + r]

    def strips(self, r):
        if 0 <= r < self.rows:
            quarter = self.rows // 4
            q, j = divmod(r, quarter)
            own = self.strip[r]
            left, right = self.left[self.col_base + j], self.right[self.col_base + j]
        else:
            own = strip_of([self.row(f, r) for f in range(3)])
            q = r + HALO if r < 0 else r - self.rows
            at = self.corner(r) + CORNER - 1
            left, right = self.corner_left[at], self.corner_right[at]
        shift = -(8 * (q % 2) + 64 * (q // 2))
        return merge_left(own, roll(left, shift)), merge_right(own, roll(right, shift))


def limited(ahead, behind):
    return jnp.maximum(
        jnp.minimum(ahead, jnp.maximum(behind, 0.0)), jnp.minimum(behind, 0.0)
    )


def face_pair(vel, vel_next, wet):
    a = jnp.where(wet, 0.5 * (vel + vel_next), 0.0)
    size = jnp.abs(a)
    return a, 0.5 * size * (1.0 - size)


def transport_rows(streams, ax_ref, bx_ref, ay_ref, by_ref, first, last):
    states = []
    for load, *_ in streams:
        before, here, after = load(first - 2), load(first - 1), load(first)
        states.append((here, after, limited(after - here, here - before), after - here, None))
    for i in range(first - 1, last):
        for n, (load, store, kind, xo, yo) in enumerate(streams):
            row, nxt, slope, diff, below = states[n]
            far = load(i + 2)
            diff_next = far - nxt
            slope_next = limited(diff_next, diff)
            ay, by = ay_ref[kind, yo + i], by_ref[kind, yo + i]
            positive = ay >= 0.0
            above = ay * jnp.where(positive, row, nxt) + by * jnp.where(positive, slope, slope_next)
            if below is not None:
                ax, bx = ax_ref[kind, xo + i], bx_ref[kind, xo + i]
                east = roll(row, -1)
                dx = east - row
                sx = limited(dx, roll(dx, 1))
                sx_east = roll(sx, -1)
                pos = ax >= 0.0
                fx = ax * jnp.where(pos, row, east) + bx * jnp.where(pos, sx, sx_east)
                store(i, row - (fx - roll(fx, 1)) - (above - below))
            states[n] = (nxt, far, slope_next, diff_next, above)


def select_lanes(moves):
    parts = []
    source = lax.broadcasted_iota(jnp.int32, (LANES, LANES), 0)
    target = lax.broadcasted_iota(jnp.int32, (LANES, LANES), 1)
    for f, d in moves:
        parts.append(jnp.where(source == GROUP * f + target % GROUP + d, 1.0, 0.0))
    return jnp.concatenate(parts, axis=1)


def exact_dot(a, b):
    return jnp.dot(a, b, precision=lax.Precision.HIGHEST, preferred_element_type=F32)


def transport_kernel(
    place_ref, x_ref, strip_ref, flow_ref, fstrip_ref, left_ref, right_ref, *refs, firsts, span, shards, together
):
    outer, outs, scratch = refs[: -shards - 11], refs[-shards - 11 : -11], refs[-11:]
    ext_ref, ax_ref, bx_ref, ay_ref, by_ref, first_ref, moved_ref, edge_ref, spread_ref, main_ref, shift_ref = scratch
    count, rows = x_ref.shape[0], x_ref.shape[1] // SUB
    half = rows // 2
    place = place_ref[0]
    level = level_ids().astype(F32)
    flow = Flow(flow_ref, fstrip_ref, left_ref, right_ref, outer)
    wide = span + 2 * HALO
    every = [(n, q, first + q) for n, first in enumerate(firsts) for q in range(-HALO, span + HALO)]
    tile_at = lambda n, q: pl.ds((n * wide + q + HALO) * SUB, SUB)

    for n, q, r in every:
        main_ref[tile_at(n, q), :] = flow.row(0, r)
        left, right = flow.strips(r)
        edge_ref[0, tile_at(n, q), :] = left
        edge_ref[1, tile_at(n, q), :] = right
    shift_east = jnp.where(
        lax.broadcasted_iota(jnp.int32, (LANES, LANES), 0)
        == lax.broadcasted_iota(jnp.int32, (LANES, LANES), 1) + 1,
        1.0,
        0.0,
    )
    shift_ref[...] = exact_dot(main_ref[...], shift_east)
    moves = select_lanes(((0, 0), (0, 1), (1, 0), (2, 0), (2, 1)))
    for side in range(2):
        spread_ref[side] = exact_dot(edge_ref[side], moves)

    previous = None
    for n, q, r in every:
        at = tile_at(n, q)
        aux = flow.row(2, r)
        spread = lambda v, i: jnp.broadcast_to(v[i : i + 1, :], (SUB, LANES))
        kinds = [(main_ref[at, :], shift_ref[at, :], flow.row(1, r), spread(aux, 0), spread(aux, 2))]
        for side in range(2):
            east, east_next, north, tally, tally_next = (
                spread_ref[side, at, LANES * j : LANES * (j + 1)] for j in range(5)
            )
            tally, tally_next = spread(tally, 0), spread(tally_next, 0)
            kinds.append((east, east_next, north, tally, jnp.minimum(tally, tally_next)))
        for kind, (east, east_next, north, tally, pair) in enumerate(kinds):
            if -2 <= q < span + 2:
                i = n * (span + 4) + q + 2
                ax_ref[kind, i], bx_ref[kind, i] = face_pair(east, east_next, level < pair)
            if -2 <= q < span + 3:
                i = n * (span + 5) + q + 2
                below, depth = previous[kind]
                ay_ref[kind, i], by_ref[kind, i] = face_pair(
                    below, north, level < jnp.minimum(depth, tally)
                )
        previous = [(k[2], k[3]) for k in kinds]

    for n, q, r in every:
        if r < 0 or r >= rows:
            src = flow.up if r < 0 else flow.down
            j = r + HALO if r < 0 else r - rows
            fields = [src[t * HALO + j] for t in range(count)]
            own = strip_of(fields)
            at = flow.corner(r) + j % 2
            left, right = flow.corner_left[at], flow.corner_right[at]
            swap = j >= 2
        else:
            fields = [x_ref[t, pl.ds(r, SUB, stride=rows), :] for t in range(count)]
            own = strip_ref[r]
            left, right = left_ref[r % half], right_ref[r % half]
            swap = r >= half
        if swap:
            left, right = roll(left, -8), roll(right, -8)
        fields += [merge_left(own, left), merge_right(own, right)]
        for t, value in enumerate(fields):
            ext_ref[t, n * wide + HALO + q] = value

    def some(c, carry):
        before, after = [], []
        for j in range(together):
            p = c * together + j
            kind = jnp.maximum(p - (count - 1), 0)
            for n in range(len(firsts)):
                xo, yo = n * (span + 4) + 2, n * (span + 5) + 3

                def load_start(i, p=p, n=n):
                    return ext_ref[p, n * wide + HALO + i]

                def store_first(i, value, j=j, xo=xo):
                    first_ref[j, xo + i] = value

                def load_first(i, j=j, xo=xo):
                    return first_ref[j, xo + i]

                def store_moved(i, value, p=p, n=n):
                    moved_ref[p, n * span + i] = value

                before.append((load_start, store_first, kind, xo, yo))
                after.append((load_first, store_moved, kind, xo, yo))
        transport_rows(before, ax_ref, bx_ref, ay_ref, by_ref, -2, span + 2)
        transport_rows(after, ax_ref, bx_ref, ay_ref, by_ref, 0, span)
        return carry

    lax.fori_loop(0, (count + 2) // together, some, 0)

    lane = lane_ids()
    edge = (lane < 4) | (lane >= LANES - 4)
    from_right = (lane % GROUP >= 4) & (lane % GROUP < 8)
    share = span * len(firsts) // len(outs)
    for k, out_ref in enumerate(outs):
        base = (place ^ k) * share
        for r in range(share):
            joined = jnp.where(from_right, moved_ref[count + 1, base + r], moved_ref[count, base + r])
            for t in range(count):
                out_ref[t * share + r] = jnp.where(
                    edge, roll(joined, -(GROUP * t + 8)), moved_ref[t, base + r]
                )


def transport(place, shards, x, strip, flow_parts, firsts, span, together):
    count = x.shape[0]
    vmem = pl.BlockSpec(memory_space=pltpu.VMEM)
    tile = lambda *n: pltpu.VMEM(n + (SUB, LANES), F32)
    flat = lambda *n: pltpu.VMEM(n, F32)
    args = (x, strip) + flow_parts
    pieces = len(firsts)
    wide = (span + 2 * HALO) * pieces
    return pl.pallas_call(
        functools.partial(transport_kernel, firsts=firsts, span=span, shards=shards, together=together),
        in_specs=[pl.BlockSpec(memory_space=pltpu.SMEM)] + [vmem] * len(args),
        out_shape=tuple(
            jax.ShapeDtypeStruct((count * span * pieces // shards, SUB, LANES), F32)
            for _ in range(shards)
        ),
        scratch_shapes=[
            tile(count + 2, wide),
            tile(3, (span + 4) * pieces),
            tile(3, (span + 4) * pieces),
            tile(3, (span + 5) * pieces),
            tile(3, (span + 5) * pieces),
            tile(together, (span + 4) * pieces),
            tile(count + 2, span * pieces),
            flat(2, wide * SUB, LANES),
            flat(2, wide * SUB, 5 * LANES),
            flat(wide * SUB, LANES),
            flat(wide * SUB, LANES),
        ],
        compiler_params=grant(20),
        name="transport",
    )(place, *args)


def react_kernel(place_ref, table_ref, pace_ref, uptake_ref, surface_ref, tally_ref, *refs, firsts):
    shards = (len(refs) - 3) // 2
    ins, outs = refs[:shards], refs[shards : 2 * shards]
    light_ref, wet_ref, heat_ref = refs[2 * shards :]
    total = pace_ref.shape[0]
    count = total // shards
    share = ins[0].shape[0] // count
    place = place_ref[0]
    level = level_ids()
    heat_ref[...] = jnp.zeros_like(heat_ref)

    for r in range(share):
        row = band_row(firsts, share * shards // len(firsts), place * share + r)
        tally = jnp.broadcast_to(tally_ref[pl.ds(row, 1), :], (SUB, LANES))
        surface = surface_ref[row]
        wet = jnp.where(level < tally, 1.0, 0.0)
        absorbed = jnp.zeros((SUB, LANES), F32)
        for k, ref in enumerate(ins):
            for t in range(count):
                absorbed = absorbed + uptake_ref[(place ^ k) * count + t] * jnp.abs(ref[t * share + r])
        layer = (COLUMN_DEPTH / SUB) * (WATER_ABSORB + absorbed) * wet
        total_depth = jnp.where(level >= 1, pltpu.roll(layer, 1, 0), 0.0)
        for shift in (1, 2, 4):
            total_depth = total_depth + jnp.where(
                level >= shift, pltpu.roll(total_depth, shift, 0), 0.0
            )
        top = surface * jnp.exp(-total_depth)
        heat_ref[pl.ds(r * SUB, SUB), :] = top * (1.0 - jnp.exp(-layer))
        light_ref[r] = REACT_STEP * wet * (top / (top + HALF_LIGHT))
        wet_ref[r] = REACT_STEP * wet

    block = 4
    for k, out_ref in enumerate(outs):
        for m0 in range(0, count, block):
            dest = [(place ^ k) * count + m0 + j for j in range(block)]
            acc = [[None] * share for _ in range(block)]
            for kk, ref in enumerate(ins):
                for t in range(count):
                    n = (place ^ kk) * count + t
                    values = [ref[t * share + r] for r in range(share)]
                    for j in range(block):
                        c = table_ref[dest[j], n]
                        for r in range(share):
                            term = c * values[r]
                            acc[j][r] = term if acc[j][r] is None else acc[j][r] + term
            for j in range(block):
                pace = pace_ref[dest[j]]
                for r in range(share):
                    own = ins[k][(m0 + j) * share + r]
                    out_ref[(m0 + j) * share + r] = (
                        own + wet_ref[r] * acc[j][r] + pace * (light_ref[r] * own)
                    )
        own_levels = SUB // shards
        for q in range(own_levels):
            level_at = (place ^ k) * own_levels + q
            out_ref[count * share + q] = heat_ref[pl.ds(level_at, SUB, stride=SUB), :]


def react(place, table, pace, uptake, surface, tally, blocks, firsts):
    shards = len(blocks)
    share = blocks[0].shape[0] // (pace.shape[0] // shards)
    smem = pl.BlockSpec(memory_space=pltpu.SMEM)
    vmem = pl.BlockSpec(memory_space=pltpu.VMEM)
    assert share <= SUB
    return pl.pallas_call(
        functools.partial(react_kernel, firsts=firsts),
        in_specs=[smem] * 5 + [vmem] * (1 + shards),
        out_shape=tuple(
            jax.ShapeDtypeStruct((b.shape[0] + SUB // shards, SUB, LANES), F32) for b in blocks
        ),
        scratch_shapes=[
            pltpu.VMEM((share, SUB, LANES), F32),
            pltpu.VMEM((share, SUB, LANES), F32),
            pltpu.VMEM((SUB * SUB, LANES), F32),
        ],
        compiler_params=grant(8),
        name="react",
    )(place, table, pace, uptake, surface, tally, *blocks)


def finish_kernel(place_ref, thermal_ref, *refs, bands, shards):
    *ins, out_ref, temp_ref, cells_ref = refs
    count, _, rows, _ = out_ref.shape
    own_levels = SUB // shards
    place = place_ref[0]
    for n, (firsts, span) in enumerate(bands):
        share = span * len(firsts) // shards
        for k, ref in enumerate(ins[n * shards : (n + 1) * shards]):
            for r in range(share):
                row = band_row(firsts, span, (place ^ k) * share + r)
                for m in range(count):
                    at = pl.multiple_of((m * rows + row) * SUB, SUB)
                    cells_ref[pl.ds(at, SUB), :] = ref[m * share + r]
                for q in range(own_levels):
                    heat = ref[count * share + q]
                    at = pl.multiple_of(((count + q) * rows + row) * SUB, SUB)
                    cells_ref[pl.ds(at, SUB), :] = jnp.broadcast_to(heat[r : r + 1, :], (SUB, LANES))
    for b in range(0, rows, SUB):
        for m in range(count):
            for lev in range(SUB):
                start = (m * rows + b) * SUB + lev
                out_ref[m, lev, b : b + SUB, :] = cells_ref[pl.ds(start, SUB, stride=SUB), :]
        for q in range(own_levels):
            heat = cells_ref[pl.ds(((count + q) * rows + b) * SUB, SUB, stride=SUB), :]
            temp_ref[q, b : b + SUB, :] = thermal_ref[q, b : b + SUB, :] + WARMING_WEIGHT * heat


def finish(place, thermal, blocks, shape, bands):
    count, _, rows, _ = shape
    own_levels = thermal.shape[0]
    shards = SUB // own_levels
    vmem = pl.BlockSpec(memory_space=pltpu.VMEM)
    return pl.pallas_call(
        functools.partial(finish_kernel, bands=bands, shards=shards),
        in_specs=[pl.BlockSpec(memory_space=pltpu.SMEM)] + [vmem] * (1 + len(blocks)),
        out_shape=(jax.ShapeDtypeStruct(shape, F32), jax.ShapeDtypeStruct(thermal.shape, F32)),
        scratch_shapes=[pltpu.VMEM(((count + own_levels) * rows * SUB, LANES), F32)],
        compiler_params=grant(12),
        name="finish",
    )(place, thermal, *blocks)


def level_sum(x):
    for shift in (4, 2, 1):
        x = x + pltpu.roll(x, shift, 0)
    return x


def momentum_kernel(
    place_ref,
    coriolis_ref,
    inside_ref,
    flow_ref,
    strip_ref,
    left_ref,
    right_ref,
    up_ref,
    down_ref,
    cleft_ref,
    cright_ref,
    east_ref,
    north_ref,
    height_ref,
    a_ref,
    b_ref,
    c_ref,
):
    rows = height_ref.shape[0]
    own_levels = east_ref.shape[0] // rows
    place = place_ref[0]
    lane = lane_ids()
    level = level_ids().astype(F32)
    flow = Flow(flow_ref, strip_ref, left_ref, right_ref, (up_ref, down_ref, cleft_ref, cright_ref))
    for r in range(-2, rows + 2):
        east, north, aux = (flow.row(f, r) for f in range(3))
        left, right = flow.strips(r)
        both = [
            jnp.where(lane < GROUP, roll(left, -GROUP * f), roll(right, GROUP - GROUP * f))
            for f in range(3)
        ]
        for p, (u, v, w) in enumerate(((east, north, aux), both)):
            wet = jnp.where(level < over_levels(w), 1.0, 0.0)
            h = jnp.broadcast_to(w[1:2, :], (SUB, LANES))
            for f, value in enumerate((u, v, h, wet)):
                a_ref[p, f, r + 2] = value

    def substep(src, offset, put, first, last):
        for p in range(2):
            for i in range(first, last):
                g = lambda f, d: src[p, f, i + offset + d]
                u, v, h = g(0, 0), g(1, 0), g(2, 0)
                un, us, vn, vs, hn, hs = g(0, 1), g(0, -1), g(1, 1), g(1, -1), g(2, 1), g(2, -1)
                wet = a_ref[p, 3, i + 2]
                cor = coriolis_ref[i + 2]
                ue, uw, ve, vw, he, hw = (
                    roll(u, -1), roll(u, 1), roll(v, -1), roll(v, 1), roll(h, -1), roll(h, 1),
                )
                div = level_sum(0.5 * (ue - uw) + 0.5 * (vn - vs))
                nu = wet * (
                    u
                    + TIME_STEP
                    * (
                        cor * v
                        - GRAVITY * (0.5 * (he - hw))
                        + VISCOSITY * (un + us + ue + uw - 4.0 * u)
                        - BOTTOM_DRAG * u
                    )
                )
                nv = wet * (
                    v
                    + TIME_STEP
                    * (
                        -cor * u
                        - GRAVITY * (0.5 * (hn - hs))
                        + VISCOSITY * (vn + vs + ve + vw - 4.0 * v)
                        - BOTTOM_DRAG * v
                    )
                )
                nh = h - TIME_STEP * DEPTH_SCALE * div
                put(p, i, nu, nv, nh)

    def put_first(p, i, nu, nv, nh):
        inside = inside_ref[i + 2]
        for f, value in enumerate((nu, nv, nh * inside)):
            b_ref[p, f, i + 1] = value

    def put_second(p, i, nu, nv, nh):
        for f, value in enumerate((nu, nv, nh)):
            c_ref[p, f, pl.ds(i * SUB, SUB), :] = value

    substep(a_ref, 2, put_first, -1, rows + 1)
    substep(b_ref, 1, put_second, 0, rows)

    def joined(f, start):
        lane8 = lax.broadcasted_iota(jnp.int32, (SUB, LANES), 1)
        main = c_ref[0, f, pl.ds(start, SUB, stride=SUB), :]
        edge = c_ref[1, f, pl.ds(start, SUB, stride=SUB), :]
        out = jnp.where(lane8 < 2, roll(edge, -8), main)
        return jnp.where(lane8 >= LANES - 2, roll(edge, LANES - 2 - (GROUP + 6)), out)

    for j in range(rows // SUB):
        for q in range(own_levels):
            lev = place * own_levels + q
            dst = q * rows + j * SUB
            east_ref[dst : dst + SUB, :] = joined(0, j * SUB * SUB + lev)
            north_ref[dst : dst + SUB, :] = joined(1, j * SUB * SUB + lev)
        height_ref[j * SUB : (j + 1) * SUB, :] = joined(2, j * SUB * SUB)


def momentum(place, coriolis, inside, flow_parts, rows, own_levels):
    vmem = pl.BlockSpec(memory_space=pltpu.VMEM)
    args = (coriolis, inside) + flow_parts
    return pl.pallas_call(
        momentum_kernel,
        in_specs=[pl.BlockSpec(memory_space=pltpu.SMEM)] * 3 + [vmem] * len(flow_parts),
        out_shape=(
            jax.ShapeDtypeStruct((own_levels * rows, LANES), F32),
            jax.ShapeDtypeStruct((own_levels * rows, LANES), F32),
            jax.ShapeDtypeStruct((rows, LANES), F32),
        ),
        scratch_shapes=[
            pltpu.VMEM((2, 4, rows + 4, SUB, LANES), F32),
            pltpu.VMEM((2, 3, rows + 2, SUB, LANES), F32),
            pltpu.VMEM((2, 3, rows * SUB, LANES), F32),
        ],
        compiler_params=grant(12),
        name="momentum",
    )(place, *args)


def to_peer(block, k):
    count = lax.axis_size("trc")
    return lax.ppermute(block, "trc", [(i, i ^ k) for i in range(count)])


def exchanged(blocks):
    out = [blocks[0]]
    for k in range(1, len(blocks)):
        out.append(to_peer(blocks[k], k))
    return out


def from_lat(block, step):
    count = lax.axis_size("lat")
    return lax.ppermute(
        block, "lat", [(i, i + step) for i in range(count) if 0 <= i + step < count]
    )


def both_sides(block):
    count = lax.axis_size("lon")
    left = lax.ppermute(block, "lon", [(i, (i + 1) % count) for i in range(count)])
    if count == 2:
        return left, left
    return left, lax.ppermute(block, "lon", [(i, (i - 1) % count) for i in range(count)])


def body(
    species_concentrations,
    zonal_velocity_array,
    meridional_velocity_array,
    thermal_anomaly,
    ocean_top_height_grid,
    water_layer_tally,
    species_interaction_table,
    species_production_pace,
    photon_uptake,
):
    count, levels, rows, cols = species_concentrations.shape
    own_levels = zonal_velocity_array.shape[0]
    shards = lax.axis_size("trc")
    assert levels == SUB and cols == LANES and count * GROUP == LANES and shards & (shards - 1) == 0
    trc_place = lax.axis_index("trc")
    place = trc_place.astype(jnp.int32).reshape(1)
    lat_total = rows * lax.axis_size("lat")
    lat_first = lax.axis_index("lat") * rows
    lat_global = (lat_first + jnp.arange(-2, rows + 2)).astype(F32)
    angle = math.pi * ((lat_global + 0.5) / lat_total - 0.5)
    coriolis = CORIOLIS_SCALE * jnp.sin(angle)
    surface = 1.0 + jnp.cos(angle[2:-2])
    inside = ((lat_global >= 0) & (lat_global < lat_total)).astype(F32)

    x = species_concentrations.reshape(count, levels * rows, cols)
    own = jnp.stack([zonal_velocity_array, meridional_velocity_array]).reshape(
        2, own_levels * rows, cols
    )
    peers = [to_peer(own, k) for k in range(1, shards)]
    strip, *messages = pack_tracers(x)
    flow, fstrip, fcols, fup, fdown = pack_flow(
        place, own, peers, water_layer_tally, ocean_top_height_grid, messages
    )
    left_in, right_in = both_sides(fcols)
    up_in, down_in = from_lat(fup, 1), from_lat(fdown, -1)
    corner = pack_edges(up_in, down_in)
    cleft_in, cright_in = both_sides(corner)
    inner = (flow, fstrip, left_in, right_in)
    outer = (up_in, down_in, cleft_in, cright_in)
    bands = (
        ((HALO,), rows - 2 * HALO, 1, inner),
        ((0, rows - HALO), HALO, 2, inner + outer),
    )
    assert all(len(firsts) * span % shards == 0 for firsts, span, *_ in bands)
    blocks = []
    for firsts, span, together, parts in bands:
        moved = transport(place, shards, x, strip, parts, firsts, span, together)
        blocks.append(exchanged(moved))
    back = []
    for n, (firsts, *_) in enumerate(bands):
        reacted = react(
            place,
            species_interaction_table,
            species_production_pace,
            photon_uptake,
            surface,
            water_layer_tally,
            blocks[n],
            firsts,
        )
        back.append(exchanged(reacted))
    late, back[-1][0] = lax.optimization_barrier((place, back[-1][0]))
    east_out, north_out, height_out = momentum(
        late, coriolis, inside, inner + outer, rows, own_levels
    )
    updated, temperature = finish(
        place,
        thermal_anomaly,
        back[0] + back[1],
        species_concentrations.shape,
        tuple((firsts, span) for firsts, span, *_ in bands),
    )
    vel = (own_levels, rows, cols)
    return (
        updated,
        east_out.reshape(vel),
        north_out.reshape(vel),
        temperature,
        height_out,
    )


def solution(mesh):
    return jax.shard_map(
        body,
        mesh=mesh,
        in_specs=(
            P("trc", None, "lat", "lon"),
            P("trc", "lat", "lon"),
            P("trc", "lat", "lon"),
            P("trc", "lat", "lon"),
            P("lat", "lon"),
            P("lat", "lon"),
            P(),
            P(),
            P(),
        ),
        out_specs=(
            P("trc", None, "lat", "lon"),
            P("trc", "lat", "lon"),
            P("trc", "lat", "lon"),
            P("trc", "lat", "lon"),
            P("lat", "lon"),
        ),
        check_vma=False,
    )
```

```python
import functools
import math

import jax
import jax.numpy as jnp
from jax import lax
from jax.experimental import pallas as pl
from jax.experimental.pallas import tpu as pltpu
from jax.sharding import PartitionSpec as P

TIME_STEP = 0.1
GRAVITY = 1.0
VISCOSITY = 0.2
BOTTOM_DRAG = 0.05
DEPTH_SCALE = 0.5
CORIOLIS_SCALE = 0.5
COLUMN_DEPTH = 2.0
WATER_ABSORB = 0.2
HALF_LIGHT = 0.5
REACT_STEP = 0.1
WARMING_WEIGHT = 1.0

SUB = 8
LANES = 128
HALO = 4
CORNER = 3
GROUP = 16
F32 = jnp.float32


def lane_ids():
    return lax.broadcasted_iota(jnp.int32, (SUB, LANES), 1)


def level_ids():
    return lax.broadcasted_iota(jnp.int32, (SUB, LANES), 0)


def roll(x, shift):
    shift = shift % LANES
    return x if shift == 0 else pltpu.roll(x, shift, 1)


def strip_of(rows):
    lane = lane_ids()
    out = None
    for t, value in enumerate(rows):
        rolled = roll(value, GROUP * t + GROUP // 2)
        if out is None:
            out = rolled
        else:
            out = jnp.where(lane // GROUP == t, rolled, out)
    return out


def middle_mask():
    lane = lane_ids() % GROUP
    return (lane >= 4) & (lane < 12)


def pair_up(first, second):
    return jnp.where(middle_mask(), first, roll(second, 8))


def quad_up(a, b, c, d):
    return jnp.where(lane_ids() < 64, pair_up(a, b), roll(pair_up(c, d), 64))


def merge_left(own, got):
    lane = lane_ids() % GROUP
    return jnp.where((lane >= 4) & (lane < 8), got, own)


def merge_right(own, got):
    lane = lane_ids() % GROUP
    return jnp.where((lane >= 8) & (lane < 12), got, own)


def band_row(firsts, span, at):
    row = firsts[0] + at
    for n in range(1, len(firsts)):
        row = jnp.where(at >= n * span, firsts[n] + at - n * span, row)
    return row


def over_levels(row):
    return jnp.broadcast_to(row[0:1, :], (SUB, LANES))


def grant(mib):
    return pltpu.CompilerParams(vmem_limit_bytes=mib << 20)


def pack_tracers_kernel(x_ref, strip_ref, up_ref, down_ref, cols_ref):
    count, rows = x_ref.shape[0], x_ref.shape[1] // SUB
    half = rows // 2

    def row_strip(r):
        return strip_of([x_ref[t, pl.ds(r, SUB, stride=rows), :] for t in range(count)])

    for r in range(half):
        low, high = row_strip(r), row_strip(r + half)
        strip_ref[r] = low
        strip_ref[r + half] = high
        cols_ref[r] = pair_up(low, high)
    for t in range(count):
        for j in range(HALO):
            down_ref[t * HALO + j] = x_ref[t, pl.ds(j, SUB, stride=rows), :]
            up_ref[t * HALO + j] = x_ref[t, pl.ds(rows - HALO + j, SUB, stride=rows), :]


def pack_tracers(x):
    count, rows = x.shape[0], x.shape[1] // SUB
    tile = lambda n: jax.ShapeDtypeStruct((n, SUB, LANES), F32)
    return pl.pallas_call(
        pack_tracers_kernel,
        out_shape=(
            tile(rows),
            tile(count * HALO),
            tile(count * HALO),
            tile(rows // 2),
        ),
        compiler_params=grant(8),
        name="pack_tracers",
    )(x)


def pack_flow_kernel(place_ref, own_ref, *refs):
    peers, rest = refs[:-11], refs[-11:]
    tally_ref, height_ref, tup_ref, tdown_ref, tcols_ref = rest[:5]
    flow_ref, strip_ref, cols_ref, up_ref, down_ref, all_ref = rest[5:]
    rows = tally_ref.shape[0]
    span = own_ref.shape[1]
    place = place_ref[0]
    for k, ref in enumerate((own_ref,) + tuple(peers)):
        base = pl.multiple_of((place ^ k) * span, SUB)
        for f in range(2):
            all_ref[f, pl.ds(base, span), :] = ref[f]
    for src, dst in ((tup_ref, up_ref), (tdown_ref, down_ref), (tcols_ref, cols_ref)):
        dst[0 : src.shape[0]] = src[...]
    nrow, ncol = tup_ref.shape[0], tcols_ref.shape[0]
    level = level_ids()
    tally_all = tally_ref[...].astype(F32)
    pair_all = jnp.minimum(tally_all, pltpu.roll(tally_all, LANES - 1, 1))
    wide = lambda v, r: jnp.broadcast_to(v[r : r + 1, :], (SUB, LANES))
    for r in range(rows):
        tally, height, pair = wide(tally_all, r), wide(height_ref, r), wide(pair_all, r)
        wet = level.astype(F32) < tally
        east = jnp.where(wet, all_ref[0, pl.ds(r, SUB, stride=rows), :], 0.0)
        north = jnp.where(wet, all_ref[1, pl.ds(r, SUB, stride=rows), :], 0.0)
        aux = jnp.where(level == 0, tally, jnp.where(level == 1, height, pair))
        for f, value in enumerate((east, north, aux)):
            flow_ref[f * rows + r] = value
            if r < HALO:
                down_ref[nrow + f * HALO + r] = value
            if r >= rows - HALO:
                up_ref[nrow + f * HALO + r - (rows - HALO)] = value
        strip_ref[r] = strip_of([east, north, aux])
    quarter = rows // 4
    for r in range(quarter):
        cols_ref[ncol + r] = quad_up(*[strip_ref[r + quarter * q] for q in range(4)])


def pack_flow(place, own, peers, tally, height, messages):
    rows = tally.shape[0]
    tile = lambda n: jax.ShapeDtypeStruct((n, SUB, LANES), F32)
    vmem = pl.BlockSpec(memory_space=pltpu.VMEM)
    tup, tdown, tcols = messages
    return pl.pallas_call(
        pack_flow_kernel,
        in_specs=[pl.BlockSpec(memory_space=pltpu.SMEM)] + [vmem] * (3 + len(peers) + len(messages)),
        out_shape=(
            tile(3 * rows),
            tile(rows),
            tile(tcols.shape[0] + rows // 4),
            tile(tup.shape[0] + 3 * HALO),
            tile(tdown.shape[0] + 3 * HALO),
        ),
        scratch_shapes=[pltpu.VMEM((2, SUB * rows, LANES), F32)],
        compiler_params=grant(8),
        name="pack_flow",
    )(place, own, *peers, tally, height, *messages)


def pack_edges_kernel(up_ref, down_ref, out_ref):
    count = up_ref.shape[0] // HALO - 3
    for n, ref in enumerate((up_ref, down_ref)):
        row = lambda f, j: ref[f * HALO + j]
        tracers = [strip_of([row(t, j) for t in range(count)]) for j in range(HALO)]
        flows = [strip_of([row(count + f, j) for f in range(3)]) for j in range(HALO)]
        base = n * CORNER
        for j in range(2):
            out_ref[base + j] = pair_up(tracers[j], tracers[j + 2])
        out_ref[base + 2] = quad_up(*flows)


def pack_edges(up, down):
    return pl.pallas_call(
        pack_edges_kernel,
        out_shape=jax.ShapeDtypeStruct((2 * CORNER, SUB, LANES), F32),
        compiler_params=grant(8),
        name="pack_edges",
    )(up, down)


class Flow:
    def __init__(self, flow_ref, strip_ref, left_ref, right_ref, outer=()):
        self.flow, self.strip = flow_ref, strip_ref
        self.left, self.right = left_ref, right_ref
        self.rows = strip_ref.shape[0]
        self.col_base = left_ref.shape[0] - self.rows // 4
        if outer:
            self.up, self.down, self.corner_left, self.corner_right = outer
            self.row_base = self.up.shape[0] - 3 * HALO

    def corner(self, r):
        return 0 if r < 0 else CORNER

    def row(self, f, r):
        if r < 0:
            return self.up[self.row_base + f * HALO + HALO + r]
        if r >= self.rows:
            return self.down[self.row_base + f * HALO + r - self.rows]
        return self.flow[f * self.rows + r]

    def strips(self, r):
        if 0 <= r < self.rows:
            quarter = self.rows // 4
            q, j = divmod(r, quarter)
            own = self.strip[r]
            left, right = self.left[self.col_base + j], self.right[self.col_base + j]
        else:
            own = strip_of([self.row(f, r) for f in range(3)])
            q = r + HALO if r < 0 else r - self.rows
            at = self.corner(r) + CORNER - 1
            left, right = self.corner_left[at], self.corner_right[at]
        shift = -(8 * (q % 2) + 64 * (q // 2))
        return merge_left(own, roll(left, shift)), merge_right(own, roll(right, shift))


def limited(ahead, behind):
    return jnp.maximum(
        jnp.minimum(ahead, jnp.maximum(behind, 0.0)), jnp.minimum(behind, 0.0)
    )


def face_pair(vel, vel_next, wet):
    a = jnp.where(wet, 0.5 * (vel + vel_next), 0.0)
    size = jnp.abs(a)
    return a, 0.5 * size * (1.0 - size)


def transport_rows(streams, ax_ref, bx_ref, ay_ref, by_ref, first, last):
    states = []
    for load, *_ in streams:
        before, here, after = load(first - 2), load(first - 1), load(first)
        states.append((here, after, limited(after - here, here - before), after - here, None))
    for i in range(first - 1, last):
        for n, (load, store, kind, xo, yo) in enumerate(streams):
            row, nxt, slope, diff, below = states[n]
            far = load(i + 2)
            diff_next = far - nxt
            slope_next = limited(diff_next, diff)
            ay, by = ay_ref[kind, yo + i], by_ref[kind, yo + i]
            positive = ay >= 0.0
            above = ay * jnp.where(positive, row, nxt) + by * jnp.where(positive, slope, slope_next)
            if below is not None:
                ax, bx = ax_ref[kind, xo + i], bx_ref[kind, xo + i]
                east = roll(row, -1)
                dx = east - row
                sx = limited(dx, roll(dx, 1))
                sx_east = roll(sx, -1)
                pos = ax >= 0.0
                fx = ax * jnp.where(pos, row, east) + bx * jnp.where(pos, sx, sx_east)
                store(i, row - (fx - roll(fx, 1)) - (above - below))
            states[n] = (nxt, far, slope_next, diff_next, above)


def select_lanes(moves):
    parts = []
    source = lax.broadcasted_iota(jnp.int32, (LANES, LANES), 0)
    target = lax.broadcasted_iota(jnp.int32, (LANES, LANES), 1)
    for f, d in moves:
        parts.append(jnp.where(source == GROUP * f + target % GROUP + d, 1.0, 0.0))
    return jnp.concatenate(parts, axis=1)


def exact_dot(a, b):
    return jnp.dot(a, b, precision=lax.Precision.HIGHEST, preferred_element_type=F32)


def transport_kernel(
    place_ref, x_ref, strip_ref, flow_ref, fstrip_ref, left_ref, right_ref, *refs, firsts, span, shards, together
):
    outer, outs, scratch = refs[: -shards - 11], refs[-shards - 11 : -11], refs[-11:]
    ext_ref, ax_ref, bx_ref, ay_ref, by_ref, first_ref, moved_ref, edge_ref, spread_ref, main_ref, shift_ref = scratch
    count, rows = x_ref.shape[0], x_ref.shape[1] // SUB
    half = rows // 2
    place = place_ref[0]
    level = level_ids().astype(F32)
    flow = Flow(flow_ref, fstrip_ref, left_ref, right_ref, outer)
    wide = span + 2 * HALO
    every = [(n, q, first + q) for n, first in enumerate(firsts) for q in range(-HALO, span + HALO)]
    tile_at = lambda n, q: pl.ds((n * wide + q + HALO) * SUB, SUB)

    for n, q, r in every:
        main_ref[tile_at(n, q), :] = flow.row(0, r)
        left, right = flow.strips(r)
        edge_ref[0, tile_at(n, q), :] = left
        edge_ref[1, tile_at(n, q), :] = right
    shift_east = jnp.where(
        lax.broadcasted_iota(jnp.int32, (LANES, LANES), 0)
        == lax.broadcasted_iota(jnp.int32, (LANES, LANES), 1) + 1,
        1.0,
        0.0,
    )
    shift_ref[...] = exact_dot(main_ref[...], shift_east)
    moves = select_lanes(((0, 0), (0, 1), (1, 0), (2, 0), (2, 1)))
    for side in range(2):
        spread_ref[side] = exact_dot(edge_ref[side], moves)

    previous = None
    for n, q, r in every:
        at = tile_at(n, q)
        aux = flow.row(2, r)
        spread = lambda v, i: jnp.broadcast_to(v[i : i + 1, :], (SUB, LANES))
        kinds = [(main_ref[at, :], shift_ref[at, :], flow.row(1, r), spread(aux, 0), spread(aux, 2))]
        for side in range(2):
            east, east_next, north, tally, tally_next = (
                spread_ref[side, at, LANES * j : LANES * (j + 1)] for j in range(5)
            )
            tally, tally_next = spread(tally, 0), spread(tally_next, 0)
            kinds.append((east, east_next, north, tally, jnp.minimum(tally, tally_next)))
        for kind, (east, east_next, north, tally, pair) in enumerate(kinds):
            if -2 <= q < span + 2:
                i = n * (span + 4) + q + 2
                ax_ref[kind, i], bx_ref[kind, i] = face_pair(east, east_next, level < pair)
            if -2 <= q < span + 3:
                i = n * (span + 5) + q + 2
                below, depth = previous[kind]
                ay_ref[kind, i], by_ref[kind, i] = face_pair(
                    below, north, level < jnp.minimum(depth, tally)
                )
        previous = [(k[2], k[3]) for k in kinds]

    for n, q, r in every:
        if r < 0 or r >= rows:
            src = flow.up if r < 0 else flow.down
            j = r + HALO if r < 0 else r - rows
            fields = [src[t * HALO + j] for t in range(count)]
            own = strip_of(fields)
            at = flow.corner(r) + j % 2
            left, right = flow.corner_left[at], flow.corner_right[at]
            swap = j >= 2
        else:
            fields = [x_ref[t, pl.ds(r, SUB, stride=rows), :] for t in range(count)]
            own = strip_ref[r]
            left, right = left_ref[r % half], right_ref[r % half]
            swap = r >= half
        if swap:
            left, right = roll(left, -8), roll(right, -8)
        fields += [merge_left(own, left), merge_right(own, right)]
        for t, value in enumerate(fields):
            ext_ref[t, n * wide + HALO + q] = value

    def some(c, carry):
        before, after = [], []
        for j in range(together):
            p = c * together + j
            kind = jnp.maximum(p - (count - 1), 0)
            for n in range(len(firsts)):
                xo, yo = n * (span + 4) + 2, n * (span + 5) + 3

                def load_start(i, p=p, n=n):
                    return ext_ref[p, n * wide + HALO + i]

                def store_first(i, value, j=j, xo=xo):
                    first_ref[j, xo + i] = value

                def load_first(i, j=j, xo=xo):
                    return first_ref[j, xo + i]

                def store_moved(i, value, p=p, n=n):
                    moved_ref[p, n * span + i] = value

                before.append((load_start, store_first, kind, xo, yo))
                after.append((load_first, store_moved, kind, xo, yo))
        transport_rows(before, ax_ref, bx_ref, ay_ref, by_ref, -2, span + 2)
        transport_rows(after, ax_ref, bx_ref, ay_ref, by_ref, 0, span)
        return carry

    lax.fori_loop(0, (count + 2) // together, some, 0)

    lane = lane_ids()
    edge = (lane < 4) | (lane >= LANES - 4)
    from_right = (lane % GROUP >= 4) & (lane % GROUP < 8)
    share = span * len(firsts) // len(outs)
    for k, out_ref in enumerate(outs):
        base = (place ^ k) * share
        for r in range(share):
            joined = jnp.where(from_right, moved_ref[count + 1, base + r], moved_ref[count, base + r])
            for t in range(count):
                out_ref[t * share + r] = jnp.where(
                    edge, roll(joined, -(GROUP * t + 8)), moved_ref[t, base + r]
                )


def transport(place, shards, x, strip, flow_parts, firsts, span, together):
    count = x.shape[0]
    vmem = pl.BlockSpec(memory_space=pltpu.VMEM)
    tile = lambda *n: pltpu.VMEM(n + (SUB, LANES), F32)
    flat = lambda *n: pltpu.VMEM(n, F32)
    args = (x, strip) + flow_parts
    pieces = len(firsts)
    wide = (span + 2 * HALO) * pieces
    return pl.pallas_call(
        functools.partial(transport_kernel, firsts=firsts, span=span, shards=shards, together=together),
        in_specs=[pl.BlockSpec(memory_space=pltpu.SMEM)] + [vmem] * len(args),
        out_shape=tuple(
            jax.ShapeDtypeStruct((count * span * pieces // shards, SUB, LANES), F32)
            for _ in range(shards)
        ),
        scratch_shapes=[
            tile(count + 2, wide),
            tile(3, (span + 4) * pieces),
            tile(3, (span + 4) * pieces),
            tile(3, (span + 5) * pieces),
            tile(3, (span + 5) * pieces),
            tile(together, (span + 4) * pieces),
            tile(count + 2, span * pieces),
            flat(2, wide * SUB, LANES),
            flat(2, wide * SUB, 5 * LANES),
            flat(wide * SUB, LANES),
            flat(wide * SUB, LANES),
        ],
        compiler_params=grant(20),
        name="transport",
    )(place, *args)


def react_kernel(place_ref, table_ref, pace_ref, uptake_ref, surface_ref, tally_ref, *refs, firsts):
    shards = (len(refs) - 3) // 2
    ins, outs = refs[:shards], refs[shards : 2 * shards]
    light_ref, wet_ref, heat_ref = refs[2 * shards :]
    total = pace_ref.shape[0]
    count = total // shards
    share = ins[0].shape[0] // count
    place = place_ref[0]
    level = level_ids()
    heat_ref[...] = jnp.zeros_like(heat_ref)

    for r in range(share):
        row = band_row(firsts, share * shards // len(firsts), place * share + r)
        tally = jnp.broadcast_to(tally_ref[pl.ds(row, 1), :], (SUB, LANES))
        surface = surface_ref[row]
        wet = jnp.where(level < tally, 1.0, 0.0)
        absorbed = jnp.zeros((SUB, LANES), F32)
        for k, ref in enumerate(ins):
            for t in range(count):
                absorbed = absorbed + uptake_ref[(place ^ k) * count + t] * jnp.abs(ref[t * share + r])
        layer = (COLUMN_DEPTH / SUB) * (WATER_ABSORB + absorbed) * wet
        total_depth = jnp.where(level >= 1, pltpu.roll(layer, 1, 0), 0.0)
        for shift in (1, 2, 4):
            total_depth = total_depth + jnp.where(
                level >= shift, pltpu.roll(total_depth, shift, 0), 0.0
            )
        top = surface * jnp.exp(-total_depth)
        heat_ref[pl.ds(r * SUB, SUB), :] = top * (1.0 - jnp.exp(-layer))
        light_ref[r] = REACT_STEP * wet * (top / (top + HALF_LIGHT))
        wet_ref[r] = REACT_STEP * wet

    block = 4
    for k, out_ref in enumerate(outs):
        for m0 in range(0, count, block):
            dest = [(place ^ k) * count + m0 + j for j in range(block)]
            acc = [[None] * share for _ in range(block)]
            for kk, ref in enumerate(ins):
                for t in range(count):
                    n = (place ^ kk) * count + t
                    values = [ref[t * share + r] for r in range(share)]
                    for j in range(block):
                        c = table_ref[dest[j], n]
                        for r in range(share):
                            term = c * values[r]
                            acc[j][r] = term if acc[j][r] is None else acc[j][r] + term
            for j in range(block):
                pace = pace_ref[dest[j]]
                for r in range(share):
                    own = ins[k][(m0 + j) * share + r]
                    out_ref[(m0 + j) * share + r] = (
                        own + wet_ref[r] * acc[j][r] + pace * (light_ref[r] * own)
                    )
        own_levels = SUB // shards
        for q in range(own_levels):
            level_at = (place ^ k) * own_levels + q
            out_ref[count * share + q] = heat_ref[pl.ds(level_at, SUB, stride=SUB), :]


def react(place, table, pace, uptake, surface, tally, blocks, firsts):
    shards = len(blocks)
    share = blocks[0].shape[0] // (pace.shape[0] // shards)
    smem = pl.BlockSpec(memory_space=pltpu.SMEM)
    vmem = pl.BlockSpec(memory_space=pltpu.VMEM)
    assert share <= SUB
    return pl.pallas_call(
        functools.partial(react_kernel, firsts=firsts),
        in_specs=[smem] * 5 + [vmem] * (1 + shards),
        out_shape=tuple(
            jax.ShapeDtypeStruct((b.shape[0] + SUB // shards, SUB, LANES), F32) for b in blocks
        ),
        scratch_shapes=[
            pltpu.VMEM((share, SUB, LANES), F32),
            pltpu.VMEM((share, SUB, LANES), F32),
            pltpu.VMEM((SUB * SUB, LANES), F32),
        ],
        compiler_params=grant(8),
        name="react",
    )(place, table, pace, uptake, surface, tally, *blocks)


def finish_kernel(place_ref, thermal_ref, *refs, bands, shards):
    *ins, out_ref, temp_ref, cells_ref = refs
    count, _, rows, _ = out_ref.shape
    own_levels = SUB // shards
    place = place_ref[0]
    for n, (firsts, span) in enumerate(bands):
        share = span * len(firsts) // shards
        for k, ref in enumerate(ins[n * shards : (n + 1) * shards]):
            for r in range(share):
                row = band_row(firsts, span, (place ^ k) * share + r)
                for m in range(count):
                    at = pl.multiple_of((m * rows + row) * SUB, SUB)
                    cells_ref[pl.ds(at, SUB), :] = ref[m * share + r]
                for q in range(own_levels):
                    heat = ref[count * share + q]
                    at = pl.multiple_of(((count + q) * rows + row) * SUB, SUB)
                    cells_ref[pl.ds(at, SUB), :] = jnp.broadcast_to(heat[r : r + 1, :], (SUB, LANES))
    for b in range(0, rows, SUB):
        for m in range(count):
            for lev in range(SUB):
                start = (m * rows + b) * SUB + lev
                out_ref[m, lev, b : b + SUB, :] = cells_ref[pl.ds(start, SUB, stride=SUB), :]
        for q in range(own_levels):
            heat = cells_ref[pl.ds(((count + q) * rows + b) * SUB, SUB, stride=SUB), :]
            temp_ref[q, b : b + SUB, :] = thermal_ref[q, b : b + SUB, :] + WARMING_WEIGHT * heat


def finish(place, thermal, blocks, shape, bands):
    count, _, rows, _ = shape
    own_levels = thermal.shape[0]
    shards = SUB // own_levels
    vmem = pl.BlockSpec(memory_space=pltpu.VMEM)
    return pl.pallas_call(
        functools.partial(finish_kernel, bands=bands, shards=shards),
        in_specs=[pl.BlockSpec(memory_space=pltpu.SMEM)] + [vmem] * (1 + len(blocks)),
        out_shape=(jax.ShapeDtypeStruct(shape, F32), jax.ShapeDtypeStruct(thermal.shape, F32)),
        scratch_shapes=[pltpu.VMEM(((count + own_levels) * rows * SUB, LANES), F32)],
        compiler_params=grant(12),
        name="finish",
    )(place, thermal, *blocks)


def level_sum(x):
    for shift in (4, 2, 1):
        x = x + pltpu.roll(x, shift, 0)
    return x


def momentum_kernel(
    place_ref,
    coriolis_ref,
    inside_ref,
    flow_ref,
    strip_ref,
    left_ref,
    right_ref,
    up_ref,
    down_ref,
    cleft_ref,
    cright_ref,
    east_ref,
    north_ref,
    height_ref,
    a_ref,
    b_ref,
    c_ref,
):
    rows = height_ref.shape[0]
    own_levels = east_ref.shape[0] // rows
    place = place_ref[0]
    lane = lane_ids()
    level = level_ids().astype(F32)
    flow = Flow(flow_ref, strip_ref, left_ref, right_ref, (up_ref, down_ref, cleft_ref, cright_ref))
    for r in range(-2, rows + 2):
        east, north, aux = (flow.row(f, r) for f in range(3))
        left, right = flow.strips(r)
        both = [
            jnp.where(lane < GROUP, roll(left, -GROUP * f), roll(right, GROUP - GROUP * f))
            for f in range(3)
        ]
        for p, (u, v, w) in enumerate(((east, north, aux), both)):
            wet = jnp.where(level < over_levels(w), 1.0, 0.0)
            h = jnp.broadcast_to(w[1:2, :], (SUB, LANES))
            for f, value in enumerate((u, v, h, wet)):
                a_ref[p, f, r + 2] = value

    def substep(src, offset, put, first, last):
        for p in range(2):
            for i in range(first, last):
                g = lambda f, d: src[p, f, i + offset + d]
                u, v, h = g(0, 0), g(1, 0), g(2, 0)
                un, us, vn, vs, hn, hs = g(0, 1), g(0, -1), g(1, 1), g(1, -1), g(2, 1), g(2, -1)
                wet = a_ref[p, 3, i + 2]
                cor = coriolis_ref[i + 2]
                ue, uw, ve, vw, he, hw = (
                    roll(u, -1), roll(u, 1), roll(v, -1), roll(v, 1), roll(h, -1), roll(h, 1),
                )
                div = level_sum(0.5 * (ue - uw) + 0.5 * (vn - vs))
                nu = wet * (
                    u
                    + TIME_STEP
                    * (
                        cor * v
                        - GRAVITY * (0.5 * (he - hw))
                        + VISCOSITY * (un + us + ue + uw - 4.0 * u)
                        - BOTTOM_DRAG * u
                    )
                )
                nv = wet * (
                    v
                    + TIME_STEP
                    * (
                        -cor * u
                        - GRAVITY * (0.5 * (hn - hs))
                        + VISCOSITY * (vn + vs + ve + vw - 4.0 * v)
                        - BOTTOM_DRAG * v
                    )
                )
                nh = h - TIME_STEP * DEPTH_SCALE * div
                put(p, i, nu, nv, nh)

    def put_first(p, i, nu, nv, nh):
        inside = inside_ref[i + 2]
        for f, value in enumerate((nu, nv, nh * inside)):
            b_ref[p, f, i + 1] = value

    def put_second(p, i, nu, nv, nh):
        for f, value in enumerate((nu, nv, nh)):
            c_ref[p, f, pl.ds(i * SUB, SUB), :] = value

    substep(a_ref, 2, put_first, -1, rows + 1)
    substep(b_ref, 1, put_second, 0, rows)

    def joined(f, start):
        lane8 = lax.broadcasted_iota(jnp.int32, (SUB, LANES), 1)
        main = c_ref[0, f, pl.ds(start, SUB, stride=SUB), :]
        edge = c_ref[1, f, pl.ds(start, SUB, stride=SUB), :]
        out = jnp.where(lane8 < 2, roll(edge, -8), main)
        return jnp.where(lane8 >= LANES - 2, roll(edge, LANES - 2 - (GROUP + 6)), out)

    for j in range(rows // SUB):
        for q in range(own_levels):
            lev = place * own_levels + q
            dst = q * rows + j * SUB
            east_ref[dst : dst + SUB, :] = joined(0, j * SUB * SUB + lev)
            north_ref[dst : dst + SUB, :] = joined(1, j * SUB * SUB + lev)
        height_ref[j * SUB : (j + 1) * SUB, :] = joined(2, j * SUB * SUB)


def momentum(place, coriolis, inside, flow_parts, rows, own_levels):
    vmem = pl.BlockSpec(memory_space=pltpu.VMEM)
    args = (coriolis, inside) + flow_parts
    return pl.pallas_call(
        momentum_kernel,
        in_specs=[pl.BlockSpec(memory_space=pltpu.SMEM)] * 3 + [vmem] * len(flow_parts),
        out_shape=(
            jax.ShapeDtypeStruct((own_levels * rows, LANES), F32),
            jax.ShapeDtypeStruct((own_levels * rows, LANES), F32),
            jax.ShapeDtypeStruct((rows, LANES), F32),
        ),
        scratch_shapes=[
            pltpu.VMEM((2, 4, rows + 4, SUB, LANES), F32),
            pltpu.VMEM((2, 3, rows + 2, SUB, LANES), F32),
            pltpu.VMEM((2, 3, rows * SUB, LANES), F32),
        ],
        compiler_params=grant(12),
        name="momentum",
    )(place, *args)


def to_peer(block, k):
    count = lax.axis_size("trc")
    return lax.ppermute(block, "trc", [(i, i ^ k) for i in range(count)])


def exchanged(blocks):
    out = [blocks[0]]
    for k in range(1, len(blocks)):
        out.append(to_peer(blocks[k], k))
    return out


def from_lat(block, step):
    count = lax.axis_size("lat")
    return lax.ppermute(
        block, "lat", [(i, i + step) for i in range(count) if 0 <= i + step < count]
    )


def both_sides(block):
    count = lax.axis_size("lon")
    left = lax.ppermute(block, "lon", [(i, (i + 1) % count) for i in range(count)])
    if count == 2:
        return left, left
    return left, lax.ppermute(block, "lon", [(i, (i - 1) % count) for i in range(count)])


def body(
    species_concentrations,
    zonal_velocity_array,
    meridional_velocity_array,
    thermal_anomaly,
    ocean_top_height_grid,
    water_layer_tally,
    species_interaction_table,
    species_production_pace,
    photon_uptake,
):
    count, levels, rows, cols = species_concentrations.shape
    own_levels = zonal_velocity_array.shape[0]
    shards = lax.axis_size("trc")
    assert levels == SUB and cols == LANES and count * GROUP == LANES and shards & (shards - 1) == 0
    trc_place = lax.axis_index("trc")
    place = trc_place.astype(jnp.int32).reshape(1)
    lat_total = rows * lax.axis_size("lat")
    lat_first = lax.axis_index("lat") * rows
    lat_global = (lat_first + jnp.arange(-2, rows + 2)).astype(F32)
    angle = math.pi * ((lat_global + 0.5) / lat_total - 0.5)
    coriolis = CORIOLIS_SCALE * jnp.sin(angle)
    surface = 1.0 + jnp.cos(angle[2:-2])
    inside = ((lat_global >= 0) & (lat_global < lat_total)).astype(F32)

    x = species_concentrations.reshape(count, levels * rows, cols)
    own = jnp.stack([zonal_velocity_array, meridional_velocity_array]).reshape(
        2, own_levels * rows, cols
    )
    peers = [to_peer(own, k) for k in range(1, shards)]
    strip, *messages = pack_tracers(x)
    flow, fstrip, fcols, fup, fdown = pack_flow(
        place, own, peers, water_layer_tally, ocean_top_height_grid, messages
    )
    left_in, right_in = both_sides(fcols)
    up_in, down_in = from_lat(fup, 1), from_lat(fdown, -1)
    corner = pack_edges(up_in, down_in)
    cleft_in, cright_in = both_sides(corner)
    inner = (flow, fstrip, left_in, right_in)
    outer = (up_in, down_in, cleft_in, cright_in)
    edge = HALO + 2
    bands = (
        ((edge,), rows - 2 * edge, 2, inner),
        ((0, rows - edge), edge, 2, inner + outer),
    )
    assert all(len(firsts) * span % shards == 0 for firsts, span, *_ in bands)
    blocks = []
    for firsts, span, together, parts in bands:
        moved = transport(place, shards, x, strip, parts, firsts, span, together)
        blocks.append(exchanged(moved))
    back = []
    for n, (firsts, *_) in enumerate(bands):
        reacted = react(
            place,
            species_interaction_table,
            species_production_pace,
            photon_uptake,
            surface,
            water_layer_tally,
            blocks[n],
            firsts,
        )
        back.append(exchanged(reacted))
    late, back[-1][0] = lax.optimization_barrier((place, back[-1][0]))
    east_out, north_out, height_out = momentum(
        late, coriolis, inside, inner + outer, rows, own_levels
    )
    updated, temperature = finish(
        place,
        thermal_anomaly,
        back[0] + back[1],
        species_concentrations.shape,
        tuple((firsts, span) for firsts, span, *_ in bands),
    )
    vel = (own_levels, rows, cols)
    return (
        updated,
        east_out.reshape(vel),
        north_out.reshape(vel),
        temperature,
        height_out,
    )


def solution(mesh):
    return jax.shard_map(
        body,
        mesh=mesh,
        in_specs=(
            P("trc", None, "lat", "lon"),
            P("trc", "lat", "lon"),
            P("trc", "lat", "lon"),
            P("trc", "lat", "lon"),
            P("lat", "lon"),
            P("lat", "lon"),
            P(),
            P(),
            P(),
        ),
        out_specs=(
            P("trc", None, "lat", "lon"),
            P("trc", "lat", "lon"),
            P("trc", "lat", "lon"),
            P("trc", "lat", "lon"),
            P("lat", "lon"),
        ),
        check_vma=False,
    )
```
